128 devices in a mesh: gx: 8 (over y, z_hi), gz: 16 (over x, z_lo, core).
Axes of the slice: x: 4, y: 4, z: 4 (z_hi: 2, z_lo: 2; z = z_hi * 2 + z_lo), core: 2. Of those that a mesh axis runs over, the one named last changes fastest.
Arguments:
- estimate: float32 [256, 128, 128], P('gz', 'gx'), may hold values from 0.5 to 2
- view_tiles: bfloat16 [128, 128, 2048], P(('gx', 'gz')), may hold values from 0.25 to 4
- incoming_label: int32 [128, 128], P(('gx', 'gz')), may hold values from -1 to 95, as said below
- lateral_bank: float32 [6, 16, 2, 33], replicated, may hold values from 0.05 to 1
- axial_kernel: float32 [6, 33], replicated, may hold values from 0.05 to 1
- kernel_index: int32 [256], replicated, may hold values from 0 to 15
Outputs:
- joined: float32 [256, 128, 128], P('gz', 'gx')
The draws below stay inside these ranges and needn't reach their ends.
Inputs may be any that keep to these rules, and one draw needn't show every extreme that they name: `incoming_label`: for every block owner, every plane of each view that covers the block arrives in exactly one slot, labelled view * 16 + plane, and a view covers either all planes of a block or none; other slots are -1. Every block is covered by at least one view, and in every draw one block is covered by all 6 views.
All inputs are finite; a program needn't handle non-finite values.
Results may differ from the reference program's by a relative error of at most 0.00055.
Values may be sent and summed in bfloat16 or wider, within the bound.
A program may use at most 128 MiB of HBM per device.

```python
import math
import jax
import jax.numpy as jnp
from jax import lax

DEPTH_DEV = 16
COLS_DEV = 16
LINE = 128
VIEWS = 6
TAPS = 33
KERNELS = 16
ITERS = 2
HALO = 16
CAP = 1
SLOTS = 128
TILE = 2048
NZ = 256
NX = 128
N_GX = 8
N_GZ = 16


def draw_incoming_label(key, part):
    devices = N_GX * N_GZ
    slots = devices * CAP
    planes = VIEWS * DEPTH_DEV
    key_order = jax.random.fold_in(key, 11)
    key_cover = jax.random.fold_in(key, 23)
    key_base = jax.random.fold_in(key, 37)
    key_full = jax.random.fold_in(key, 41)
    order = jax.vmap(lambda single: jax.random.permutation(single, slots))(jax.random.split(key_order, devices))
    order = order.astype(jnp.int32)
    cover = jax.random.randint(key_cover, (devices, VIEWS), 0, 10) < 6
    base = jax.random.randint(key_base, (devices,), 0, VIEWS)
    full = jax.random.randint(key_full, (), 0, devices)
    cover = cover | (jnp.arange(VIEWS)[None, :] == base[:, None])
    cover = cover | (jnp.arange(devices)[:, None] == full)
    owner_view = jnp.minimum(order // DEPTH_DEV, VIEWS - 1)
    live = (order < planes) & jnp.take_along_axis(cover, owner_view, axis=1)
    return jnp.where(live, order, -1).astype(jnp.int32)


def touch_ends(result, own_key, least, high):
    spot = [jax.random.randint(jax.random.fold_in(own_key, axis), (), 0, length) for axis, length in enumerate(result.shape)]
    longest = result.shape.index(max(result.shape))
    beside = spot[:longest] + [(spot[longest] + 1) % result.shape[longest]] + spot[longest + 1:]
    return result.at[tuple(spot)].set(least).at[tuple(beside)].set(high)


def shard_levels(rng, extent, cuts, low, top_value):
    factor_of = 1.0
    for axis_at, parts in cuts:
        steps = jax.random.uniform(jax.random.fold_in(jax.random.fold_in(rng, 6), axis_at), (parts,), jnp.float32, low / len(cuts), top_value / len(cuts))
        factor_of = factor_of * jnp.repeat(jnp.exp(steps), extent[axis_at] // parts).reshape((-1,) + (1,) * (len(extent) - 1 - axis_at))
    return factor_of


def setup_inputs(seed: int = 0) -> dict:
    seeds = jax.random.split(jax.random.key(seed), 7)
    return {
        "estimate": jnp.clip(jnp.exp(math.log(2.0) - 1.3862944 * jax.random.uniform(seeds[0], (NZ, NX, LINE), jnp.float32) ** shard_levels(seeds[0], (NZ, NX, LINE), ((0, 16), (1, 8)), -0.2, 0.2)), 0.5, 2.0),
        "view_tiles": jnp.clip(jnp.exp(math.log(4.0) - 2.7725887 * jax.random.uniform(seeds[1], (N_GX * N_GZ, SLOTS, TILE), jnp.float32) ** shard_levels(seeds[1], (N_GX * N_GZ, SLOTS, TILE), ((0, 128),), -0.2, 0.2)), 0.25, 4.0).astype(jnp.bfloat16),
        "incoming_label": draw_incoming_label(jax.random.fold_in(seeds[6], 71), 0),
        "lateral_bank": jnp.clip(jnp.exp(jax.random.uniform(seeds[3], (VIEWS, KERNELS, 2, TAPS), jnp.float32, math.log(0.05), math.log(1.0))), 0.05, 1.0),
        "axial_kernel": jnp.clip(jnp.exp(jax.random.uniform(seeds[4], (VIEWS, TAPS), jnp.float32, math.log(0.05), math.log(1.0))), 0.05, 1.0),
        "kernel_index": touch_ends(jax.random.randint(seeds[5], (NZ,), 0, KERNELS), jax.random.fold_in(seeds[5], 1), 0, KERNELS - 1).astype(jnp.int32),
    }


def shifted_sum(padded, weights, axis, length, flip):
    total = None
    for tap in range(TAPS):
        start = 2 * HALO - tap if flip else tap
        piece = lax.slice_in_dim(padded, start, start + length, axis=axis)
        term = weights[tap] * piece
        total = term if total is None else total + term
    return total


def pad_axis(field, axis):
    widths = [(0, 0)] * field.ndim
    widths[axis] = (HALO, HALO)
    return jnp.pad(field, widths)


def lateral(padx, kernel_x, kernel_y, cols, flip):
    across = shifted_sum(padx, kernel_x, 1, cols, flip)
    return shifted_sum(pad_axis(across, 2), kernel_y, 2, across.shape[2], flip)


def axial_sum(padz, weights, depth, flip):
    return shifted_sum(padz, weights, 0, depth, flip)


def reference(estimate, view_tiles, incoming_label, lateral_bank, axial_kernel, kernel_index):
    bank = lateral_bank / jnp.sum(lateral_bank, axis=-1, keepdims=True)
    axial_norm = axial_kernel / jnp.sum(axial_kernel, axis=-1, keepdims=True)
    devices = N_GX * N_GZ
    codes = jnp.arange(VIEWS * DEPTH_DEV, dtype=jnp.int32)

    def owner_planes(owner):
        labels = incoming_label[owner]
        arrived = lax.dynamic_slice_in_dim(view_tiles, owner * CAP, CAP, 1).reshape(SLOTS, TILE)
        select = (labels[None, :] == codes[:, None]).astype(jnp.bfloat16)
        return jnp.dot(select, arrived, preferred_element_type=jnp.float32).astype(jnp.bfloat16)

    blocks = lax.map(owner_planes, jnp.arange(devices, dtype=jnp.int32))
    data = blocks.reshape(N_GX, N_GZ, VIEWS, DEPTH_DEV, COLS_DEV, LINE)
    data = data.transpose(2, 1, 3, 0, 4, 5).reshape(VIEWS, NZ, NX, LINE)
    owner_view = jnp.where(incoming_label >= 0, incoming_label // DEPTH_DEV, -1)
    counts = jnp.sum((owner_view[:, None, :] == jnp.arange(VIEWS, dtype=jnp.int32)[None, :, None]).astype(jnp.int32), axis=2)
    covered = (counts > 0).reshape(N_GX, N_GZ, VIEWS).transpose(2, 1, 0)
    covered = jnp.repeat(jnp.repeat(covered, DEPTH_DEV, axis=1), COLS_DEV, axis=2)[..., None]
    weights = []
    for view in range(VIEWS):
        rows = bank[view][kernel_index]
        weights.append((rows[:, 0, :].T[:, :, None, None], rows[:, 1, :].T[:, :, None, None]))
    joined = estimate
    for sweep in range(ITERS):
        correction = jnp.zeros((NZ, NX, LINE), jnp.float32)
        for view in range(VIEWS):
            kernel_x, kernel_y = weights[view]
            grown = lateral(pad_axis(joined, 1), kernel_x, kernel_y, NX, False)
            blurred = axial_sum(pad_axis(grown, 0), axial_norm[view], NZ, False)
            ratio = jnp.where(covered[view], data[view].astype(jnp.float32) / blurred, 1.0).astype(jnp.bfloat16)
            ratio = lax.optimization_barrier(ratio).astype(jnp.float32)
            spread = axial_sum(pad_axis(ratio, 0), axial_norm[view], NZ, True)
            correction = correction + lateral(pad_axis(spread, 1), kernel_x, kernel_y, NX, True)
        joined = joined * (correction / VIEWS)
    return joined
```

```python
import jax
import jax.numpy as jnp
from jax import lax
from jax.experimental import pallas as pl
from jax.experimental.pallas import tpu as pltpu
from jax.sharding import PartitionSpec as P

TAPS = 33
ITERS = 2
HALO = 16
VIEWS = 6
KERNELS = 16
BLK = 16
NEAR = 48
LINE = 128
F32 = jnp.float32
BF = jnp.bfloat16
HI = lax.Precision.HIGHEST


def iota(shape, dim):
    return lax.broadcasted_iota(jnp.int32, shape, dim)


def build_bands(kx_ref, ky_ref, fwd_y, bwd_y, fwd_x, bwd_x):
    inside = jnp.abs(iota((LINE, LINE), 0) - iota((LINE, LINE), 1)) <= HALO

    @pl.loop(0, KERNELS)
    def _(k):
        kx = kx_ref[k]
        ky = ky_ref[k]
        rows = []
        for v in range(VIEWS):
            band = pltpu.roll(jnp.broadcast_to(ky[v : v + 1], (LINE, LINE)), LINE - HALO, 1, stride=1, stride_axis=0)
            band = jnp.where(inside, band, 0.0)
            bwd_y[k, v] = band.astype(BF)
            fwd_y[k, v] = band.T.astype(BF)
            rows.append(pltpu.roll(jnp.broadcast_to(kx[v : v + 1], (BLK, LINE)), 0, 1, stride=1, stride_axis=0))
        across = jnp.concatenate(rows, 0)
        fwd_x[k] = across.astype(BF)
        bwd_x[k] = across.T.astype(BF)


def ones_response(index_ref, ax_ref, kx_ref, ky_ref, col0, depth0, edge_x, edge_y, base_ref, cols, depths):
    tap = iota((LINE, LINE), 0)
    pos = iota((LINE, LINE), 1)
    at_x = col0 + pos - tap + HALO
    at_y = pos - tap + HALO
    ok_x = jnp.where((at_x >= 0) & (at_x < cols), 1.0, 0.0)
    ok_y = jnp.where((at_y >= 0) & (at_y < LINE), 1.0, 0.0)
    kx = kx_ref[...].reshape(KERNELS * 8, LINE)
    ky = ky_ref[...].reshape(KERNELS * 8, LINE)
    edge_x[...] = jnp.dot(kx, ok_x, precision=HI, preferred_element_type=F32).reshape(KERNELS, 8, LINE)
    edge_y[...] = jnp.dot(ky, ok_y, precision=HI, preferred_element_type=F32).reshape(KERNELS, 8, LINE)
    axial = ax_ref[...]
    lane = iota((8, LINE), 1)
    for z in range(BLK):
        k = index_ref[HALO + z]
        at_z = depth0 + z - lane + HALO
        part = jnp.sum(jnp.where((at_z >= 0) & (at_z < depths), axial, 0.0), axis=1, keepdims=True)
        left = edge_x[k][:, :BLK] * part
        base_ref[z] = lax.dot_general(
            left, edge_y[k], (((0,), (0,)), ((), ())), precision=HI, preferred_element_type=F32
        )


def lateral_forward(index_ref, fwd_x, fwd_y, wide_ref, mid, grown, first, last, unroll):
    @pl.loop(first // unroll, last // unroll)
    def _(s):
        for u in range(unroll):
            z = s * unroll + u
            k = index_ref[z]
            mid[z] = jnp.dot(fwd_x[k][:, :NEAR], wide_ref[z], preferred_element_type=F32).astype(BF)

    @pl.loop(first // unroll, last // unroll)
    def _(s):
        for u in range(unroll):
            z = s * unroll + u
            k = index_ref[z]
            for v in range(VIEWS):
                grown[v, z] = jnp.dot(mid[z, v * BLK : (v + 1) * BLK, :], fwd_y[k, v], preferred_element_type=F32)


def lateral_backward(index_ref, bwd_x, bwd_y, spread, mid, out_ref, first, last, unroll):
    @pl.loop(first // unroll, last // unroll)
    def _(s):
        for u in range(unroll):
            z = s * unroll + u
            k = index_ref[z]
            for v in range(VIEWS):
                mid[z, v * BLK : (v + 1) * BLK, :] = jnp.dot(
                    spread[v, z], bwd_y[k, v], preferred_element_type=F32
                ).astype(BF)

    @pl.loop(first // unroll, last // unroll)
    def _(s):
        for u in range(unroll):
            z = s * unroll + u
            k = index_ref[z]
            out_ref[z] = jnp.dot(bwd_x[k][:NEAR], mid[z], preferred_element_type=F32).astype(out_ref.dtype)


def taps_over(zi):
    return range(max(0, zi - 2 * HALO), min(BLK - 1, zi) + 1)


def axial_and_ratio(axial_ref, slot_ref, cover_ref, grown, tiles, spread):
    @pl.loop(0, VIEWS)
    def _(v):
        weights = [axial_ref[v, t] for t in range(TAPS)]
        seen = jnp.full((8, LINE), cover_ref[v], jnp.int32) > 0
        for half in range(2):
            rows = slice(half * 8, half * 8 + 8)
            total = [None] * BLK
            for zi in range(NEAR):
                g = grown[v, zi, rows, :]
                for zo in taps_over(zi):
                    term = weights[zi - zo] * g
                    total[zo] = term if total[zo] is None else total[zo] + term
            excess = []
            for zo in range(BLK):
                tile = tiles[slot_ref[v * BLK + zo]][rows].astype(F32)
                ratio = (tile / total[zo]).astype(BF).astype(F32)
                excess.append(jnp.where(seen, ratio - 1.0, 0.0))
            for zi in range(NEAR):
                acc = None
                for zo in taps_over(zi):
                    term = weights[zi - zo] * excess[zo]
                    acc = term if acc is None else acc + term
                spread[v, zi, rows, :] = acc.astype(BF)


def sweep_kernel(depths, cols):
    def body(index_ref, slot_ref, cover_ref, axial_ref, ax_ref, kx_ref, ky_ref, wide_ref, tiles,
             out_ref, base_ref, fwd_y, bwd_y, fwd_x, bwd_x, edge_x, edge_y, mid, grown, spread):
        col0 = lax.axis_index("gx") * BLK
        depth0 = lax.axis_index("gz") * BLK
        build_bands(kx_ref, ky_ref, fwd_y, bwd_y, fwd_x, bwd_x)
        ones_response(index_ref, ax_ref, kx_ref, ky_ref, col0, depth0, edge_x, edge_y, base_ref, cols, depths)
        lateral_forward(index_ref, fwd_x, fwd_y, wide_ref, mid, grown, 0, NEAR, 4)
        axial_and_ratio(axial_ref, slot_ref, cover_ref, grown, tiles, spread)
        lateral_backward(index_ref, bwd_x, bwd_y, spread, mid, out_ref, 0, NEAR, 4)

    smem = pl.BlockSpec(memory_space=pltpu.SMEM)
    vmem = pl.BlockSpec(memory_space=pltpu.VMEM)
    return pl.pallas_call(
        body,
        name="sweep",
        out_shape=(
            jax.ShapeDtypeStruct((NEAR, NEAR, LINE), F32),
            jax.ShapeDtypeStruct((BLK, BLK, LINE), F32),
        ),
        in_specs=[smem] * 4 + [vmem] * 5,
        out_specs=(vmem, vmem),
        scratch_shapes=[
            pltpu.VMEM((KERNELS, VIEWS, LINE, LINE), BF),
            pltpu.VMEM((KERNELS, VIEWS, LINE, LINE), BF),
            pltpu.VMEM((KERNELS, VIEWS * BLK, LINE), BF),
            pltpu.VMEM((KERNELS, LINE, VIEWS * BLK), BF),
            pltpu.VMEM((KERNELS, 8, LINE), F32),
            pltpu.VMEM((KERNELS, 8, LINE), F32),
            pltpu.VMEM((NEAR, VIEWS * BLK, LINE), BF),
            pltpu.VMEM((VIEWS, NEAR, BLK, LINE), F32),
            pltpu.VMEM((VIEWS, NEAR, BLK, LINE), BF),
        ],
        compiler_params=pltpu.CompilerParams(vmem_limit_bytes=48 << 20),
    )


def pairs(axis):
    up = [(i, i + 1) for i in range(lax.axis_size(axis) - 1)]
    return up, [(j, i) for i, j in up]


def extended(x, axis, dim):
    up, down = pairs(axis)
    return jnp.concatenate([lax.ppermute(x, axis, up), x, lax.ppermute(x, axis, down)], axis=dim)


def gathered(x, axis, dim):
    up, down = pairs(axis)
    low, own, high = (lax.slice_in_dim(x, i * BLK, (i + 1) * BLK, axis=dim) for i in range(3))
    return own + lax.ppermute(high, axis, up) + lax.ppermute(low, axis, down)


def small_tables(incoming_label, lateral_bank, axial_kernel, kernel_index):
    bank = lateral_bank / jnp.sum(lateral_bank, axis=-1, keepdims=True)
    axial = axial_kernel / jnp.sum(axial_kernel, axis=-1, keepdims=True)
    taps = jnp.pad(bank.transpose(1, 0, 2, 3), ((0, 0), (0, 8 - VIEWS), (0, 0), (0, LINE - TAPS)))
    ax = jnp.pad(axial, ((0, 8 - VIEWS), (0, LINE - TAPS)))
    near = lax.dynamic_slice_in_dim(
        jnp.pad(kernel_index, (HALO, HALO)), lax.axis_index("gz") * BLK, NEAR
    )
    labels = incoming_label[0]
    match = labels[None, :] == jnp.arange(VIEWS * BLK, dtype=jnp.int32)[:, None]
    slot = jnp.sum(jnp.where(match, jnp.arange(labels.shape[0], dtype=jnp.int32)[None, :], 0), axis=1)
    cover = jnp.sum(match.astype(jnp.int32).reshape(VIEWS, -1), axis=1)
    return axial, ax, taps[:, :, 0], taps[:, :, 1], near, slot, cover


def shards(estimate, view_tiles, incoming_label, lateral_bank, axial_kernel, kernel_index):
    depths = lax.axis_size("gz") * BLK
    cols = lax.axis_size("gx") * BLK
    axial, ax, kx, ky, near, slot, cover = small_tables(incoming_label, lateral_bank, axial_kernel, kernel_index)
    outgoing = view_tiles[0].reshape(-1, BLK, LINE)
    tiles = lax.all_to_all(outgoing, ("gx", "gz"), split_axis=0, concat_axis=0, tiled=True)
    sweep = sweep_kernel(depths, cols)
    joined = estimate
    for _ in range(ITERS):
        wide = extended(extended(joined.astype(BF), "gx", 1), "gz", 0)
        part, base = sweep(near, slot, cover, axial, ax, kx, ky, wide, tiles)
        part = gathered(part, "gz", 0)
        joined = joined * ((base + gathered(part, "gx", 1)) / VIEWS)
    return joined


def solution(mesh):
    return jax.shard_map(
        shards,
        mesh=mesh,
        in_specs=(P("gz", "gx", None), P(("gx", "gz"), None, None), P(("gx", "gz"), None), P(), P(), P()),
        out_specs=P("gz", "gx", None),
        check_vma=False,
    )
```

```python
import jax
import jax.numpy as jnp
from jax import lax
from jax.experimental import pallas as pl
from jax.experimental.pallas import tpu as pltpu
from jax.sharding import PartitionSpec as P

TAPS = 33
ITERS = 2
HALO = 16
VIEWS = 6
KERNELS = 16
BLK = 16
NEAR = 48
LINE = 128
F32 = jnp.float32
BF = jnp.bfloat16
HI = lax.Precision.HIGHEST


def iota(shape, dim):
    return lax.broadcasted_iota(jnp.int32, shape, dim)


def build_bands(kx_ref, ky_ref, fwd_y, bwd_y, fwd_x, bwd_x):
    inside = jnp.abs(iota((LINE, LINE), 0) - iota((LINE, LINE), 1)) <= HALO

    @pl.loop(0, KERNELS)
    def _(k):
        kx = kx_ref[k]
        ky = ky_ref[k]
        rows = []
        for v in range(VIEWS):
            band = pltpu.roll(jnp.broadcast_to(ky[v : v + 1], (LINE, LINE)), LINE - HALO, 1, stride=1, stride_axis=0)
            band = jnp.where(inside, band, 0.0)
            bwd_y[k, v] = band.astype(BF)
            fwd_y[k, v] = band.T.astype(BF)
            rows.append(pltpu.roll(jnp.broadcast_to(kx[v : v + 1], (BLK, LINE)), 0, 1, stride=1, stride_axis=0))
        across = jnp.concatenate(rows, 0)
        fwd_x[k] = across.astype(BF)
        bwd_x[k] = across.T.astype(BF)


def ones_response(index_ref, ax_ref, kx_ref, ky_ref, col0, depth0, edge_x, edge_y, base_ref, cols, depths):
    tap = iota((LINE, LINE), 0)
    pos = iota((LINE, LINE), 1)
    at_x = col0 + pos - tap + HALO
    at_y = pos - tap + HALO
    ok_x = jnp.where((at_x >= 0) & (at_x < cols), 1.0, 0.0)
    ok_y = jnp.where((at_y >= 0) & (at_y < LINE), 1.0, 0.0)
    kx = kx_ref[...].reshape(KERNELS * 8, LINE)
    ky = ky_ref[...].reshape(KERNELS * 8, LINE)
    edge_x[...] = jnp.dot(kx, ok_x, precision=HI, preferred_element_type=F32).reshape(KERNELS, 8, LINE)
    edge_y[...] = jnp.dot(ky, ok_y, precision=HI, preferred_element_type=F32).reshape(KERNELS, 8, LINE)
    axial = ax_ref[...]
    lane = iota((8, LINE), 1)
    for z in range(BLK):
        k = index_ref[HALO + z]
        at_z = depth0 + z - lane + HALO
        part = jnp.sum(jnp.where((at_z >= 0) & (at_z < depths), axial, 0.0), axis=1, keepdims=True)
        left = edge_x[k][:, :BLK] * part
        base_ref[z] = lax.dot_general(
            left, edge_y[k], (((0,), (0,)), ((), ())), precision=HI, preferred_element_type=F32
        )


def lateral_forward(index_ref, fwd_x, fwd_y, wide_ref, mid, grown, first, last, unroll):
    @pl.loop(first // unroll, last // unroll)
    def _(s):
        for u in range(unroll):
            z = s * unroll + u
            k = index_ref[z]
            mid[z] = jnp.dot(fwd_x[k][:, :NEAR], wide_ref[z], preferred_element_type=F32).astype(BF)

    @pl.loop(first // unroll, last // unroll)
    def _(s):
        for u in range(unroll):
            z = s * unroll + u
            k = index_ref[z]
            for v in range(VIEWS):
                grown[v, z] = jnp.dot(mid[z, v * BLK : (v + 1) * BLK, :], fwd_y[k, v], preferred_element_type=F32)


def lateral_backward(index_ref, bwd_x, bwd_y, spread, mid, out_ref, first, last, unroll):
    @pl.loop(first // unroll, last // unroll)
    def _(s):
        for u in range(unroll):
            z = s * unroll + u
            k = index_ref[z]
            for v in range(VIEWS):
                mid[z, v * BLK : (v + 1) * BLK, :] = jnp.dot(
                    spread[v, z], bwd_y[k, v], preferred_element_type=F32
                ).astype(BF)

    @pl.loop(first // unroll, last // unroll)
    def _(s):
        for u in range(unroll):
            z = s * unroll + u
            k = index_ref[z]
            out_ref[z] = jnp.dot(bwd_x[k][:NEAR], mid[z], preferred_element_type=F32).astype(out_ref.dtype)


def taps_over(zi):
    return range(max(0, zi - 2 * HALO), min(BLK - 1, zi) + 1)


def axial_and_ratio(axial_ref, slot_ref, cover_ref, grown, tile_of, spread):
    @pl.loop(0, VIEWS)
    def _(v):
        weights = [axial_ref[v, t] for t in range(TAPS)]
        seen = jnp.full((8, LINE), cover_ref[v], jnp.int32) > 0
        for half in range(2):
            rows = slice(half * 8, half * 8 + 8)
            total = [None] * BLK
            for zi in range(NEAR):
                g = grown[v, zi, rows, :]
                for zo in taps_over(zi):
                    term = weights[zi - zo] * g
                    total[zo] = term if total[zo] is None else total[zo] + term
            excess = []
            for zo in range(BLK):
                tile = tile_of(slot_ref[v * BLK + zo])[rows].astype(F32)
                ratio = (tile / total[zo]).astype(BF).astype(F32)
                excess.append(jnp.where(seen, ratio - 1.0, 0.0))
            for zi in range(NEAR):
                acc = None
                for zo in taps_over(zi):
                    term = weights[zi - zo] * excess[zo]
                    acc = term if acc is None else acc + term
                spread[v, zi, rows, :] = acc.astype(BF)


LOW, OWN, HIGH = slice(0, BLK), slice(BLK, 2 * BLK), slice(2 * BLK, NEAR)


class Copy:
    def __init__(self, src, dst, sems, slot, device, sends, receives):
        self.sends, self.receives = sends, receives
        self.copy = pltpu.make_async_remote_copy(
            src_ref=src, dst_ref=dst, send_sem=sems[0].at[slot], recv_sem=sems[1].at[slot],
            device_id=device, device_id_type=pl.DeviceIdType.MESH,
        )

    def start(self):
        pl.when(self.sends)(self.copy.start)

    def wait_recv(self):
        pl.when(self.receives)(self.copy.wait_recv)

    def wait_send(self):
        pl.when(self.sends)(self.copy.wait_send)


def joint_kernel(nx, nz):
    def body(index_ref, slot_ref, cover_ref, axial_ref, ax_ref, kx_ref, ky_ref, estimate_ref, outgoing,
             out_ref, fwd_y, bwd_y, fwd_x, bwd_x, edge_x, edge_y, base, mid, grown, spread, total,
             wide, part_z, side, part_x, passing, arrived,
             halo_sems, sum_sems, first_send, first_recv, second_send, second_recv, local_sems):
        gx, gz = lax.axis_index("gx"), lax.axis_index("gz")
        has_l, has_r, has_d, has_u = gx > 0, gx < nx - 1, gz > 0, gz < nz - 1
        left, right = (lax.rem(gx + nx - 1, nx), gz), (lax.rem(gx + 1, nx), gz)
        down, up = (gx, lax.rem(gz + nz - 1, nz)), (gx, lax.rem(gz + 1, nz))
        halo_s, halo_r = halo_sems
        sum_s, sum_r = sum_sems

        for it in range(ITERS):
            wide[it] = jnp.zeros_like(wide[it])
        part_z[...] = jnp.zeros_like(part_z)
        part_x[...] = jnp.zeros_like(part_x)
        wide[0, OWN, OWN] = estimate_ref[...].astype(BF)

        barrier = pltpu.get_barrier_semaphore()
        for d in range(1, nz):
            pl.semaphore_signal(barrier, inc=1, device_id=(gx, lax.rem(gz + d, nz)), device_id_type=pl.DeviceIdType.MESH)
        for d in range(1, nx):
            pl.semaphore_signal(barrier, inc=1, device_id=(lax.rem(gx + d, nx), gz), device_id_type=pl.DeviceIdType.MESH)
        pl.semaphore_wait(barrier, nx + nz - 2)

        def halo(it):
            w = wide.at[it]
            sems = (halo_s.at[it], halo_r.at[it])
            own = w.at[OWN, OWN]
            near = [
                Copy(own, w.at[OWN, LOW], sems, 0, right, has_r, has_l),
                Copy(own, w.at[OWN, HIGH], sems, 1, left, has_l, has_r),
            ]
            far = [
                Copy(own, w.at[LOW, OWN], sems, 2, up, has_u, has_d),
                Copy(own, w.at[HIGH, OWN], sems, 3, down, has_d, has_u),
            ]
            corner = [
                Copy(w.at[OWN, LOW], w.at[LOW, LOW], sems, 4, up, has_u & has_l, has_d & has_l),
                Copy(w.at[OWN, LOW], w.at[HIGH, LOW], sems, 5, down, has_d & has_l, has_u & has_l),
                Copy(w.at[OWN, HIGH], w.at[LOW, HIGH], sems, 6, up, has_u & has_r, has_d & has_r),
                Copy(w.at[OWN, HIGH], w.at[HIGH, HIGH], sems, 7, down, has_d & has_r, has_u & has_r),
            ]
            return near, far, corner

        def sums(it):
            sems = (sum_s.at[it], sum_r.at[it])
            return (
                Copy(total.at[LOW], part_z.at[it, 1], sems, 0, down, has_d, has_u),
                Copy(total.at[HIGH], part_z.at[it, 0], sems, 1, up, has_u, has_d),
                Copy(side.at[0], part_x.at[it, 1], sems, 2, left, has_l, has_r),
                Copy(side.at[1], part_x.at[it, 0], sems, 3, right, has_r, has_l),
            )

        def along_gz(d):
            return pltpu.make_async_remote_copy(
                src_ref=outgoing.at[:, lax.rem(gz + d, nz)], dst_ref=passing.at[:, gz],
                send_sem=first_send.at[d], recv_sem=first_recv.at[d],
                device_id=(gx, lax.rem(gz + d, nz)), device_id_type=pl.DeviceIdType.MESH,
            )

        def along_gx(d):
            return pltpu.make_async_remote_copy(
                src_ref=passing.at[lax.rem(gx + d, nx)], dst_ref=arrived.at[gx],
                send_sem=second_send.at[d], recv_sem=second_recv.at[d],
                device_id=(lax.rem(gx + d, nx), gz), device_id_type=pl.DeviceIdType.MESH,
            )

        for it in range(ITERS):
            near, far, corner = halo(it)
            for copy in near + far:
                copy.start()
            if it == 0:
                keep = pltpu.make_async_copy(outgoing.at[:, gz], passing.at[:, gz], local_sems.at[0])
                keep.start()
                for d in range(1, nz):
                    along_gz(d).start()
                build_bands(kx_ref, ky_ref, fwd_y, bwd_y, fwd_x, bwd_x)
            for copy in near:
                copy.wait_recv()
            for copy in corner:
                copy.start()
            lateral_forward(index_ref, fwd_x, fwd_y, wide.at[it], mid, grown, BLK, 2 * BLK, 4)
            if it == 0:
                keep.wait()
                for d in range(1, nz):
                    along_gz(d).wait_recv()
                for d in range(1, nx):
                    along_gx(d).start()
                stay = pltpu.make_async_copy(passing.at[gx], arrived.at[gx], local_sems.at[1])
                stay.start()
            for copy in far + corner:
                copy.wait_recv()
            lateral_forward(index_ref, fwd_x, fwd_y, wide.at[it], mid, grown, 0, BLK, 4)
            lateral_forward(index_ref, fwd_x, fwd_y, wide.at[it], mid, grown, 2 * BLK, NEAR, 4)
            if it == 0:
                ones_response(index_ref, ax_ref, kx_ref, ky_ref, gx * BLK, gz * BLK, edge_x, edge_y, base,
                              nx * BLK, nz * BLK)
                for d in range(1, nz):
                    along_gz(d).wait_send()
                for d in range(1, nx):
                    along_gx(d).wait()
                stay.wait()
            for copy in near + far + corner:
                copy.wait_send()

            axial_and_ratio(axial_ref, slot_ref, cover_ref, grown,
                            lambda s: arrived[s // nz, lax.rem(s, nz)], spread)
            below, above, to_left, to_right = sums(it)
            lateral_backward(index_ref, bwd_x, bwd_y, spread, mid, total, 0, BLK, 4)
            below.start()
            lateral_backward(index_ref, bwd_x, bwd_y, spread, mid, total, 2 * BLK, NEAR, 4)
            above.start()
            lateral_backward(index_ref, bwd_x, bwd_y, spread, mid, total, BLK, 2 * BLK, 4)
            below.wait_recv()
            above.wait_recv()
            reach = total[OWN] + part_z[it, 0] + part_z[it, 1]
            side[0] = reach[:, LOW]
            side[1] = reach[:, HIGH]
            to_left.start()
            to_right.start()
            inner = base[...] + reach[:, OWN]
            before = estimate_ref if it == 0 else out_ref
            to_left.wait_recv()
            to_right.wait_recv()
            after = before[...] * ((inner + part_x[it, 0] + part_x[it, 1]) / VIEWS)
            out_ref[...] = after
            if it + 1 < ITERS:
                wide[it + 1, OWN, OWN] = after.astype(BF)
            for copy in (below, above, to_left, to_right):
                copy.wait_send()

    smem = pl.BlockSpec(memory_space=pltpu.SMEM)
    vmem = pl.BlockSpec(memory_space=pltpu.VMEM)
    dma = pltpu.SemaphoreType.DMA
    return pl.pallas_call(
        body,
        name="joint",
        out_shape=jax.ShapeDtypeStruct((BLK, BLK, LINE), F32),
        in_specs=[smem] * 4 + [vmem] * 4 + [pl.BlockSpec(memory_space=pl.ANY)],
        out_specs=vmem,
        scratch_shapes=[
            pltpu.VMEM((KERNELS, VIEWS, LINE, LINE), BF),
            pltpu.VMEM((KERNELS, VIEWS, LINE, LINE), BF),
            pltpu.VMEM((KERNELS, VIEWS * BLK, LINE), BF),
            pltpu.VMEM((KERNELS, LINE, VIEWS * BLK), BF),
            pltpu.VMEM((KERNELS, 8, LINE), F32),
            pltpu.VMEM((KERNELS, 8, LINE), F32),
            pltpu.VMEM((BLK, BLK, LINE), F32),
            pltpu.VMEM((NEAR, VIEWS * BLK, LINE), BF),
            pltpu.VMEM((VIEWS, NEAR, BLK, LINE), F32),
            pltpu.VMEM((VIEWS, NEAR, BLK, LINE), BF),
            pltpu.VMEM((NEAR, NEAR, LINE), F32),
            pltpu.VMEM((ITERS, NEAR, NEAR, LINE), BF),
            pltpu.VMEM((ITERS, 2, BLK, NEAR, LINE), F32),
            pltpu.VMEM((2, BLK, BLK, LINE), F32),
            pltpu.VMEM((ITERS, 2, BLK, BLK, LINE), F32),
            pltpu.VMEM((nx, nz, BLK, LINE), BF),
            pltpu.VMEM((nx, nz, BLK, LINE), BF),
            (dma((ITERS, 8)), dma((ITERS, 8))),
            (dma((ITERS, 4)), dma((ITERS, 4))),
            dma((nz,)), dma((nz,)), dma((nx,)), dma((nx,)), dma((2,)),
        ],
        compiler_params=pltpu.CompilerParams(
            vmem_limit_bytes=48 << 20, collective_id=0, has_side_effects=True
        ),
    )


def small_tables(incoming_label, lateral_bank, axial_kernel, kernel_index):
    bank = lateral_bank / jnp.sum(lateral_bank, axis=-1, keepdims=True)
    axial = axial_kernel / jnp.sum(axial_kernel, axis=-1, keepdims=True)
    taps = jnp.pad(bank.transpose(1, 0, 2, 3), ((0, 0), (0, 8 - VIEWS), (0, 0), (0, LINE - TAPS)))
    ax = jnp.pad(axial, ((0, 8 - VIEWS), (0, LINE - TAPS)))
    near = lax.dynamic_slice_in_dim(
        jnp.pad(kernel_index, (HALO, HALO)), lax.axis_index("gz") * BLK, NEAR
    )
    labels = incoming_label[0]
    match = labels[None, :] == jnp.arange(VIEWS * BLK, dtype=jnp.int32)[:, None]
    slot = jnp.sum(jnp.where(match, jnp.arange(labels.shape[0], dtype=jnp.int32)[None, :], 0), axis=1)
    cover = jnp.sum(match.astype(jnp.int32).reshape(VIEWS, -1), axis=1)
    return axial, ax, taps[:, :, 0], taps[:, :, 1], near, slot, cover


def shards(estimate, view_tiles, incoming_label, lateral_bank, axial_kernel, kernel_index):
    nx, nz = lax.axis_size("gx"), lax.axis_size("gz")
    tables = small_tables(incoming_label, lateral_bank, axial_kernel, kernel_index)
    axial, ax, kx, ky, near, slot, cover = tables
    outgoing = view_tiles[0].reshape(nx, nz, BLK, LINE)
    return joint_kernel(nx, nz)(near, slot, cover, axial, ax, kx, ky, estimate, outgoing)


def solution(mesh):
    return jax.shard_map(
        shards,
        mesh=mesh,
        in_specs=(P("gz", "gx", None), P(("gx", "gz"), None, None), P(("gx", "gz"), None), P(), P(), P()),
        out_specs=P("gz", "gx", None),
        check_vma=False,
    )
```

```python
import jax
import jax.numpy as jnp
from jax import lax
from jax.experimental import pallas as pl
from jax.experimental.pallas import tpu as pltpu
from jax.sharding import PartitionSpec as P

TAPS = 33
ITERS = 2
HALO = 16
VIEWS = 6
KERNELS = 16
BLK = 16
NEAR = 48
LINE = 128
F32 = jnp.float32
BF = jnp.bfloat16
HI = lax.Precision.HIGHEST


def iota(shape, dim):
    return lax.broadcasted_iota(jnp.int32, shape, dim)


def load_taps(bank_ref, axial_in, kx, ky, ax):
    ax[...] = jnp.zeros_like(ax)
    ax[:VIEWS, :TAPS] = axial_in[...]
    for dim, taps in ((0, kx), (1, ky)):
        taps[...] = jnp.zeros_like(taps)
        for v in range(VIEWS):
            taps[:, v, :TAPS] = bank_ref[v, :, dim, :]
        raw = taps[...]
        total = jnp.sum(raw, axis=-1, keepdims=True)
        taps[...] = raw / jnp.where(total > 0.0, total, 1.0)


def build_bands(kx_ref, ky_ref, ax, fwd_y, bwd_y, fwd_x, bwd_x, first, last):
    inside = jnp.abs(iota((LINE, LINE), 0) - iota((LINE, LINE), 1)) <= HALO
    axial = jnp.sum(ax[...], axis=1, keepdims=True)
    scale = jnp.broadcast_to(1.0 / jnp.where(axial > 0.0, axial, 1.0), (8, LINE))

    @pl.loop(first, last)
    def _(k):
        kx = kx_ref[k]
        ky = ky_ref[k] * scale
        rows = []
        for v in range(VIEWS):
            band = pltpu.roll(jnp.broadcast_to(ky[v : v + 1], (LINE, LINE)), LINE - HALO, 1, stride=1, stride_axis=0)
            band = jnp.where(inside, band, 0.0)
            bwd_y[k, v] = band.astype(BF)
            fwd_y[k, v] = band.T.astype(BF)
            rows.append(pltpu.roll(jnp.broadcast_to(kx[v : v + 1], (BLK, LINE)), 0, 1, stride=1, stride_axis=0))
        across = jnp.concatenate(rows, 0)
        fwd_x[k] = across.astype(BF)
        bwd_x[k] = across.T.astype(BF)


def ones_response(index_of, ax, kx_ref, ky_ref, col0, depth0, edge_x, edge_y, base_ref, cols, depths):
    tap = iota((LINE, LINE), 0)
    pos = iota((LINE, LINE), 1)
    at_x = col0 + pos - tap + HALO
    at_y = pos - tap + HALO
    ok_x = jnp.where((at_x >= 0) & (at_x < cols), 1.0, 0.0)
    ok_y = jnp.where((at_y >= 0) & (at_y < LINE), 1.0, 0.0)
    kx = kx_ref[...].reshape(KERNELS * 8, LINE)
    ky = ky_ref[...].reshape(KERNELS * 8, LINE)
    edge_x[...] = jnp.dot(kx, ok_x, precision=HI, preferred_element_type=F32).reshape(KERNELS, 8, LINE)
    edge_y[...] = jnp.dot(ky, ok_y, precision=HI, preferred_element_type=F32).reshape(KERNELS, 8, LINE)
    axial = ax[...]
    total = jnp.sum(axial, axis=1, keepdims=True)
    axial = axial / jnp.where(total > 0.0, total, 1.0)
    lane = iota((8, LINE), 1)
    for z in range(BLK):
        k = index_of(HALO + z)
        at_z = depth0 + z - lane + HALO
        part = jnp.sum(jnp.where((at_z >= 0) & (at_z < depths), axial, 0.0), axis=1, keepdims=True)
        left = edge_x[k][:, :BLK] * part
        base_ref[z] = lax.dot_general(
            left, edge_y[k], (((0,), (0,)), ((), ())), precision=HI, preferred_element_type=F32
        )


def slots_of(labels, slots):
    column = jnp.broadcast_to(labels, (LINE, LINE)).T
    hit = column == iota((LINE, LINE), 1)
    slots[...] = jnp.max(jnp.where(hit, iota((LINE, LINE), 0), -1), axis=0, keepdims=True)


def lateral_forward(index_of, fwd_x, fwd_y, wide_ref, mid, grown, first, last, unroll):
    @pl.loop(first // unroll, last // unroll)
    def _(s):
        for u in range(unroll):
            z = s * unroll + u
            k = index_of(z)
            mid[z] = jnp.dot(fwd_x[k][:, :NEAR], wide_ref[z], preferred_element_type=F32).astype(BF)

    @pl.loop(first // unroll, last // unroll)
    def _(s):
        for u in range(unroll):
            z = s * unroll + u
            k = index_of(z)
            for v in range(VIEWS):
                grown[v, z] = jnp.dot(mid[z, v * BLK : (v + 1) * BLK, :], fwd_y[k, v], preferred_element_type=F32)


def lateral_backward(index_of, bwd_x, bwd_y, spread, mid, out_ref, first, last, unroll):
    @pl.loop(first // unroll, last // unroll)
    def _(s):
        for u in range(unroll):
            z = s * unroll + u
            k = index_of(z)
            for v in range(VIEWS):
                mid[z, v * BLK : (v + 1) * BLK, :] = jnp.dot(
                    spread[v, z], bwd_y[k, v], preferred_element_type=F32
                ).astype(BF)

    @pl.loop(first // unroll, last // unroll)
    def _(s):
        for u in range(unroll):
            z = s * unroll + u
            k = index_of(z)
            out_ref[z] = jnp.dot(bwd_x[k][:NEAR], mid[z], preferred_element_type=F32).astype(out_ref.dtype)


def taps_over(zi):
    return range(max(0, zi - 2 * HALO), min(BLK - 1, zi) + 1)


def axial_and_ratio(axial_ref, slot_ref, grown, tile_of, spread):
    @pl.loop(0, VIEWS)
    def _(v):
        weights = [axial_ref[v, t] for t in range(TAPS)]
        seen = jnp.full((8, LINE), slot_ref[0, v * BLK], jnp.int32) >= 0
        for half in range(2):
            rows = slice(half * 8, half * 8 + 8)
            total = [None] * BLK
            for zi in range(NEAR):
                g = grown[v, zi, rows, :]
                for zo in taps_over(zi):
                    term = weights[zi - zo] * g
                    total[zo] = term if total[zo] is None else total[zo] + term
            excess = []
            for zo in range(BLK):
                tile = tile_of(jnp.maximum(slot_ref[0, v * BLK + zo], 0))[rows].astype(F32)
                ratio = (tile / total[zo]).astype(BF).astype(F32)
                excess.append(jnp.where(seen, ratio - 1.0, 0.0))
            for zi in range(NEAR):
                acc = None
                for zo in taps_over(zi):
                    term = weights[zi - zo] * excess[zo]
                    acc = term if acc is None else acc + term
                spread[v, zi, rows, :] = acc.astype(BF)


LOW, OWN, HIGH = slice(0, BLK), slice(BLK, 2 * BLK), slice(2 * BLK, NEAR)
MESH = pl.DeviceIdType.MESH


def worker_of(bx, bz):
    turn_x = bx // 4
    y = bx + turn_x * (7 - 2 * bx)
    chip = bz // 2
    turn_z = chip // 4
    x = chip + turn_z * (7 - 2 * chip)
    return 2 * y + turn_x, 4 * x + 2 * ((turn_x + turn_z) % 2) + bz % 2


def column_turn(gz, turn_x):
    x = gz // 4
    turn_z = (turn_x + (gz // 2) % 2) % 2
    return 2 * (x + turn_z * (7 - 2 * x)) + gz % 2


def row_of(gx):
    y = gx // 2
    return y + (gx % 2) * (7 - 2 * y)


class Copy:
    def __init__(self, src, dst, sems, slot, device, sends, receives):
        self.sends, self.receives = sends, receives
        self.copy = pltpu.make_async_remote_copy(
            src_ref=src, dst_ref=dst, send_sem=sems[0].at[slot], recv_sem=sems[1].at[slot],
            device_id=device, device_id_type=MESH,
        )

    def start(self):
        pl.when(self.sends)(self.copy.start)

    def wait_recv(self):
        pl.when(self.receives)(self.copy.wait_recv)

    def wait_send(self):
        pl.when(self.sends)(self.copy.wait_send)


def joint_kernel(nx, nz):
    def body(index_ref, axial_ref, axial_in, bank_ref, labels_ref, estimate_ref, outgoing,
             out_ref, kx, ky, ax, fwd_y, bwd_y, fwd_x, bwd_x, edge_x, edge_y, base, mid, grown, spread, total,
             staged, wide, part_z, part_x, product, back, passing, arrived, labels, slots, slot_ref,
             move_sems, halo_sems, sum_sems, first_sems, second_sems, local_sems):
        gx, gz = lax.axis_index("gx"), lax.axis_index("gz")
        bx = row_of(gx)
        bz = column_turn(gz, gx % 2)
        has_l, has_r, has_d, has_u = bx > 0, bx < nx - 1, bz > 0, bz < nz - 1
        left, right = worker_of((bx + nx - 1) % nx, bz), worker_of((bx + 1) % nx, bz)
        down, up = worker_of(bx, (bz + nz - 1) % nz), worker_of(bx, (bz + 1) % nz)
        worker = worker_of(gx, gz)
        owner = (bx, bz)
        moved = (bx != gx) | (bz != gz)

        def index_of(z):
            return index_ref[jnp.clip(bz * BLK - HALO + z, 0, nz * BLK - 1)]

        staged[...] = estimate_ref[...].astype(BF)
        for it in range(ITERS):
            for missing, rows, columns in (
                (bx == 0, slice(0, NEAR), LOW), (bx == nx - 1, slice(0, NEAR), HIGH),
                (bz == 0, LOW, slice(0, NEAR)), (bz == nz - 1, HIGH, slice(0, NEAR)),
            ):
                @pl.when(missing)
                def _():
                    region = wide.at[it, rows, columns]
                    region[...] = jnp.zeros(region.shape, BF)

        barrier = pltpu.get_barrier_semaphore()

        def greet(device):
            pl.semaphore_signal(barrier, inc=1, device_id=device, device_id_type=MESH)

        for d in range(1, nz):
            greet((gx, (gz + d) % nz))
        for d in range(1, nx):
            greet(((gx + d) % nx, gz))
        for there, device in ((has_l, left), (has_r, right), (has_d, down), (has_u, up), (moved, worker), (moved, owner)):
            pl.when(there)(lambda device=device: greet(device))
        extra = sum(there.astype(jnp.int32) for there in (has_l, has_r, has_d, has_u, moved, moved))
        pl.semaphore_wait(barrier, nx + nz - 2 + extra)

        own_0 = wide.at[0, OWN, OWN]
        moves = [
            Copy(staged, own_0, move_sems, 0, worker, moved, moved),
            Copy(labels_ref, labels, move_sems, 1, worker, moved, moved),
        ]
        bring = Copy(product, back, move_sems, 2, owner, moved, moved)

        def halo(it):
            w = wide.at[it]
            sems = (halo_sems[0].at[it], halo_sems[1].at[it])
            own = w.at[OWN, OWN]
            near = [
                Copy(own, w.at[OWN, LOW], sems, 0, right, has_r, has_l),
                Copy(own, w.at[OWN, HIGH], sems, 1, left, has_l, has_r),
            ]
            far = [
                Copy(own, w.at[LOW, OWN], sems, 2, up, has_u, has_d),
                Copy(own, w.at[HIGH, OWN], sems, 3, down, has_d, has_u),
            ]
            corner = [
                Copy(w.at[OWN, LOW], w.at[LOW, LOW], sems, 4, up, has_u & has_l, has_d & has_l),
                Copy(w.at[OWN, LOW], w.at[HIGH, LOW], sems, 5, down, has_d & has_l, has_u & has_l),
                Copy(w.at[OWN, HIGH], w.at[LOW, HIGH], sems, 6, up, has_u & has_r, has_d & has_r),
                Copy(w.at[OWN, HIGH], w.at[HIGH, HIGH], sems, 7, down, has_d & has_r, has_u & has_r),
            ]
            return near, far, corner

        def sums(it):
            sems = (sum_sems[0].at[it], sum_sems[1].at[it])
            return (
                Copy(total.at[LOW], part_z.at[it, 1], sems, 0, down, has_d, has_u),
                Copy(total.at[HIGH], part_z.at[it, 0], sems, 1, up, has_u, has_d),
                Copy(total.at[OWN, LOW], part_x.at[it, 1], sems, 2, left, has_l, has_r),
                Copy(total.at[OWN, HIGH], part_x.at[it, 0], sems, 3, right, has_r, has_l),
            )

        def quarter(turn, device_gz):
            return slice(4 * turn, 4 * turn + 4), column_turn(device_gz, turn)

        def along_gz(d, turn):
            target = (gz + d) % nz
            rows, column = quarter(turn, target)
            return pltpu.make_async_remote_copy(
                src_ref=outgoing.at[rows, column], dst_ref=passing.at[rows, gz],
                send_sem=first_sems[0].at[d, turn], recv_sem=first_sems[1].at[d, turn],
                device_id=(gx, target), device_id_type=MESH,
            )

        def stay_gz(turn):
            rows, column = quarter(turn, gz)
            return pltpu.make_async_copy(outgoing.at[rows, column], passing.at[rows, gz], local_sems.at[turn])

        def along_gx(d):
            target = (gx + d) % nx
            return pltpu.make_async_remote_copy(
                src_ref=passing.at[row_of(target)], dst_ref=arrived.at[gx],
                send_sem=second_sems[0].at[d], recv_sem=second_sems[1].at[d],
                device_id=(target, gz), device_id_type=MESH,
            )

        stay_gx = pltpu.make_async_copy(passing.at[bx], arrived.at[gx], local_sems.at[2])
        slot_copy = pltpu.make_async_copy(slots, slot_ref, local_sems.at[3])
        ends = [(d, turn) for d in range(1, nz) for turn in range(2)]

        for copy in moves:
            copy.start()

        @pl.when(jnp.logical_not(moved))
        def _():
            wide[0, OWN, OWN] = staged[...]
            labels[...] = labels_ref[...]

        for turn in range(2):
            stay_gz(turn).start()
        for d, turn in ends:
            along_gz(d, turn).start()
        load_taps(bank_ref, axial_in, kx, ky, ax)
        build_bands(kx, ky, ax, fwd_y, bwd_y, fwd_x, bwd_x, 0, KERNELS // 2)
        for copy in moves:
            copy.wait_recv()

        for it in range(ITERS):
            near, far, corner = halo(it)
            for copy in near + far:
                copy.start()
            if it == 0:
                build_bands(kx, ky, ax, fwd_y, bwd_y, fwd_x, bwd_x, KERNELS // 2, KERNELS)
            for copy in near:
                copy.wait_recv()
            for copy in corner:
                copy.start()
            if it == 0:
                slots_of(labels[...], slots)
                slot_copy.start()
                ones_response(index_of, ax, kx, ky, bx * BLK, bz * BLK, edge_x, edge_y, base, nx * BLK, nz * BLK)
            lateral_forward(index_of, fwd_x, fwd_y, wide.at[it], mid, grown, BLK, 2 * BLK, 4)
            if it == 0:
                for turn in range(2):
                    stay_gz(turn).wait()
                for d, turn in ends:
                    along_gz(d, turn).wait_recv()
                for d in range(1, nx):
                    along_gx(d).start()
                stay_gx.start()
            for copy in far + corner:
                copy.wait_recv()
            lateral_forward(index_of, fwd_x, fwd_y, wide.at[it], mid, grown, 0, BLK, 4)
            lateral_forward(index_of, fwd_x, fwd_y, wide.at[it], mid, grown, 2 * BLK, NEAR, 4)
            if it == 0:
                for d, turn in ends:
                    along_gz(d, turn).wait_send()
                for d in range(1, nx):
                    along_gx(d).wait()
                stay_gx.wait()
                slot_copy.wait()
                for copy in moves:
                    copy.wait_send()
            for copy in near + far + corner:
                copy.wait_send()

            axial_and_ratio(axial_ref, slot_ref, grown, lambda s: arrived[s // nz, s % nz], spread)
            below, above, to_left, to_right = sums(it)
            lateral_backward(index_of, bwd_x, bwd_y, spread, mid, total, 0, BLK, 4)
            below.start()
            lateral_backward(index_of, bwd_x, bwd_y, spread, mid, total, 2 * BLK, NEAR, 4)
            above.start()
            lateral_backward(index_of, bwd_x, bwd_y, spread, mid, total, BLK, 2 * BLK, 4)
            below.wait_recv()
            above.wait_recv()
            for there, which in ((has_d, 0), (has_u, 1)):
                @pl.when(there)
                def _():
                    total[OWN] += part_z[it, which]
            to_left.start()
            to_right.start()
            base_now = base[...] + total[OWN, OWN]
            gain = (1.0 / VIEWS) if it == 0 else product[...] * (1.0 / VIEWS)
            to_left.wait_recv()
            to_right.wait_recv()
            left_part = jnp.where(has_l, part_x[it, 0], 0.0)
            right_part = jnp.where(has_r, part_x[it, 1], 0.0)
            product[...] = (base_now + left_part + right_part) * gain
            if it + 1 < ITERS:
                wide[it + 1, OWN, OWN] = (wide[it, OWN, OWN].astype(F32) * product[...]).astype(BF)
            else:
                bring.start()
            for copy in (below, above, to_left, to_right):
                copy.wait_send()

        @pl.when(jnp.logical_not(moved))
        def _():
            back[...] = product[...]

        bring.wait_recv()
        out_ref[...] = estimate_ref[...] * back[...]
        bring.wait_send()

    smem = pl.BlockSpec(memory_space=pltpu.SMEM)
    vmem = pl.BlockSpec(memory_space=pltpu.VMEM)
    dma = pltpu.SemaphoreType.DMA
    block = (BLK, BLK, LINE)
    return pl.pallas_call(
        body,
        name="joint",
        out_shape=jax.ShapeDtypeStruct(block, F32),
        in_specs=[smem] * 2 + [vmem] * 4 + [pl.BlockSpec(memory_space=pl.ANY)],
        out_specs=vmem,
        scratch_shapes=[
            pltpu.VMEM((KERNELS, 8, LINE), F32),
            pltpu.VMEM((KERNELS, 8, LINE), F32),
            pltpu.VMEM((8, LINE), F32),
            pltpu.VMEM((KERNELS, VIEWS, LINE, LINE), BF),
            pltpu.VMEM((KERNELS, VIEWS, LINE, LINE), BF),
            pltpu.VMEM((KERNELS, VIEWS * BLK, LINE), BF),
            pltpu.VMEM((KERNELS, LINE, VIEWS * BLK), BF),
            pltpu.VMEM((KERNELS, 8, LINE), F32),
            pltpu.VMEM((KERNELS, 8, LINE), F32),
            pltpu.VMEM(block, F32),
            pltpu.VMEM((NEAR, VIEWS * BLK, LINE), BF),
            pltpu.VMEM((VIEWS, NEAR, BLK, LINE), F32),
            pltpu.VMEM((VIEWS, NEAR, BLK, LINE), BF),
            pltpu.VMEM((NEAR, NEAR, LINE), F32),
            pltpu.VMEM(block, BF),
            pltpu.VMEM((ITERS, NEAR, NEAR, LINE), BF),
            pltpu.VMEM((ITERS, 2, BLK, NEAR, LINE), F32),
            pltpu.VMEM((ITERS, 2) + block, F32),
            pltpu.VMEM(block, F32),
            pltpu.VMEM(block, F32),
            pltpu.VMEM((nx, nz, BLK, LINE), BF),
            pltpu.VMEM((nx, nz, BLK, LINE), BF),
            pltpu.VMEM((1, LINE), jnp.int32),
            pltpu.VMEM((1, LINE), jnp.int32),
            pltpu.SMEM((1, LINE), jnp.int32),
            (dma((3,)), dma((3,))),
            (dma((ITERS, 8)), dma((ITERS, 8))),
            (dma((ITERS, 4)), dma((ITERS, 4))),
            (dma((nz, 2)), dma((nz, 2))),
            (dma((nx,)), dma((nx,))),
            dma((4,)),
        ],
        compiler_params=pltpu.CompilerParams(
            vmem_limit_bytes=48 << 20, collective_id=0, has_side_effects=True
        ),
    )


def shards(estimate, view_tiles, incoming_label, lateral_bank, axial_kernel, kernel_index):
    nx, nz = lax.axis_size("gx"), lax.axis_size("gz")
    outgoing = view_tiles[0].reshape(nx, nz, BLK, LINE)
    return joint_kernel(nx, nz)(
        kernel_index, axial_kernel, axial_kernel, lateral_bank, incoming_label, estimate, outgoing
    )


def solution(mesh):
    return jax.shard_map(
        shards,
        mesh=mesh,
        in_specs=(P("gz", "gx", None), P(("gx", "gz"), None, None), P(("gx", "gz"), None), P(), P(), P()),
        out_specs=P("gz", "gx", None),
        check_vma=False,
    )
```

```python
import jax
import jax.numpy as jnp
from jax import lax
from jax.experimental import pallas as pl
from jax.experimental.pallas import tpu as pltpu
from jax.sharding import PartitionSpec as P

TAPS = 33
ITERS = 2
HALO = 16
VIEWS = 6
KERNELS = 16
BLK = 16
NEAR = 48
UNROLL = 8
LINE = 128
F32 = jnp.float32
BF = jnp.bfloat16
HI = lax.Precision.HIGHEST


def iota(shape, dim):
    return lax.broadcasted_iota(jnp.int32, shape, dim)


def load_taps(bank_ref, axial_in, kx, ky, ax):
    ax[...] = jnp.zeros_like(ax)
    ax[:VIEWS, :TAPS] = axial_in[...]
    for dim, taps in ((0, kx), (1, ky)):
        taps[...] = jnp.zeros_like(taps)
        for v in range(VIEWS):
            taps[:, v, :TAPS] = bank_ref[v, :, dim, :]
        raw = taps[...]
        total = jnp.sum(raw, axis=-1, keepdims=True)
        taps[...] = raw / jnp.where(total > 0.0, total, 1.0)


def build_bands(kx_ref, ky_ref, ax, fwd_y, bwd_y, fwd_x, bwd_x, first, last):
    inside = jnp.abs(iota((LINE, LINE), 0) - iota((LINE, LINE), 1)) <= HALO
    axial = jnp.sum(ax[...], axis=1, keepdims=True)
    scale = jnp.broadcast_to(1.0 / jnp.where(axial > 0.0, axial, 1.0), (8, LINE))

    @pl.loop(first, last)
    def _(k):
        kx = kx_ref[k]
        ky = ky_ref[k] * scale
        rows = []
        for v in range(VIEWS):
            band = pltpu.roll(jnp.broadcast_to(ky[v : v + 1], (LINE, LINE)), LINE - HALO, 1, stride=1, stride_axis=0)
            band = jnp.where(inside, band, 0.0)
            bwd_y[k, v] = band.astype(BF)
            fwd_y[k, v] = band.T.astype(BF)
            rows.append(pltpu.roll(jnp.broadcast_to(kx[v : v + 1], (BLK, LINE)), 0, 1, stride=1, stride_axis=0))
        across = jnp.concatenate(rows, 0)
        fwd_x[k] = across.astype(BF)
        bwd_x[k] = across.T.astype(BF)


def ones_response(index_of, ax, kx_ref, ky_ref, col0, depth0, edge_x, edge_y, base_ref, cols, depths):
    tap = iota((LINE, LINE), 0)
    pos = iota((LINE, LINE), 1)
    at_x = col0 + pos - tap + HALO
    at_y = pos - tap + HALO
    ok_x = jnp.where((at_x >= 0) & (at_x < cols), 1.0, 0.0)
    ok_y = jnp.where((at_y >= 0) & (at_y < LINE), 1.0, 0.0)
    kx = kx_ref[...].reshape(KERNELS * 8, LINE)
    ky = ky_ref[...].reshape(KERNELS * 8, LINE)
    edge_x[...] = jnp.dot(kx, ok_x, precision=HI, preferred_element_type=F32).reshape(KERNELS, 8, LINE)
    edge_y[...] = jnp.dot(ky, ok_y, precision=HI, preferred_element_type=F32).reshape(KERNELS, 8, LINE)
    axial = ax[...]
    total = jnp.sum(axial, axis=1, keepdims=True)
    axial = axial / jnp.where(total > 0.0, total, 1.0)
    lane = iota((8, LINE), 1)
    for z in range(BLK):
        k = index_of(HALO + z)
        at_z = depth0 + z - lane + HALO
        part = jnp.sum(jnp.where((at_z >= 0) & (at_z < depths), axial, 0.0), axis=1, keepdims=True)
        left = edge_x[k][:, :BLK] * part
        base_ref[z] = lax.dot_general(
            left, edge_y[k], (((0,), (0,)), ((), ())), precision=HI, preferred_element_type=F32
        )


def slots_of(labels, slots):
    column = jnp.broadcast_to(labels, (LINE, LINE)).T
    hit = column == iota((LINE, LINE), 1)
    slots[...] = jnp.max(jnp.where(hit, iota((LINE, LINE), 0), -1), axis=0, keepdims=True)


def lateral_forward(index_of, fwd_x, fwd_y, wide, mid, grown, first, count, unroll):
    @pl.loop(0, count // unroll)
    def _(s):
        start = first + s * unroll
        kernels = [index_of(start + u) for u in range(unroll)]
        for u, k in enumerate(kernels):
            mid[start + u] = jnp.dot(fwd_x[k][:, :NEAR], wide[start + u], preferred_element_type=F32).astype(BF)
        for u, k in enumerate(kernels):
            for v in range(VIEWS):
                grown[v, start + u] = jnp.dot(
                    mid[start + u, v * BLK : (v + 1) * BLK, :], fwd_y[k, v], preferred_element_type=F32
                )


def lateral_backward(index_of, bwd_x, bwd_y, spread, mid, total, first, count, unroll):
    @pl.loop(0, count // unroll)
    def _(s):
        start = first + s * unroll
        kernels = [index_of(start + u) for u in range(unroll)]
        for u, k in enumerate(kernels):
            for v in range(VIEWS):
                mid[start + u, v * BLK : (v + 1) * BLK, :] = jnp.dot(
                    spread[v, start + u], bwd_y[k, v], preferred_element_type=F32
                ).astype(BF)
        for u, k in enumerate(kernels):
            total[start + u] = jnp.dot(bwd_x[k][:NEAR], mid[start + u], preferred_element_type=F32)


def taps_over(zi):
    return range(max(0, zi - 2 * HALO), min(BLK - 1, zi) + 1)


def axial_and_ratio(axial_ref, slot_ref, grown, tile_of, spread):
    @pl.loop(0, VIEWS)
    def _(v):
        weights = [axial_ref[v, t] for t in range(TAPS)]
        seen = jnp.full((8, LINE), slot_ref[0, v * BLK], jnp.int32) >= 0
        for half in range(2):
            rows = slice(half * 8, half * 8 + 8)
            total = [None] * BLK
            for zi in range(NEAR):
                g = grown[v, zi, rows, :]
                for zo in taps_over(zi):
                    term = weights[zi - zo] * g
                    total[zo] = term if total[zo] is None else total[zo] + term
            excess = []
            for zo in range(BLK):
                tile = tile_of(jnp.maximum(slot_ref[0, v * BLK + zo], 0))[rows].astype(F32)
                ratio = (tile / total[zo]).astype(BF).astype(F32)
                excess.append(jnp.where(seen, ratio - 1.0, 0.0))
            for zi in range(NEAR):
                acc = None
                for zo in taps_over(zi):
                    term = weights[zi - zo] * excess[zo]
                    acc = term if acc is None else acc + term
                spread[v, zi, rows, :] = acc.astype(BF)


LOW, OWN, HIGH = slice(0, BLK), slice(BLK, 2 * BLK), slice(2 * BLK, NEAR)
MESH = pl.DeviceIdType.MESH


class Copy:
    def __init__(self, src, dst, sems, slot, device, sends, receives):
        self.src, self.sems, self.slot = src, sems, slot
        self.sends, self.receives = sends, receives
        self.out = self.back = self.make(dst, device)
        self.device = device

    def make(self, dst, device):
        return pltpu.make_async_remote_copy(
            src_ref=self.src, dst_ref=dst, send_sem=self.sems[0].at[self.slot], recv_sem=self.sems[1].at[self.slot],
            device_id=device, device_id_type=MESH,
        )

    def lands_in(self, region):
        self.back = self.make(region, self.device)

    def start(self):
        pl.when(self.sends)(self.out.start)

    def wait_recv(self):
        pl.when(self.receives)(self.back.wait_recv)

    def wait_send(self):
        pl.when(self.sends)(self.out.wait_send)


def joint_kernel(nx, nz):
    def body(index_ref, axial_ref, axial_in, bank_ref, labels_ref, estimate_ref, outgoing,
             out_ref, kx, ky, ax, fwd_y, bwd_y, fwd_x, bwd_x, edge_x, edge_y, base, mid, grown, spread, total,
             wide, part_mate, part, passing, arrived, slots, slot_ref,
             halo_sems, sum_sems, first_sems, second_sems, local_sems):
        gx, gz = lax.axis_index("gx"), lax.axis_index("gz")
        core = gz % 2
        has_l, has_r = gx > 0, gx < nx - 1
        across = gz - 1 + 2 * core
        has_c = (across >= 0) & (across < nz)
        across = (across + nz) % nz
        gl, gr = (gx + nx - 1) % nx, (gx + 1) % nx
        mate = (gx, gz + 1 - 2 * core)
        mate_rows, cross_rows = pl.ds(2 * BLK * (1 - core), BLK), pl.ds(2 * BLK * core, BLK)
        at_mate, at_cross = cross_rows, mate_rows

        def index_of(z):
            return index_ref[jnp.clip(gz * BLK - HALO + z, 0, nz * BLK - 1)]

        wide[0, OWN, OWN] = estimate_ref[...].astype(BF)
        for it in range(ITERS):
            for missing, rows, columns in (
                (gx == 0, slice(0, NEAR), LOW), (gx == nx - 1, slice(0, NEAR), HIGH),
                (gz == 0, LOW, slice(0, NEAR)), (gz == nz - 1, HIGH, slice(0, NEAR)),
            ):
                @pl.when(missing)
                def _():
                    region = wide.at[it, rows, columns]
                    region[...] = jnp.zeros(region.shape, BF)

        barrier = pltpu.get_barrier_semaphore()

        def greet(device):
            pl.semaphore_signal(barrier, inc=1, device_id=device, device_id_type=MESH)

        for d in range(1, nz):
            greet((gx, (gz + d) % nz))
        for d in range(1, nx):
            greet(((gx + d) % nx, gz))
        pl.when(has_c & has_l)(lambda: greet((gl, across)))
        pl.when(has_c & has_r)(lambda: greet((gr, across)))
        extra = (has_c & has_l).astype(jnp.int32) + (has_c & has_r).astype(jnp.int32)
        pl.semaphore_wait(barrier, nx + nz - 2 + extra)

        def halo(it):
            w = wide.at[it]
            sems = (halo_sems[0].at[it], halo_sems[1].at[it])
            own = w.at[OWN, OWN]
            near = [
                Copy(own, w.at[OWN, LOW], sems, 0, (gr, gz), has_r, has_l),
                Copy(own, w.at[OWN, HIGH], sems, 1, (gl, gz), has_l, has_r),
            ]
            far = [
                Copy(own, w.at[at_mate, OWN], sems, 2, mate, True, True),
                Copy(own, w.at[at_cross, LOW], sems, 3, (gr, across), has_c & has_r, has_c & has_l),
                Copy(own, w.at[at_cross, HIGH], sems, 4, (gl, across), has_c & has_l, has_c & has_r),
                Copy(own, w.at[at_cross, OWN], sems, 5, (gx, across), has_c, has_c),
            ]
            relay = [
                Copy(w.at[OWN, LOW], w.at[at_mate, LOW], sems, 6, mate, has_l, has_l),
                Copy(w.at[OWN, HIGH], w.at[at_mate, HIGH], sems, 7, mate, has_r, has_r),
            ]
            for copy, rows, columns in (
                (far[0], mate_rows, OWN), (far[1], cross_rows, LOW), (far[2], cross_rows, HIGH),
                (far[3], cross_rows, OWN), (relay[0], mate_rows, LOW), (relay[1], mate_rows, HIGH),
            ):
                copy.lands_in(w.at[rows, columns])
            return near, far, relay

        def sums(it):
            sems = (sum_sems[0].at[it], sum_sems[1].at[it])
            p = part.at[it]
            to_mate = Copy(total.at[mate_rows], part_mate.at[it], sems, 0, mate, True, True)
            to_cross = [
                Copy(total.at[cross_rows, LOW], p.at[2], sems, 1, (gl, across), has_c & has_l, has_c & has_r),
                Copy(total.at[cross_rows, HIGH], p.at[1], sems, 2, (gr, across), has_c & has_r, has_c & has_l),
                Copy(total.at[cross_rows, OWN], p.at[0], sems, 3, (gx, across), has_c, has_c),
            ]
            aside = []
            for half in range(2):
                rows = slice(BLK + 8 * half, BLK + 8 * half + 8)
                there = slice(8 * half, 8 * half + 8)
                aside.append([
                    Copy(total.at[rows, LOW], p.at[4, there], sems, 4 + 2 * half, (gl, gz), has_l, has_r),
                    Copy(total.at[rows, HIGH], p.at[3, there], sems, 5 + 2 * half, (gr, gz), has_r, has_l),
                ])
            return to_mate, to_cross, aside

        def along_gz(d):
            target = (gz + d) % nz
            return pltpu.make_async_remote_copy(
                src_ref=outgoing.at[:, target], dst_ref=passing.at[:, gz],
                send_sem=first_sems[0].at[d], recv_sem=first_sems[1].at[d],
                device_id=(gx, target), device_id_type=MESH,
            )

        def along_gx(d):
            target = (gx + d) % nx
            return pltpu.make_async_remote_copy(
                src_ref=passing.at[target], dst_ref=arrived.at[gx],
                send_sem=second_sems[0].at[d], recv_sem=second_sems[1].at[d],
                device_id=(target, gz), device_id_type=MESH,
            )

        stay_gz = pltpu.make_async_copy(outgoing.at[:, gz], passing.at[:, gz], local_sems.at[0])
        stay_gx = pltpu.make_async_copy(passing.at[gx], arrived.at[gx], local_sems.at[1])
        slot_copy = pltpu.make_async_copy(slots, slot_ref, local_sems.at[2])

        for it in range(ITERS):
            w = wide.at[it]
            near, far, relay = halo(it)
            for copy in near + far:
                copy.start()
            if it == 0:
                stay_gz.start()
                for d in range(1, nz):
                    along_gz(d).start()
                slots_of(labels_ref[...], slots)
                slot_copy.start()
                load_taps(bank_ref, axial_in, kx, ky, ax)
                build_bands(kx, ky, ax, fwd_y, bwd_y, fwd_x, bwd_x, 0, KERNELS)
            for copy in near:
                copy.wait_recv()
            for copy in relay:
                copy.start()
            lateral_forward(index_of, fwd_x, fwd_y, w, mid, grown, BLK, BLK, UNROLL)
            if it == 0:
                stay_gz.wait()
                for d in range(1, nz):
                    along_gz(d).wait_recv()
                for d in range(1, nx):
                    along_gx(d).start()
                stay_gx.start()
            for copy in [far[0]] + relay:
                copy.wait_recv()
            lateral_forward(index_of, fwd_x, fwd_y, w, mid, grown, 2 * BLK * (1 - core), BLK, UNROLL)
            for copy in far[1:]:
                copy.wait_recv()
            lateral_forward(index_of, fwd_x, fwd_y, w, mid, grown, 2 * BLK * core, BLK, UNROLL)
            if it == 0:
                ones_response(index_of, ax, kx, ky, gx * BLK, gz * BLK, edge_x, edge_y, base, nx * BLK, nz * BLK)
                for d in range(1, nz):
                    along_gz(d).wait_send()
                for d in range(1, nx):
                    along_gx(d).wait()
                stay_gx.wait()
                slot_copy.wait()
            for copy in near + far + relay:
                copy.wait_send()

            axial_and_ratio(axial_ref, slot_ref, grown, lambda s: arrived[s // nz, s % nz], spread)
            to_mate, to_cross, aside = sums(it)
            lateral_backward(index_of, bwd_x, bwd_y, spread, mid, total, 2 * BLK * core, BLK, UNROLL)
            for copy in to_cross:
                copy.start()
            lateral_backward(index_of, bwd_x, bwd_y, spread, mid, total, 2 * BLK * (1 - core), BLK, UNROLL)
            to_mate.start()
            for half in range(2):
                first = BLK + 8 * half
                lateral_backward(index_of, bwd_x, bwd_y, spread, mid, total, first, 8, UNROLL)
                if half == 0:
                    to_mate.wait_recv()
                total[first : first + 8] += part_mate[it, 8 * half : 8 * half + 8]
                for copy in aside[half]:
                    copy.start()
            inner = base[...] + total[OWN, OWN]
            for copy in to_cross:
                copy.wait_recv()
            for there, which in ((has_c, 0), (has_c & has_l, 1), (has_c & has_r, 2)):
                inner = inner + jnp.where(there, part[it, which], 0.0)
            before = estimate_ref if it == 0 else out_ref
            scaled = before[...] * (1.0 / VIEWS)
            for pair in aside:
                for copy in pair:
                    copy.wait_recv()
            for there, which in ((has_l, 3), (has_r, 4)):
                inner = inner + jnp.where(there, part[it, which], 0.0)
            after = scaled * inner
            out_ref[...] = after
            if it + 1 < ITERS:
                wide[it + 1, OWN, OWN] = after.astype(BF)
            for copy in [to_mate] + to_cross + aside[0] + aside[1]:
                copy.wait_send()

    smem = pl.BlockSpec(memory_space=pltpu.SMEM)
    vmem = pl.BlockSpec(memory_space=pltpu.VMEM)
    dma = pltpu.SemaphoreType.DMA
    block = (BLK, BLK, LINE)
    return pl.pallas_call(
        body,
        name="joint",
        out_shape=jax.ShapeDtypeStruct(block, F32),
        in_specs=[smem] * 2 + [vmem] * 4 + [pl.BlockSpec(memory_space=pl.ANY)],
        out_specs=vmem,
        scratch_shapes=[
            pltpu.VMEM((KERNELS, 8, LINE), F32),
            pltpu.VMEM((KERNELS, 8, LINE), F32),
            pltpu.VMEM((8, LINE), F32),
            pltpu.VMEM((KERNELS, VIEWS, LINE, LINE), BF),
            pltpu.VMEM((KERNELS, VIEWS, LINE, LINE), BF),
            pltpu.VMEM((KERNELS, VIEWS * BLK, LINE), BF),
            pltpu.VMEM((KERNELS, LINE, VIEWS * BLK), BF),
            pltpu.VMEM((KERNELS, 8, LINE), F32),
            pltpu.VMEM((KERNELS, 8, LINE), F32),
            pltpu.VMEM(block, F32),
            pltpu.VMEM((NEAR, VIEWS * BLK, LINE), BF),
            pltpu.VMEM((VIEWS, NEAR, BLK, LINE), F32),
            pltpu.VMEM((VIEWS, NEAR, BLK, LINE), BF),
            pltpu.VMEM((NEAR, NEAR, LINE), F32),
            pltpu.VMEM((ITERS, NEAR, NEAR, LINE), BF),
            pltpu.VMEM((ITERS, BLK, NEAR, LINE), F32),
            pltpu.VMEM((ITERS, 5) + block, F32),
            pltpu.VMEM((nx, nz, BLK, LINE), BF),
            pltpu.VMEM((nx, nz, BLK, LINE), BF),
            pltpu.VMEM((1, LINE), jnp.int32),
            pltpu.SMEM((1, LINE), jnp.int32),
            (dma((ITERS, 8)), dma((ITERS, 8))),
            (dma((ITERS, 8)), dma((ITERS, 8))),
            (dma((nz,)), dma((nz,))),
            (dma((nx,)), dma((nx,))),
            dma((3,)),
        ],
        compiler_params=pltpu.CompilerParams(
            vmem_limit_bytes=48 << 20, collective_id=0, has_side_effects=True
        ),
    )


def shards(estimate, view_tiles, incoming_label, lateral_bank, axial_kernel, kernel_index):
    nx, nz = lax.axis_size("gx"), lax.axis_size("gz")
    outgoing = view_tiles[0].reshape(nx, nz, BLK, LINE)
    return joint_kernel(nx, nz)(
        kernel_index, axial_kernel, axial_kernel, lateral_bank, incoming_label, estimate, outgoing
    )


def solution(mesh):
    return jax.shard_map(
        shards,
        mesh=mesh,
        in_specs=(P("gz", "gx", None), P(("gx", "gz"), None, None), P(("gx", "gz"), None), P(), P(), P()),
        out_specs=P("gz", "gx", None),
        check_vma=False,
    )
```

```python
import jax
import jax.numpy as jnp
from jax import lax
from jax.experimental import pallas as pl
from jax.experimental.pallas import tpu as pltpu
from jax.sharding import PartitionSpec as P

TAPS = 33
ITERS = 2
HALO = 16
VIEWS = 6
KERNELS = 16
BLK = 16
NEAR = 48
UNROLL = 8
LINE = 128
F32 = jnp.float32
BF = jnp.bfloat16
HI = lax.Precision.HIGHEST


def iota(shape, dim):
    return lax.broadcasted_iota(jnp.int32, shape, dim)


def load_taps(bank_ref, axial_in, kx, ky, ax):
    ax[...] = jnp.zeros_like(ax)
    ax[:VIEWS, :TAPS] = axial_in[...]
    for dim, taps in ((0, kx), (1, ky)):
        taps[...] = jnp.zeros_like(taps)
        for v in range(VIEWS):
            taps[:, v, :TAPS] = bank_ref[v, :, dim, :]
        raw = taps[...]
        total = jnp.sum(raw, axis=-1, keepdims=True)
        taps[...] = raw / jnp.where(total > 0.0, total, 1.0)


def line_scale(ax):
    axial = jnp.sum(ax[...], axis=1, keepdims=True)
    return jnp.broadcast_to(1.0 / jnp.where(axial > 0.0, axial, 1.0), (8, LINE))


def reverse_taps(ky, ky_back):
    flip = jnp.where(iota((LINE, LINE), 0) + iota((LINE, LINE), 1) == TAPS - 1, 1.0, 0.0)
    taps = ky[...].reshape(KERNELS * 8, LINE)
    ky_back[...] = jnp.dot(taps, flip, precision=HI, preferred_element_type=F32).reshape(KERNELS, 8, LINE)


def build_bands(ky, kx, ax, bands_y, bands_x, spread_out):
    inside = jnp.abs(iota((LINE, LINE), 0) - iota((LINE, LINE), 1)) <= HALO
    scale = line_scale(ax)

    @pl.loop(0, KERNELS)
    def _(k):
        taps_x = kx[k]
        taps_y = ky[k] * scale
        rows = []
        for v in range(VIEWS):
            band = jnp.broadcast_to(taps_y[v : v + 1], (LINE, LINE))
            band = pltpu.roll(band, LINE - HALO, 1, stride=1, stride_axis=0)
            bands_y[k, v] = jnp.where(inside, band, 0.0).astype(BF)
            rows.append(pltpu.roll(jnp.broadcast_to(taps_x[v : v + 1], (BLK, LINE)), 0, 1, stride=1, stride_axis=0))
        across = jnp.concatenate(rows, 0)
        bands_x[k] = (across.T if spread_out else across).astype(BF)


def ones_response(index_of, ax, kx_ref, ky_ref, col0, depth0, edge_x, edge_y, base_ref, cols, depths):
    tap = iota((LINE, LINE), 0)
    pos = iota((LINE, LINE), 1)
    at_x = col0 + pos - tap + HALO
    at_y = pos - tap + HALO
    ok_x = jnp.where((at_x >= 0) & (at_x < cols), 1.0, 0.0)
    ok_y = jnp.where((at_y >= 0) & (at_y < LINE), 1.0, 0.0)
    kx = kx_ref[...].reshape(KERNELS * 8, LINE)
    ky = ky_ref[...].reshape(KERNELS * 8, LINE)
    edge_x[...] = jnp.dot(kx, ok_x, precision=HI, preferred_element_type=F32).reshape(KERNELS, 8, LINE)
    edge_y[...] = jnp.dot(ky, ok_y, precision=HI, preferred_element_type=F32).reshape(KERNELS, 8, LINE)
    axial = ax[...]
    total = jnp.sum(axial, axis=1, keepdims=True)
    axial = axial / jnp.where(total > 0.0, total, 1.0)
    lane = iota((8, LINE), 1)
    for z in range(BLK):
        k = index_of(HALO + z)
        at_z = depth0 + z - lane + HALO
        part = jnp.sum(jnp.where((at_z >= 0) & (at_z < depths), axial, 0.0), axis=1, keepdims=True)
        left = edge_x[k][:, :BLK] * part
        base_ref[z] = lax.dot_general(
            left, edge_y[k], (((0,), (0,)), ((), ())), precision=HI, preferred_element_type=F32
        )


def slots_of(labels, slots):
    column = jnp.broadcast_to(labels, (LINE, LINE)).T
    hit = column == iota((LINE, LINE), 1)
    slots[...] = jnp.max(jnp.where(hit, iota((LINE, LINE), 0), -1), axis=0, keepdims=True)


def lateral_forward(index_of, fwd_x, fwd_y, wide, mid, grown, first, count, unroll):
    @pl.loop(0, count // unroll)
    def _(s):
        start = first + s * unroll
        kernels = [index_of(start + u) for u in range(unroll)]
        for u, k in enumerate(kernels):
            mid[start + u] = jnp.dot(fwd_x[k][:, :NEAR], wide[start + u], preferred_element_type=F32).astype(BF)
        for u, k in enumerate(kernels):
            for v in range(VIEWS):
                grown[v, start + u] = jnp.dot(
                    mid[start + u, v * BLK : (v + 1) * BLK, :], fwd_y[k, v], preferred_element_type=F32
                )


def lateral_backward(index_of, bwd_x, bwd_y, spread, mid, total, shift, first, count, unroll):
    @pl.loop(0, count // unroll)
    def _(s):
        start = first + s * unroll
        kernels = [index_of(start + u) for u in range(unroll)]
        for u, k in enumerate(kernels):
            for v in range(VIEWS):
                mid[start + u, v * BLK : (v + 1) * BLK, :] = jnp.dot(
                    spread[v, start + u], bwd_y[k, v], preferred_element_type=F32
                ).astype(BF)
        for u, k in enumerate(kernels):
            total[start + u - shift] = jnp.dot(bwd_x[k][:NEAR], mid[start + u], preferred_element_type=F32).astype(total.dtype)


def taps_over(zi):
    return range(max(0, zi - 2 * HALO), min(BLK - 1, zi) + 1)


def axial_and_ratio(axial_ref, slot_ref, grown, tile_of, spread):
    @pl.loop(0, VIEWS)
    def _(v):
        weights = [axial_ref[v, t] for t in range(TAPS)]
        seen = jnp.full((8, LINE), slot_ref[0, v * BLK], jnp.int32) >= 0
        for half in range(2):
            rows = slice(half * 8, half * 8 + 8)
            total = [None] * BLK
            for zi in range(NEAR):
                g = grown[v, zi, rows, :]
                for zo in taps_over(zi):
                    term = weights[zi - zo] * g
                    total[zo] = term if total[zo] is None else total[zo] + term
            excess = []
            for zo in range(BLK):
                tile = tile_of(jnp.maximum(slot_ref[0, v * BLK + zo], 0))[rows].astype(F32)
                ratio = (tile / total[zo]).astype(BF).astype(F32)
                excess.append(jnp.where(seen, ratio - 1.0, 0.0))
            for zi in range(NEAR):
                acc = None
                for zo in taps_over(zi):
                    term = weights[zi - zo] * excess[zo]
                    acc = term if acc is None else acc + term
                spread[v, zi, rows, :] = acc.astype(BF)


LOW, OWN, HIGH = slice(0, BLK), slice(BLK, 2 * BLK), slice(2 * BLK, NEAR)
MESH = pl.DeviceIdType.MESH


class Copy:
    def __init__(self, src, dst, sems, slot, device, sends, receives):
        self.src, self.sems, self.slot = src, sems, slot
        self.sends, self.receives = sends, receives
        self.out = self.back = self.make(dst, device)
        self.device = device

    def make(self, dst, device):
        return pltpu.make_async_remote_copy(
            src_ref=self.src, dst_ref=dst, send_sem=self.sems[0].at[self.slot], recv_sem=self.sems[1].at[self.slot],
            device_id=device, device_id_type=MESH,
        )

    def lands_in(self, region):
        self.back = self.make(region, self.device)

    def start(self):
        pl.when(self.sends)(self.out.start)

    def wait_recv(self):
        pl.when(self.receives)(self.back.wait_recv)

    def wait_send(self):
        pl.when(self.sends)(self.out.wait_send)


def joint_kernel(nx, nz):
    def body(index_ref, axial_ref, axial_in, bank_ref, labels_ref, estimate_ref, outgoing,
             out_ref, kx, ky, ky_back, ax, fwd_y, bwd_y, fwd_x, bwd_x, edge_x, edge_y, base, mid, grown, spread, total,
             to_far, to_side, wide, part_mate, part, passing, arrived, slots, slot_ref,
             halo_sems, sum_sems, first_sems, second_sems, local_sems):
        gx, gz = lax.axis_index("gx"), lax.axis_index("gz")
        core = gz % 2
        has_l, has_r = gx > 0, gx < nx - 1
        across = gz - 1 + 2 * core
        has_c = (across >= 0) & (across < nz)
        across = (across + nz) % nz
        gl, gr = (gx + nx - 1) % nx, (gx + 1) % nx
        mate = (gx, gz + 1 - 2 * core)
        mate_rows, cross_rows = pl.ds(2 * BLK * (1 - core), BLK), pl.ds(2 * BLK * core, BLK)
        at_mate, at_cross = cross_rows, mate_rows

        def index_of(z):
            return index_ref[jnp.clip(gz * BLK - HALO + z, 0, nz * BLK - 1)]

        wide[0, OWN, OWN] = estimate_ref[...].astype(BF)
        for it in range(ITERS):
            for missing, rows, columns in (
                (gx == 0, slice(0, NEAR), LOW), (gx == nx - 1, slice(0, NEAR), HIGH),
                (gz == 0, LOW, slice(0, NEAR)), (gz == nz - 1, HIGH, slice(0, NEAR)),
            ):
                @pl.when(missing)
                def _():
                    region = wide.at[it, rows, columns]
                    region[...] = jnp.zeros(region.shape, BF)

        barrier = pltpu.get_barrier_semaphore()

        def greet(device):
            pl.semaphore_signal(barrier, inc=1, device_id=device, device_id_type=MESH)

        for d in range(1, 16):
            greet((2 * ((gx // 2 + d // 4) % 4) + gx % 2, 4 * ((gz // 4 + d % 4) % 4) + gz % 4))
        for d in range(1, 8):
            greet((gx - gx % 2 + (gx % 2 + d // 4) % 2, gz - gz % 4 + (gz % 4 + d % 4) % 4))
        extra = 0
        for there, device in (
            (has_l, (gl, gz)), (has_r, (gr, gz)), (has_c, (gx, across)),
            (has_c & has_l, (gl, across)), (has_c & has_r, (gr, across)),
        ):
            pl.when(there)(lambda device=device: greet(device))
            extra = extra + there.astype(jnp.int32)
        pl.semaphore_wait(barrier, 22 + extra)

        def halo(it):
            w = wide.at[it]
            sems = (halo_sems[0].at[it], halo_sems[1].at[it])
            own = w.at[OWN, OWN]
            near = [
                Copy(own, w.at[OWN, LOW], sems, 0, (gr, gz), has_r, has_l),
                Copy(own, w.at[OWN, HIGH], sems, 1, (gl, gz), has_l, has_r),
            ]
            far = [
                Copy(own, w.at[at_mate, OWN], sems, 2, mate, True, True),
                Copy(own, w.at[at_cross, LOW], sems, 3, (gr, across), has_c & has_r, has_c & has_l),
                Copy(own, w.at[at_cross, HIGH], sems, 4, (gl, across), has_c & has_l, has_c & has_r),
                Copy(own, w.at[at_cross, OWN], sems, 5, (gx, across), has_c, has_c),
            ]
            relay = [
                Copy(w.at[OWN, LOW], w.at[at_mate, LOW], sems, 6, mate, has_l, has_l),
                Copy(w.at[OWN, HIGH], w.at[at_mate, HIGH], sems, 7, mate, has_r, has_r),
            ]
            for copy, rows, columns in (
                (far[0], mate_rows, OWN), (far[1], cross_rows, LOW), (far[2], cross_rows, HIGH),
                (far[3], cross_rows, OWN), (relay[0], mate_rows, LOW), (relay[1], mate_rows, HIGH),
            ):
                copy.lands_in(w.at[rows, columns])
            return near, far, relay

        def sums(it):
            sems = (sum_sems[0].at[it], sum_sems[1].at[it])
            p = part.at[it]
            to_mate = Copy(total.at[mate_rows], part_mate.at[it], sems, 0, mate, True, True)
            to_cross = [
                Copy(to_far.at[:, LOW], p.at[2], sems, 1, (gl, across), has_c & has_l, has_c & has_r),
                Copy(to_far.at[:, HIGH], p.at[1], sems, 2, (gr, across), has_c & has_r, has_c & has_l),
                Copy(to_far.at[:, OWN], p.at[0], sems, 3, (gx, across), has_c, has_c),
            ]
            aside = []
            for half in range(2):
                there = slice(8 * half, 8 * half + 8)
                aside.append([
                    Copy(to_side.at[0, there], p.at[4, there], sems, 4 + 2 * half, (gl, gz), has_l, has_r),
                    Copy(to_side.at[1, there], p.at[3, there], sems, 5 + 2 * half, (gr, gz), has_r, has_l),
                ])
            return to_mate, to_cross, aside

        def first_stage(d):
            y, x = (gx // 2 + d // 4) % 4, (gz // 4 + d % 4) % 4
            return pltpu.make_async_remote_copy(
                src_ref=outgoing.at[y, :, x], dst_ref=passing.at[gx // 2, gz // 4],
                send_sem=first_sems[0].at[d], recv_sem=first_sems[1].at[d],
                device_id=(2 * y + gx % 2, 4 * x + gz % 4), device_id_type=MESH,
            )

        def second_stage(d):
            high, low = (gx % 2 + d // 4) % 2, (gz % 4 + d % 4) % 4
            return pltpu.make_async_remote_copy(
                src_ref=passing.at[:, :, high, low], dst_ref=arrived.at[:, gx % 2, :, gz % 4],
                send_sem=second_sems[0].at[d], recv_sem=second_sems[1].at[d],
                device_id=(gx - gx % 2 + high, gz - gz % 4 + low), device_id_type=MESH,
            )

        stay_first = pltpu.make_async_copy(
            outgoing.at[gx // 2, :, gz // 4], passing.at[gx // 2, gz // 4], local_sems.at[0]
        )
        stay_second = pltpu.make_async_copy(
            passing.at[:, :, gx % 2, gz % 4], arrived.at[:, gx % 2, :, gz % 4], local_sems.at[1]
        )
        slot_copy = pltpu.make_async_copy(slots, slot_ref, local_sems.at[2])

        for it in range(ITERS):
            w = wide.at[it]
            near, far, relay = halo(it)
            if it == 0:
                stay_first.start()
                for d in range(1, 16):
                    first_stage(d).start()
            for copy in near + far:
                copy.start()
            if it == 0:
                slots_of(labels_ref[...], slots)
                slot_copy.start()
                load_taps(bank_ref, axial_in, kx, ky, ax)
                reverse_taps(ky, ky_back)
                build_bands(ky_back, kx, ax, fwd_y, fwd_x, False)
            for copy in near:
                copy.wait_recv()
            for copy in relay:
                copy.start()
            lateral_forward(index_of, fwd_x, fwd_y, w, mid, grown, BLK, BLK, UNROLL)
            if it == 0:
                stay_first.wait()
                for d in range(1, 16):
                    first_stage(d).wait_recv()
                for d in range(1, 8):
                    second_stage(d).start()
                stay_second.start()
            for copy in [far[0]] + relay:
                copy.wait_recv()
            lateral_forward(index_of, fwd_x, fwd_y, w, mid, grown, 2 * BLK * (1 - core), BLK, UNROLL)
            for copy in far[1:]:
                copy.wait_recv()
            lateral_forward(index_of, fwd_x, fwd_y, w, mid, grown, 2 * BLK * core, BLK, UNROLL)
            if it == 0:
                ones_response(index_of, ax, kx, ky, gx * BLK, gz * BLK, edge_x, edge_y, base, nx * BLK, nz * BLK)
                build_bands(ky, kx, ax, bwd_y, bwd_x, True)
                for d in range(1, 16):
                    first_stage(d).wait_send()
                for d in range(1, 8):
                    second_stage(d).wait()
                stay_second.wait()
                slot_copy.wait()
            for copy in near + far + relay:
                copy.wait_send()

            axial_and_ratio(axial_ref, slot_ref, grown, lambda s: arrived[s // 32, (s // 16) % 2, (s // 4) % 4, s % 4], spread)
            to_mate, to_cross, aside = sums(it)
            lateral_backward(index_of, bwd_x, bwd_y, spread, mid, to_far, 2 * BLK * core, 2 * BLK * core, BLK, UNROLL)
            for copy in to_cross:
                copy.start()
            lateral_backward(index_of, bwd_x, bwd_y, spread, mid, total, 0, 2 * BLK * (1 - core), BLK, UNROLL)
            to_mate.start()
            for half in range(2):
                first = BLK + 8 * half
                lateral_backward(index_of, bwd_x, bwd_y, spread, mid, total, 0, first, 8, UNROLL)
                if half == 0:
                    to_mate.wait_recv()
                there = slice(8 * half, 8 * half + 8)
                both = total[first : first + 8] + part_mate[it, there]
                total[first : first + 8, OWN] = both[:, OWN]
                to_side[0, there] = both[:, LOW].astype(BF)
                to_side[1, there] = both[:, HIGH].astype(BF)
                for copy in aside[half]:
                    copy.start()
            inner = base[...] + total[OWN, OWN]
            for copy in to_cross:
                copy.wait_recv()
            for there, which in ((has_c, 0), (has_c & has_l, 1), (has_c & has_r, 2)):
                inner = inner + jnp.where(there, part[it, which].astype(F32), 0.0)
            before = estimate_ref if it == 0 else out_ref
            scaled = before[...] * (1.0 / VIEWS)
            for pair in aside:
                for copy in pair:
                    copy.wait_recv()
            for there, which in ((has_l, 3), (has_r, 4)):
                inner = inner + jnp.where(there, part[it, which].astype(F32), 0.0)
            after = scaled * inner
            out_ref[...] = after
            if it + 1 < ITERS:
                wide[it + 1, OWN, OWN] = after.astype(BF)
            for copy in [to_mate] + to_cross + aside[0] + aside[1]:
                copy.wait_send()

    smem = pl.BlockSpec(memory_space=pltpu.SMEM)
    vmem = pl.BlockSpec(memory_space=pltpu.VMEM)
    dma = pltpu.SemaphoreType.DMA
    block = (BLK, BLK, LINE)
    return pl.pallas_call(
        body,
        name="joint",
        out_shape=jax.ShapeDtypeStruct(block, F32),
        in_specs=[smem] * 2 + [vmem] * 4 + [pl.BlockSpec(memory_space=pl.ANY)],
        out_specs=vmem,
        scratch_shapes=[
            pltpu.VMEM((KERNELS, 8, LINE), F32),
            pltpu.VMEM((KERNELS, 8, LINE), F32),
            pltpu.VMEM((KERNELS, 8, LINE), F32),
            pltpu.VMEM((8, LINE), F32),
            pltpu.VMEM((KERNELS, VIEWS, LINE, LINE), BF),
            pltpu.VMEM((KERNELS, VIEWS, LINE, LINE), BF),
            pltpu.VMEM((KERNELS, VIEWS * BLK, LINE), BF),
            pltpu.VMEM((KERNELS, LINE, VIEWS * BLK), BF),
            pltpu.VMEM((KERNELS, 8, LINE), F32),
            pltpu.VMEM((KERNELS, 8, LINE), F32),
            pltpu.VMEM(block, F32),
            pltpu.VMEM((NEAR, VIEWS * BLK, LINE), BF),
            pltpu.VMEM((VIEWS, NEAR, BLK, LINE), F32),
            pltpu.VMEM((VIEWS, NEAR, BLK, LINE), BF),
            pltpu.VMEM((NEAR, NEAR, LINE), F32),
            pltpu.VMEM((BLK, NEAR, LINE), BF),
            pltpu.VMEM((2,) + block, BF),
            pltpu.VMEM((ITERS, NEAR, NEAR, LINE), BF),
            pltpu.VMEM((ITERS, BLK, NEAR, LINE), F32),
            pltpu.VMEM((ITERS, 5) + block, BF),
            pltpu.VMEM((4, 4, 2, 4, BLK, LINE), BF),
            pltpu.VMEM((4, 2, 4, 4, BLK, LINE), BF),
            pltpu.VMEM((1, LINE), jnp.int32),
            pltpu.SMEM((1, LINE), jnp.int32),
            (dma((ITERS, 8)), dma((ITERS, 8))),
            (dma((ITERS, 8)), dma((ITERS, 8))),
            (dma((16,)), dma((16,))),
            (dma((8,)), dma((8,))),
            dma((3,)),
        ],
        compiler_params=pltpu.CompilerParams(
            vmem_limit_bytes=48 << 20, collective_id=0, has_side_effects=True
        ),
    )


def shards(estimate, view_tiles, incoming_label, lateral_bank, axial_kernel, kernel_index):
    nx, nz = lax.axis_size("gx"), lax.axis_size("gz")
    outgoing = view_tiles[0].reshape(4, 2, 4, 4, BLK, LINE)
    return joint_kernel(nx, nz)(
        kernel_index, axial_kernel, axial_kernel, lateral_bank, incoming_label, estimate, outgoing
    )


def solution(mesh):
    return jax.shard_map(
        shards,
        mesh=mesh,
        in_specs=(P("gz", "gx", None), P(("gx", "gz"), None, None), P(("gx", "gz"), None), P(), P(), P()),
        out_specs=P("gz", "gx", None),
        check_vma=False,
    )
```

```python
import jax
import jax.numpy as jnp
from jax import lax
from jax.experimental import pallas as pl
from jax.experimental.pallas import tpu as pltpu
from jax.sharding import PartitionSpec as P

TAPS = 33
ITERS = 2
HALO = 16
VIEWS = 6
KERNELS = 16
BLK = 16
NEAR = 48
UNROLL = 8
LINE = 128
F32 = jnp.float32
BF = jnp.bfloat16
HI = lax.Precision.HIGHEST


def iota(shape, dim):
    return lax.broadcasted_iota(jnp.int32, shape, dim)


def load_taps(bank_ref, axial_in, kx, ky, ax):
    ax[...] = jnp.zeros_like(ax)
    ax[:VIEWS, :TAPS] = axial_in[...]
    for dim, taps in ((0, kx), (1, ky)):
        taps[...] = jnp.zeros_like(taps)
        for v in range(VIEWS):
            taps[:, v, :TAPS] = bank_ref[v, :, dim, :]
        raw = taps[...]
        total = jnp.sum(raw, axis=-1, keepdims=True)
        taps[...] = raw / jnp.where(total > 0.0, total, 1.0)


def line_scale(ax):
    axial = jnp.sum(ax[...], axis=1, keepdims=True)
    return jnp.broadcast_to(1.0 / jnp.where(axial > 0.0, axial, 1.0), (8, LINE))


def reverse_taps(ky, ky_back):
    flip = jnp.where(iota((LINE, LINE), 0) + iota((LINE, LINE), 1) == TAPS - 1, 1.0, 0.0)
    taps = ky[...].reshape(KERNELS * 8, LINE)
    ky_back[...] = jnp.dot(taps, flip, precision=HI, preferred_element_type=F32).reshape(KERNELS, 8, LINE)


def build_bands(ky, kx, ax, bands_y, bands_x, spread_out):
    inside = jnp.abs(iota((LINE, LINE), 0) - iota((LINE, LINE), 1)) <= HALO
    scale = line_scale(ax)

    @pl.loop(0, KERNELS)
    def _(k):
        taps_x = kx[k]
        taps_y = ky[k] * scale
        rows = []
        for v in range(VIEWS):
            band = jnp.broadcast_to(taps_y[v : v + 1], (LINE, LINE))
            band = pltpu.roll(band, LINE - HALO, 1, stride=1, stride_axis=0)
            bands_y[k, v] = jnp.where(inside, band, 0.0).astype(BF)
            rows.append(pltpu.roll(jnp.broadcast_to(taps_x[v : v + 1], (BLK, LINE)), 0, 1, stride=1, stride_axis=0))
        across = jnp.concatenate(rows, 0)
        bands_x[k] = (across.T if spread_out else across).astype(BF)


def ones_response(index_of, ax, kx_ref, ky_ref, col0, depth0, edge_x, edge_y, base_ref, cols, depths):
    tap = iota((LINE, LINE), 0)
    pos = iota((LINE, LINE), 1)
    at_x = col0 + pos - tap + HALO
    at_y = pos - tap + HALO
    ok_x = jnp.where((at_x >= 0) & (at_x < cols), 1.0, 0.0)
    ok_y = jnp.where((at_y >= 0) & (at_y < LINE), 1.0, 0.0)
    kx = kx_ref[...].reshape(KERNELS * 8, LINE)
    ky = ky_ref[...].reshape(KERNELS * 8, LINE)
    edge_x[...] = jnp.dot(kx, ok_x, precision=HI, preferred_element_type=F32).reshape(KERNELS, 8, LINE)
    edge_y[...] = jnp.dot(ky, ok_y, precision=HI, preferred_element_type=F32).reshape(KERNELS, 8, LINE)
    axial = ax[...]
    total = jnp.sum(axial, axis=1, keepdims=True)
    axial = axial / jnp.where(total > 0.0, total, 1.0)
    lane = iota((8, LINE), 1)
    for z in range(BLK):
        k = index_of(HALO + z)
        at_z = depth0 + z - lane + HALO
        part = jnp.sum(jnp.where((at_z >= 0) & (at_z < depths), axial, 0.0), axis=1, keepdims=True)
        left = edge_x[k][:, :BLK] * part
        base_ref[z] = lax.dot_general(
            left, edge_y[k], (((0,), (0,)), ((), ())), precision=HI, preferred_element_type=F32
        )


def slots_of(labels, slots):
    column = jnp.broadcast_to(labels, (LINE, LINE)).T
    hit = column == iota((LINE, LINE), 1)
    slots[...] = jnp.max(jnp.where(hit, iota((LINE, LINE), 0), -1), axis=0, keepdims=True)


def lateral_forward(index_of, fwd_x, fwd_y, wide, mid, grown, first, count, unroll):
    @pl.loop(0, count // unroll)
    def _(s):
        start = first + s * unroll
        kernels = [index_of(start + u) for u in range(unroll)]
        for u, k in enumerate(kernels):
            mid[start + u] = jnp.dot(
                fwd_x[k][:, :NEAR], wide[start + u].reshape(NEAR, LINE), preferred_element_type=F32
            ).astype(BF)
        for u, k in enumerate(kernels):
            for v in range(VIEWS):
                grown[v, start + u] = jnp.dot(
                    mid[start + u, v * BLK : (v + 1) * BLK, :], fwd_y[k, v], preferred_element_type=F32
                )


def lateral_backward(index_of, bwd_x, bwd_y, spread, mid, total, first, count, unroll):
    @pl.loop(0, count // unroll)
    def _(s):
        start = first + s * unroll
        kernels = [index_of(start + u) for u in range(unroll)]
        for u, k in enumerate(kernels):
            for v in range(VIEWS):
                mid[start + u, v * BLK : (v + 1) * BLK, :] = jnp.dot(
                    spread[v, start + u], bwd_y[k, v], preferred_element_type=F32
                ).astype(BF)
        for u, k in enumerate(kernels):
            total[start + u] = jnp.dot(
                bwd_x[k][:NEAR], mid[start + u], preferred_element_type=F32
            ).reshape(3, BLK, LINE)


def taps_over(zi):
    return range(max(0, zi - 2 * HALO), min(BLK - 1, zi) + 1)


def axial_and_ratio(axial_ref, slot_ref, grown, tile_of, spread):
    @pl.loop(0, VIEWS)
    def _(v):
        weights = [axial_ref[v, t] for t in range(TAPS)]
        seen = jnp.full((8, LINE), slot_ref[0, v * BLK], jnp.int32) >= 0
        for half in range(2):
            rows = slice(half * 8, half * 8 + 8)
            total = [None] * BLK
            for zi in range(NEAR):
                g = grown[v, zi, rows, :]
                for zo in taps_over(zi):
                    term = weights[zi - zo] * g
                    total[zo] = term if total[zo] is None else total[zo] + term
            excess = []
            for zo in range(BLK):
                tile = tile_of(jnp.maximum(slot_ref[0, v * BLK + zo], 0))[rows].astype(F32)
                ratio = (tile / total[zo]).astype(BF).astype(F32)
                excess.append(jnp.where(seen, ratio - 1.0, 0.0))
            for zi in range(NEAR):
                acc = None
                for zo in taps_over(zi):
                    term = weights[zi - zo] * excess[zo]
                    acc = term if acc is None else acc + term
                spread[v, zi, rows, :] = acc.astype(BF)


LOW, OWN, HIGH = slice(0, BLK), slice(BLK, 2 * BLK), slice(2 * BLK, NEAR)
MESH = pl.DeviceIdType.MESH


def worker_of(bx, bz):
    return 2 * (bx // 2) + (bz % 4) // 2, 4 * (bz // 4) + 2 * (bz % 2) + bx % 2


class Copy:
    def __init__(self, src, dst, sems, slot, device, sends, receives):
        self.src, self.sems, self.slot = src, sems, slot
        self.sends, self.receives = sends, receives
        self.out = self.back = self.make(dst, device)
        self.device = device

    def make(self, dst, device):
        return pltpu.make_async_remote_copy(
            src_ref=self.src, dst_ref=dst, send_sem=self.sems[0].at[self.slot], recv_sem=self.sems[1].at[self.slot],
            device_id=device, device_id_type=MESH,
        )

    def lands_in(self, region):
        self.back = self.make(region, self.device)
        return self

    def start(self):
        pl.when(self.sends)(self.out.start)

    def wait_recv(self):
        pl.when(self.receives)(self.back.wait_recv)

    def wait_send(self):
        pl.when(self.sends)(self.out.wait_send)


def joint_kernel(nx, nz):
    def body(index_ref, axial_ref, axial_in, bank_ref, labels_ref, estimate_ref, outgoing,
             out_ref, kx, ky, ky_back, ax, fwd_y, bwd_y, fwd_x, bwd_x, edge_x, edge_y, base, mid, grown, spread, total,
             to_far, to_corner, to_side, staged, wide, part_mate, part, product, back,
             passing, arrived, labels, slots, slot_ref,
             move_sems, halo_sems, sum_sems, first_sems, second_sems, local_sems):
        gx, gz = lax.axis_index("gx"), lax.axis_index("gz")
        core, high_z = gz % 2, gx % 2
        bx, bz = gx - high_z + core, gz - gz % 4 + 2 * high_z + (gz % 4) // 2
        has_d, has_u = bz > 0, bz < nz - 1
        bc = bx - 1 + 2 * core
        has_c = (bc >= 0) & (bc < nx)
        bc, bd, bu = (bc + nx) % nx, (bz + nz - 1) % nz, (bz + 1) % nz
        mate = (gx, gz + 1 - 2 * core)
        across, down, up = worker_of(bc, bz), worker_of(bx, bd), worker_of(bx, bu)
        across_down, across_up = worker_of(bc, bd), worker_of(bc, bu)
        worker, owner = worker_of(gx, gz), (bx, bz)
        moved = (bx != gx) | (bz != gz)
        far_side, mate_side = 2 * core, 2 - 2 * core

        def index_of(z):
            return index_ref[jnp.clip(bz * BLK - HALO + z, 0, nz * BLK - 1)]

        staged[...] = estimate_ref[...].astype(BF)
        for it in range(ITERS):
            @pl.when(jnp.logical_not(has_c))
            def _():
                wide[it, :, far_side] = jnp.zeros((NEAR, BLK, LINE), BF)

            for there, rows in ((has_d, LOW), (has_u, HIGH)):
                @pl.when(jnp.logical_not(there))
                def _():
                    wide[it, rows] = jnp.zeros((BLK, 3, BLK, LINE), BF)

        barrier = pltpu.get_barrier_semaphore()

        def greet(device):
            pl.semaphore_signal(barrier, inc=1, device_id=device, device_id_type=MESH)

        for d in range(1, 16):
            greet((2 * ((gx // 2 + d // 4) % 4) + gx % 2, 4 * ((gz // 4 + d % 4) % 4) + gz % 4))
        for d in range(1, 8):
            greet((gx - gx % 2 + (gx % 2 + d // 4) % 2, gz - gz % 4 + (gz % 4 + d % 4) % 4))
        extra = 0
        for there, device in (
            (has_c, across), (has_d, down), (has_u, up), (has_c & has_d, across_down), (has_c & has_u, across_up),
        ):
            pl.when(there)(lambda device=device: greet(device))
            extra = extra + there.astype(jnp.int32)
        pl.semaphore_wait(barrier, 22 + extra)

        moves = [
            Copy(staged, wide.at[0, OWN, 1], move_sems, 0, worker, moved, moved),
            Copy(labels_ref, labels, move_sems, 1, worker, moved, moved),
        ]
        bring = Copy(product, back, move_sems, 2, owner, moved, moved)

        def halo(it):
            w = wide.at[it]
            sems = (halo_sems[0].at[it], halo_sems[1].at[it])
            own = w.at[OWN, 1]
            near = [
                Copy(own, w.at[OWN, mate_side], sems, 1, across, has_c, has_c).lands_in(w.at[OWN, far_side]),
                Copy(own, w.at[OWN, far_side], sems, 0, mate, True, True).lands_in(w.at[OWN, mate_side]),
            ]
            straight = [
                Copy(own, w.at[LOW, 1], sems, 2, up, has_u, has_d),
                Copy(own, w.at[HIGH, 1], sems, 3, down, has_d, has_u),
            ]
            corner = [
                Copy(own, w.at[LOW, mate_side], sems, 4, across_up, has_c & has_u, has_c & has_d).lands_in(
                    w.at[LOW, far_side]),
                Copy(own, w.at[HIGH, mate_side], sems, 5, across_down, has_c & has_d, has_c & has_u).lands_in(
                    w.at[HIGH, far_side]),
            ]
            relay = [
                Copy(w.at[LOW, 1], w.at[LOW, far_side], sems, 6, mate, has_d, has_d).lands_in(w.at[LOW, mate_side]),
                Copy(w.at[HIGH, 1], w.at[HIGH, far_side], sems, 7, mate, has_u, has_u).lands_in(w.at[HIGH, mate_side]),
            ]
            return near, straight, corner, relay

        def sums(it):
            sems = (sum_sems[0].at[it], sum_sems[1].at[it])
            p = part.at[it]
            halves = [slice(BLK, BLK + 8), slice(BLK + 8, 2 * BLK)]
            to_mate = [
                Copy(total.at[rows, mate_side], part_mate.at[it, rows], sems, i, mate, there, there)
                for i, (rows, there) in enumerate(((LOW, has_d), (HIGH, has_u), (halves[0], True), (halves[1], True)))
            ]
            straight = [
                Copy(to_far.at[0], p.at[0], sems, 4, down, has_d, has_u),
                Copy(to_far.at[1], p.at[1], sems, 5, up, has_u, has_d),
            ]
            corner = [
                Copy(to_corner.at[0], p.at[2], sems, 6, across_down, has_c & has_d, has_c & has_u),
                Copy(to_corner.at[1], p.at[3], sems, 7, across_up, has_c & has_u, has_c & has_d),
            ]
            aside = [
                Copy(to_side.at[rows], p.at[4, rows], sems, 8 + i, across, has_c, has_c)
                for i, rows in enumerate((slice(0, 8), slice(8, 16)))
            ]
            return to_mate, straight, corner, aside

        def first_stage(d):
            y, x = (gx // 2 + d // 4) % 4, (gz // 4 + d % 4) % 4
            return pltpu.make_async_remote_copy(
                src_ref=outgoing.at[y, :, x], dst_ref=passing.at[gx // 2, gz // 4],
                send_sem=first_sems[0].at[d], recv_sem=first_sems[1].at[d],
                device_id=(2 * y + gx % 2, 4 * x + gz % 4), device_id_type=MESH,
            )

        def second_stage(d):
            high, low = (gx % 2 + d // 4) % 2, (gz % 4 + d % 4) % 4
            return pltpu.make_async_remote_copy(
                src_ref=passing.at[:, :, low % 2, 2 * high + low // 2], dst_ref=arrived.at[:, gx % 2, :, gz % 4],
                send_sem=second_sems[0].at[d], recv_sem=second_sems[1].at[d],
                device_id=(gx - gx % 2 + high, gz - gz % 4 + low), device_id_type=MESH,
            )

        stay_first = pltpu.make_async_copy(
            outgoing.at[gx // 2, :, gz // 4], passing.at[gx // 2, gz // 4], local_sems.at[0]
        )
        stay_second = pltpu.make_async_copy(
            passing.at[:, :, core, 2 * high_z + (gz % 4) // 2], arrived.at[:, gx % 2, :, gz % 4], local_sems.at[1]
        )
        slot_copy = pltpu.make_async_copy(slots, slot_ref, local_sems.at[2])

        for copy in moves:
            copy.start()

        @pl.when(jnp.logical_not(moved))
        def _():
            wide[0, OWN, 1] = staged[...]
            labels[...] = labels_ref[...]

        stay_first.start()
        for d in range(1, 16):
            first_stage(d).start()
        load_taps(bank_ref, axial_in, kx, ky, ax)
        reverse_taps(ky, ky_back)
        for copy in moves:
            copy.wait_recv()

        for it in range(ITERS):
            w = wide.at[it]
            near, straight, corner, relay = halo(it)
            for copy in near + straight + corner:
                copy.start()
            if it == 0:
                build_bands(ky_back, kx, ax, fwd_y, fwd_x, False)
                slots_of(labels[...], slots)
                slot_copy.start()
            for copy in near:
                copy.wait_recv()
            lateral_forward(index_of, fwd_x, fwd_y, w, mid, grown, BLK, BLK, UNROLL)
            for copy in straight:
                copy.wait_recv()
            for copy in relay:
                copy.start()
            if it == 0:
                stay_first.wait()
                for d in range(1, 16):
                    first_stage(d).wait_recv()
                for d in range(1, 8):
                    second_stage(d).start()
                stay_second.start()
            for copy in corner + relay:
                copy.wait_recv()
            lateral_forward(index_of, fwd_x, fwd_y, w, mid, grown, 0, BLK, UNROLL)
            lateral_forward(index_of, fwd_x, fwd_y, w, mid, grown, 2 * BLK, BLK, UNROLL)
            if it == 0:
                ones_response(index_of, ax, kx, ky, bx * BLK, bz * BLK, edge_x, edge_y, base, nx * BLK, nz * BLK)
                build_bands(ky, kx, ax, bwd_y, bwd_x, True)
                for d in range(1, 16):
                    first_stage(d).wait_send()
                for d in range(1, 8):
                    second_stage(d).wait()
                stay_second.wait()
                slot_copy.wait()
                for copy in moves:
                    copy.wait_send()
            for copy in near + straight + corner + relay:
                copy.wait_send()

            axial_and_ratio(axial_ref, slot_ref, grown, lambda s: arrived[s // 32, (s // 16) % 2, (s // 4) % 4, s % 4],
                            spread)
            to_mate, straight, corner, aside = sums(it)
            for i, rows in enumerate((LOW, HIGH)):
                lateral_backward(index_of, bwd_x, bwd_y, spread, mid, total, rows.start, BLK, UNROLL)
                to_mate[i].start()
                to_corner[i] = total[rows, far_side].astype(BF)
                corner[i].start()
            for i, rows in enumerate((LOW, HIGH)):
                to_mate[i].wait_recv()
                to_far[i] = (total[rows, 1] + jnp.where((has_d, has_u)[i], part_mate[it, rows], 0.0)).astype(BF)
                straight[i].start()
            for half in range(2):
                first = BLK + 8 * half
                lateral_backward(index_of, bwd_x, bwd_y, spread, mid, total, first, 8, UNROLL)
                to_side[8 * half : 8 * half + 8] = total[first : first + 8, far_side].astype(BF)
                aside[half].start()
                to_mate[2 + half].start()
            inner = base[...] + total[OWN, 1]
            gain = (1.0 / VIEWS) if it == 0 else product[...] * (1.0 / VIEWS)
            for copy in to_mate[2:]:
                copy.wait_recv()
            inner = inner + part_mate[it, OWN]
            for copy in straight + corner:
                copy.wait_recv()
            for there, which in ((has_u, 0), (has_d, 1), (has_c & has_u, 2), (has_c & has_d, 3)):
                inner = inner + jnp.where(there, part[it, which].astype(F32), 0.0)
            for copy in aside:
                copy.wait_recv()
            inner = inner + jnp.where(has_c, part[it, 4].astype(F32), 0.0)
            product[...] = inner * gain
            if it + 1 < ITERS:
                wide[it + 1, OWN, 1] = (wide[it, OWN, 1].astype(F32) * product[...]).astype(BF)
            else:
                bring.start()
            for copy in to_mate + straight + corner + aside:
                copy.wait_send()

        @pl.when(jnp.logical_not(moved))
        def _():
            back[...] = product[...]

        bring.wait_recv()
        out_ref[...] = estimate_ref[...] * back[...]
        bring.wait_send()

    smem = pl.BlockSpec(memory_space=pltpu.SMEM)
    vmem = pl.BlockSpec(memory_space=pltpu.VMEM)
    dma = pltpu.SemaphoreType.DMA
    block = (BLK, BLK, LINE)
    return pl.pallas_call(
        body,
        name="joint",
        out_shape=jax.ShapeDtypeStruct(block, F32),
        in_specs=[smem] * 2 + [vmem] * 4 + [pl.BlockSpec(memory_space=pl.ANY)],
        out_specs=vmem,
        scratch_shapes=[
            pltpu.VMEM((KERNELS, 8, LINE), F32),
            pltpu.VMEM((KERNELS, 8, LINE), F32),
            pltpu.VMEM((KERNELS, 8, LINE), F32),
            pltpu.VMEM((8, LINE), F32),
            pltpu.VMEM((KERNELS, VIEWS, LINE, LINE), BF),
            pltpu.VMEM((KERNELS, VIEWS, LINE, LINE), BF),
            pltpu.VMEM((KERNELS, VIEWS * BLK, LINE), BF),
            pltpu.VMEM((KERNELS, LINE, VIEWS * BLK), BF),
            pltpu.VMEM((KERNELS, 8, LINE), F32),
            pltpu.VMEM((KERNELS, 8, LINE), F32),
            pltpu.VMEM(block, F32),
            pltpu.VMEM((NEAR, VIEWS * BLK, LINE), BF),
            pltpu.VMEM((VIEWS, NEAR, BLK, LINE), F32),
            pltpu.VMEM((VIEWS, NEAR, BLK, LINE), BF),
            pltpu.VMEM((NEAR, 3, BLK, LINE), F32),
            pltpu.VMEM((2,) + block, BF),
            pltpu.VMEM((2,) + block, BF),
            pltpu.VMEM(block, BF),
            pltpu.VMEM(block, BF),
            pltpu.VMEM((ITERS, NEAR, 3, BLK, LINE), BF),
            pltpu.VMEM((ITERS, NEAR, BLK, LINE), F32),
            pltpu.VMEM((ITERS, 5) + block, BF),
            pltpu.VMEM(block, F32),
            pltpu.VMEM(block, F32),
            pltpu.VMEM((4, 4, 2, 4, BLK, LINE), BF),
            pltpu.VMEM((4, 2, 4, 4, BLK, LINE), BF),
            pltpu.VMEM((1, LINE), jnp.int32),
            pltpu.VMEM((1, LINE), jnp.int32),
            pltpu.SMEM((1, LINE), jnp.int32),
            (dma((3,)), dma((3,))),
            (dma((ITERS, 8)), dma((ITERS, 8))),
            (dma((ITERS, 10)), dma((ITERS, 10))),
            (dma((16,)), dma((16,))),
            (dma((8,)), dma((8,))),
            dma((3,)),
        ],
        compiler_params=pltpu.CompilerParams(
            vmem_limit_bytes=48 << 20, collective_id=0, has_side_effects=True
        ),
    )


def shards(estimate, view_tiles, incoming_label, lateral_bank, axial_kernel, kernel_index):
    nx, nz = lax.axis_size("gx"), lax.axis_size("gz")
    outgoing = view_tiles[0].reshape(4, 2, 4, 4, BLK, LINE)
    return joint_kernel(nx, nz)(
        kernel_index, axial_kernel, axial_kernel, lateral_bank, incoming_label, estimate, outgoing
    )


def solution(mesh):
    return jax.shard_map(
        shards,
        mesh=mesh,
        in_specs=(P("gz", "gx", None), P(("gx", "gz"), None, None), P(("gx", "gz"), None), P(), P(), P()),
        out_specs=P("gz", "gx", None),
        check_vma=False,
    )
```

```python
import jax
import jax.numpy as jnp
from jax import lax
from jax.experimental import pallas as pl
from jax.experimental.pallas import tpu as pltpu
from jax.sharding import PartitionSpec as P

TAPS = 33
ITERS = 2
HALO = 16
VIEWS = 6
KERNELS = 16
BLK = 16
NEAR = 48
UNROLL = 8
LINE = 128
F32 = jnp.float32
BF = jnp.bfloat16
HI = lax.Precision.HIGHEST


def iota(shape, dim):
    return lax.broadcasted_iota(jnp.int32, shape, dim)


def load_taps(bank_ref, axial_in, kx, ky, ax):
    ax[...] = jnp.zeros_like(ax)
    ax[:VIEWS, :TAPS] = axial_in[...]
    for dim, taps in ((0, kx), (1, ky)):
        taps[...] = jnp.zeros_like(taps)
        for v in range(VIEWS):
            taps[:, v, :TAPS] = bank_ref[v, :, dim, :]
        raw = taps[...]
        total = jnp.sum(raw, axis=-1, keepdims=True)
        taps[...] = raw / jnp.where(total > 0.0, total, 1.0)


def line_scale(ax):
    axial = jnp.sum(ax[...], axis=1, keepdims=True)
    return jnp.broadcast_to(1.0 / jnp.where(axial > 0.0, axial, 1.0), (8, LINE))


def reverse_taps(ky, ky_back):
    flip = jnp.where(iota((LINE, LINE), 0) + iota((LINE, LINE), 1) == TAPS - 1, 1.0, 0.0)
    taps = ky[...].reshape(KERNELS * 8, LINE)
    ky_back[...] = jnp.dot(taps, flip, precision=HI, preferred_element_type=F32).reshape(KERNELS, 8, LINE)


def build_bands(ky, kx, ax, bands_y, bands_x, spread_out):
    inside = jnp.abs(iota((LINE, LINE), 0) - iota((LINE, LINE), 1)) <= HALO
    scale = line_scale(ax)

    @pl.loop(0, KERNELS)
    def _(k):
        taps_x = kx[k]
        taps_y = ky[k] * scale
        rows = []
        for v in range(VIEWS):
            band = jnp.broadcast_to(taps_y[v : v + 1], (LINE, LINE))
            band = pltpu.roll(band, LINE - HALO, 1, stride=1, stride_axis=0)
            bands_y[k, v] = jnp.where(inside, band, 0.0).astype(BF)
            rows.append(pltpu.roll(jnp.broadcast_to(taps_x[v : v + 1], (BLK, LINE)), 0, 1, stride=1, stride_axis=0))
        across = jnp.concatenate(rows, 0)
        bands_x[k] = (across.T if spread_out else across).astype(BF)


def ones_response(index_of, ax, kx_ref, ky_ref, col0, depth0, edge_x, edge_y, base_ref, cols, depths):
    tap = iota((LINE, LINE), 0)
    pos = iota((LINE, LINE), 1)
    at_x = col0 + pos - tap + HALO
    at_y = pos - tap + HALO
    ok_x = jnp.where((at_x >= 0) & (at_x < cols), 1.0, 0.0)
    ok_y = jnp.where((at_y >= 0) & (at_y < LINE), 1.0, 0.0)
    kx = kx_ref[...].reshape(KERNELS * 8, LINE)
    ky = ky_ref[...].reshape(KERNELS * 8, LINE)
    edge_x[...] = jnp.dot(kx, ok_x, precision=HI, preferred_element_type=F32).reshape(KERNELS, 8, LINE)
    edge_y[...] = jnp.dot(ky, ok_y, precision=HI, preferred_element_type=F32).reshape(KERNELS, 8, LINE)
    axial = ax[...]
    total = jnp.sum(axial, axis=1, keepdims=True)
    axial = axial / jnp.where(total > 0.0, total, 1.0)
    lane = iota((8, LINE), 1)
    for z in range(BLK):
        k = index_of(HALO + z)
        at_z = depth0 + z - lane + HALO
        part = jnp.sum(jnp.where((at_z >= 0) & (at_z < depths), axial, 0.0), axis=1, keepdims=True)
        left = edge_x[k][:, :BLK] * part
        base_ref[z] = lax.dot_general(
            left, edge_y[k], (((0,), (0,)), ((), ())), precision=HI, preferred_element_type=F32
        )


def slots_of(labels, slots):
    column = jnp.broadcast_to(labels, (LINE, LINE)).T
    hit = column == iota((LINE, LINE), 1)
    slots[...] = jnp.max(jnp.where(hit, iota((LINE, LINE), 0), -1), axis=0, keepdims=True)


def by_views(body):
    @pl.loop(0, VIEWS // 2)
    def _(s):
        for u in range(2):
            body(2 * s + u)


def columns_forward(index_of, fwd_x, wide, mid, first):
    @pl.loop(0, BLK // UNROLL)
    def _(s):
        for u in range(UNROLL):
            z = s * UNROLL + u
            mid[z] = jnp.dot(
                fwd_x[index_of(first + z)][:, :NEAR], wide[first + z].reshape(NEAR, LINE), preferred_element_type=F32
            ).astype(BF).reshape(VIEWS, BLK, LINE)


def line_forward(index_of, fwd_y, mid, grown, first, v):
    for z in range(BLK):
        grown[v, z] = jnp.dot(mid[z, v], fwd_y[index_of(first + z), v], preferred_element_type=F32)


def line_backward(index_of, bwd_y, spread, mid, first, v):
    for z in range(BLK):
        mid[z, v] = jnp.dot(spread[v, z], bwd_y[index_of(first + z), v], preferred_element_type=F32).astype(BF)


def columns_backward(index_of, bwd_x, mid, total, first, start, count):
    @pl.loop(0, count // UNROLL)
    def _(s):
        for u in range(UNROLL):
            z = start + s * UNROLL + u
            total[first + z] = jnp.dot(
                bwd_x[index_of(first + z)][:NEAR], mid[z].reshape(VIEWS * BLK, LINE), preferred_element_type=F32
            ).reshape(3, BLK, LINE)


HALVES = (slice(0, 8), slice(8, 16))


def reached(zi):
    return range(max(0, zi - 2 * HALO), min(BLK - 1, zi) + 1)


def axial_forward(axial_ref, grown, first, v, rows, total):
    for z in range(BLK):
        g = grown[v, z, rows, :]
        for zo in reached(first + z):
            term = axial_ref[v, first + z - zo] * g
            total[zo] = term if total[zo] is None else total[zo] + term
    return total


def axial_backward(axial_ref, excess, spread, first, v, rows):
    for z in range(BLK):
        acc = None
        for zo in reached(first + z):
            term = axial_ref[v, first + z - zo] * excess[zo]
            acc = term if acc is None else acc + term
        spread[v, z, rows, :] = acc.astype(BF)


def gather_axial(axial_ref, grown, first, v, blurred):
    for rows in HALVES:
        total = [None if first == BLK else blurred[v, zo, rows, :] for zo in range(BLK)]
        for zo, value in enumerate(axial_forward(axial_ref, grown, first, v, rows, total)):
            blurred[v, zo, rows, :] = value


def ratios(axial_ref, slot_ref, grown, blurred, tile_of, excess, spread, v):
    seen = jnp.full((8, LINE), slot_ref[0, v * BLK], jnp.int32) >= 0
    for rows in HALVES:
        total = axial_forward(axial_ref, grown, 2 * BLK, v, rows, [blurred[v, zo, rows, :] for zo in range(BLK)])
        over = []
        for zo in range(BLK):
            tile = tile_of(jnp.maximum(slot_ref[0, v * BLK + zo], 0))[rows].astype(F32)
            ratio = (tile / total[zo]).astype(BF).astype(F32)
            over.append(jnp.where(seen, ratio - 1.0, 0.0))
            excess[v, zo, rows, :] = over[-1]
        axial_backward(axial_ref, over, spread, 0, v, rows)


def spread_axial(axial_ref, excess, spread, first, v):
    for rows in HALVES:
        axial_backward(axial_ref, [excess[v, zo, rows, :] for zo in range(BLK)], spread, first, v, rows)


LOW, OWN, HIGH = slice(0, BLK), slice(BLK, 2 * BLK), slice(2 * BLK, NEAR)
MESH = pl.DeviceIdType.MESH


def worker_of(bx, bz):
    return 2 * (bx // 2) + (bz % 4) // 2, 4 * (bz // 4) + 2 * (bz % 2) + bx % 2


class Copy:
    def __init__(self, src, dst, sems, slot, device, sends, receives):
        self.src, self.sems, self.slot = src, sems, slot
        self.sends, self.receives = sends, receives
        self.out = self.back = self.make(dst, device)
        self.device = device

    def make(self, dst, device):
        return pltpu.make_async_remote_copy(
            src_ref=self.src, dst_ref=dst, send_sem=self.sems[0].at[self.slot], recv_sem=self.sems[1].at[self.slot],
            device_id=device, device_id_type=MESH,
        )

    def lands_in(self, region):
        self.back = self.make(region, self.device)
        return self

    def start(self):
        pl.when(self.sends)(self.out.start)

    def wait_recv(self):
        pl.when(self.receives)(self.back.wait_recv)

    def wait_send(self):
        pl.when(self.sends)(self.out.wait_send)


def joint_kernel(nx, nz):
    def body(index_ref, axial_ref, axial_in, bank_ref, labels_ref, estimate_ref, outgoing,
             out_ref, kx, ky, ky_back, ax, fwd_y, bwd_y, fwd_x, bwd_x, edge_x, edge_y, base, mid, grown, blurred, excess, spread, total,
             to_far, to_corner, to_side, staged, wide, part_mate, part, product, back,
             passing, arrived, labels, slots, slot_ref,
             move_sems, halo_sems, sum_sems, first_sems, second_sems, local_sems):
        gx, gz = lax.axis_index("gx"), lax.axis_index("gz")
        core, high_z = gz % 2, gx % 2
        bx, bz = gx - high_z + core, gz - gz % 4 + 2 * high_z + (gz % 4) // 2
        has_d, has_u = bz > 0, bz < nz - 1
        bc = bx - 1 + 2 * core
        has_c = (bc >= 0) & (bc < nx)
        bc, bd, bu = (bc + nx) % nx, (bz + nz - 1) % nz, (bz + 1) % nz
        mate = (gx, gz + 1 - 2 * core)
        across, down, up = worker_of(bc, bz), worker_of(bx, bd), worker_of(bx, bu)
        across_down, across_up = worker_of(bc, bd), worker_of(bc, bu)
        worker, owner = worker_of(gx, gz), (bx, bz)
        moved = (bx != gx) | (bz != gz)
        far_side, mate_side = 2 * core, 2 - 2 * core

        def index_of(z):
            return index_ref[jnp.clip(bz * BLK - HALO + z, 0, nz * BLK - 1)]

        staged[...] = estimate_ref[...].astype(BF)
        for it in range(ITERS):
            @pl.when(jnp.logical_not(has_c))
            def _():
                wide[it, :, far_side] = jnp.zeros((NEAR, BLK, LINE), BF)

            for there, rows in ((has_d, LOW), (has_u, HIGH)):
                @pl.when(jnp.logical_not(there))
                def _():
                    wide[it, rows] = jnp.zeros((BLK, 3, BLK, LINE), BF)

        barrier = pltpu.get_barrier_semaphore()

        def greet(device):
            pl.semaphore_signal(barrier, inc=1, device_id=device, device_id_type=MESH)

        for d in range(1, 16):
            greet((2 * ((gx // 2 + d // 4) % 4) + gx % 2, 4 * ((gz // 4 + d % 4) % 4) + gz % 4))
        for d in range(1, 8):
            greet((gx - gx % 2 + (gx % 2 + d // 4) % 2, gz - gz % 4 + (gz % 4 + d % 4) % 4))
        extra = 0
        for there, device in (
            (has_c, across), (has_d, down), (has_u, up), (has_c & has_d, across_down), (has_c & has_u, across_up),
        ):
            pl.when(there)(lambda device=device: greet(device))
            extra = extra + there.astype(jnp.int32)
        pl.semaphore_wait(barrier, 22 + extra)

        moves = [
            Copy(staged, wide.at[0, OWN, 1], move_sems, 0, worker, moved, moved),
            Copy(labels_ref, labels, move_sems, 1, worker, moved, moved),
        ]
        bring = Copy(product, back, move_sems, 2, owner, moved, moved)

        def halo(it):
            w = wide.at[it]
            sems = (halo_sems[0].at[it], halo_sems[1].at[it])
            own = w.at[OWN, 1]
            near = [
                Copy(own, w.at[OWN, mate_side], sems, 1, across, has_c, has_c).lands_in(w.at[OWN, far_side]),
                Copy(own, w.at[OWN, far_side], sems, 0, mate, True, True).lands_in(w.at[OWN, mate_side]),
            ]
            straight = [
                Copy(own, w.at[LOW, 1], sems, 2, up, has_u, has_d),
                Copy(own, w.at[HIGH, 1], sems, 3, down, has_d, has_u),
            ]
            corner = [
                Copy(own, w.at[LOW, mate_side], sems, 4, across_up, has_c & has_u, has_c & has_d).lands_in(
                    w.at[LOW, far_side]),
                Copy(own, w.at[HIGH, mate_side], sems, 5, across_down, has_c & has_d, has_c & has_u).lands_in(
                    w.at[HIGH, far_side]),
            ]
            relay = [
                Copy(w.at[LOW, 1], w.at[LOW, far_side], sems, 6, mate, has_d, has_d).lands_in(w.at[LOW, mate_side]),
                Copy(w.at[HIGH, 1], w.at[HIGH, far_side], sems, 7, mate, has_u, has_u).lands_in(w.at[HIGH, mate_side]),
            ]
            return near, straight, corner, relay

        def sums(it):
            sems = (sum_sems[0].at[it], sum_sems[1].at[it])
            p = part.at[it]
            halves = [slice(BLK, BLK + 8), slice(BLK + 8, 2 * BLK)]
            to_mate = [
                Copy(total.at[rows, mate_side], part_mate.at[it, rows], sems, i, mate, there, there)
                for i, (rows, there) in enumerate(((LOW, has_d), (HIGH, has_u), (halves[0], True), (halves[1], True)))
            ]
            straight = [
                Copy(to_far.at[0], p.at[0], sems, 4, down, has_d, has_u),
                Copy(to_far.at[1], p.at[1], sems, 5, up, has_u, has_d),
            ]
            corner = [
                Copy(to_corner.at[0], p.at[2], sems, 6, across_down, has_c & has_d, has_c & has_u),
                Copy(to_corner.at[1], p.at[3], sems, 7, across_up, has_c & has_u, has_c & has_d),
            ]
            aside = [
                Copy(to_side.at[rows], p.at[4, rows], sems, 8 + i, across, has_c, has_c)
                for i, rows in enumerate((slice(0, 8), slice(8, 16)))
            ]
            return to_mate, straight, corner, aside

        def first_stage(d):
            y, x = (gx // 2 + d // 4) % 4, (gz // 4 + d % 4) % 4
            return pltpu.make_async_remote_copy(
                src_ref=outgoing.at[y, :, x], dst_ref=passing.at[gx // 2, gz // 4],
                send_sem=first_sems[0].at[d], recv_sem=first_sems[1].at[d],
                device_id=(2 * y + gx % 2, 4 * x + gz % 4), device_id_type=MESH,
            )

        def second_stage(d):
            high, low = (gx % 2 + d // 4) % 2, (gz % 4 + d % 4) % 4
            return pltpu.make_async_remote_copy(
                src_ref=passing.at[:, :, low % 2, 2 * high + low // 2], dst_ref=arrived.at[:, gx % 2, :, gz % 4],
                send_sem=second_sems[0].at[d], recv_sem=second_sems[1].at[d],
                device_id=(gx - gx % 2 + high, gz - gz % 4 + low), device_id_type=MESH,
            )

        stay_first = pltpu.make_async_copy(
            outgoing.at[gx // 2, :, gz // 4], passing.at[gx // 2, gz // 4], local_sems.at[0]
        )
        stay_second = pltpu.make_async_copy(
            passing.at[:, :, core, 2 * high_z + (gz % 4) // 2], arrived.at[:, gx % 2, :, gz % 4], local_sems.at[1]
        )
        slot_copy = pltpu.make_async_copy(slots, slot_ref, local_sems.at[2])

        for copy in moves:
            copy.start()

        @pl.when(jnp.logical_not(moved))
        def _():
            wide[0, OWN, 1] = staged[...]
            labels[...] = labels_ref[...]

        stay_first.start()
        for d in range(1, 16):
            first_stage(d).start()
        load_taps(bank_ref, axial_in, kx, ky, ax)
        reverse_taps(ky, ky_back)
        for copy in moves:
            copy.wait_recv()

        for it in range(ITERS):
            w = wide.at[it]
            near, straight, corner, relay = halo(it)
            for copy in near + straight + corner:
                copy.start()
            if it == 0:
                build_bands(ky_back, kx, ax, fwd_y, fwd_x, False)
                slots_of(labels[...], slots)
                slot_copy.start()
            for copy in near:
                copy.wait_recv()
            columns_forward(index_of, fwd_x, w, mid, BLK)
            by_views(lambda v: line_forward(index_of, fwd_y, mid, grown[1], BLK, v))
            for copy in straight:
                copy.wait_recv()
            for copy in relay:
                copy.start()
            if it == 0:
                stay_first.wait()
                for d in range(1, 16):
                    first_stage(d).wait_recv()
                for d in range(1, 8):
                    second_stage(d).start()
                stay_second.start()
            for copy in corner + relay:
                copy.wait_recv()
            for i in (0, 2):
                columns_forward(index_of, fwd_x, w, mid, i * BLK)

                def line_and_axial(v):
                    line_forward(index_of, fwd_y, mid, grown[i], i * BLK, v)
                    gather_axial(axial_ref, grown[1 - i // 2], BLK - i // 2 * BLK, v, blurred)

                by_views(line_and_axial)
            if it == 0:
                ones_response(index_of, ax, kx, ky, bx * BLK, bz * BLK, edge_x, edge_y, base, nx * BLK, nz * BLK)
                build_bands(ky, kx, ax, bwd_y, bwd_x, True)
                for d in range(1, 16):
                    first_stage(d).wait_send()
                for d in range(1, 8):
                    second_stage(d).wait()
                stay_second.wait()
                slot_copy.wait()
                for copy in moves:
                    copy.wait_send()
            for copy in near + straight + corner + relay:
                copy.wait_send()

            by_views(lambda v: ratios(
                axial_ref, slot_ref, grown[2], blurred,
                lambda s: arrived[s // 32, (s // 16) % 2, (s // 4) % 4, s % 4], excess, spread[0], v))
            to_mate, straight, corner, aside = sums(it)
            for i, rows in enumerate((LOW, HIGH)):
                this, after = (0, 2) if i == 0 else (2, 1)

                def line_and_spread(v):
                    line_backward(index_of, bwd_y, spread[this], mid, this * BLK, v)
                    spread_axial(axial_ref, excess, spread[after], after * BLK, v)

                by_views(line_and_spread)
                columns_backward(index_of, bwd_x, mid, total, this * BLK, 0, BLK)
                to_mate[i].start()
                to_corner[i] = total[rows, far_side].astype(BF)
                corner[i].start()
            for i, rows in enumerate((LOW, HIGH)):
                to_mate[i].wait_recv()
                to_far[i] = (total[rows, 1] + jnp.where((has_d, has_u)[i], part_mate[it, rows], 0.0)).astype(BF)
                straight[i].start()
            by_views(lambda v: line_backward(index_of, bwd_y, spread[1], mid, BLK, v))
            for half in range(2):
                first = BLK + 8 * half
                columns_backward(index_of, bwd_x, mid, total, BLK, 8 * half, 8)
                to_side[8 * half : 8 * half + 8] = total[first : first + 8, far_side].astype(BF)
                aside[half].start()
                to_mate[2 + half].start()
            inner = base[...] + total[OWN, 1]
            gain = (1.0 / VIEWS) if it == 0 else product[...] * (1.0 / VIEWS)
            for copy in to_mate[2:]:
                copy.wait_recv()
            inner = inner + part_mate[it, OWN]
            for copy in straight + corner:
                copy.wait_recv()
            for there, which in ((has_u, 0), (has_d, 1), (has_c & has_u, 2), (has_c & has_d, 3)):
                inner = inner + jnp.where(there, part[it, which].astype(F32), 0.0)
            for copy in aside:
                copy.wait_recv()
            inner = inner + jnp.where(has_c, part[it, 4].astype(F32), 0.0)
            product[...] = inner * gain
            if it + 1 < ITERS:
                wide[it + 1, OWN, 1] = (wide[it, OWN, 1].astype(F32) * product[...]).astype(BF)
            else:
                bring.start()
            for copy in to_mate + straight + corner + aside:
                copy.wait_send()

        @pl.when(jnp.logical_not(moved))
        def _():
            back[...] = product[...]

        bring.wait_recv()
        out_ref[...] = estimate_ref[...] * back[...]
        bring.wait_send()

    smem = pl.BlockSpec(memory_space=pltpu.SMEM)
    vmem = pl.BlockSpec(memory_space=pltpu.VMEM)
    dma = pltpu.SemaphoreType.DMA
    block = (BLK, BLK, LINE)
    return pl.pallas_call(
        body,
        name="joint",
        out_shape=jax.ShapeDtypeStruct(block, F32),
        in_specs=[smem] * 2 + [vmem] * 4 + [pl.BlockSpec(memory_space=pl.ANY)],
        out_specs=vmem,
        scratch_shapes=[
            pltpu.VMEM((KERNELS, 8, LINE), F32),
            pltpu.VMEM((KERNELS, 8, LINE), F32),
            pltpu.VMEM((KERNELS, 8, LINE), F32),
            pltpu.VMEM((8, LINE), F32),
            pltpu.VMEM((KERNELS, VIEWS, LINE, LINE), BF),
            pltpu.VMEM((KERNELS, VIEWS, LINE, LINE), BF),
            pltpu.VMEM((KERNELS, VIEWS * BLK, LINE), BF),
            pltpu.VMEM((KERNELS, LINE, VIEWS * BLK), BF),
            pltpu.VMEM((KERNELS, 8, LINE), F32),
            pltpu.VMEM((KERNELS, 8, LINE), F32),
            pltpu.VMEM(block, F32),
            pltpu.VMEM((BLK, VIEWS, BLK, LINE), BF),
            [pltpu.VMEM((VIEWS,) + block, F32)] * 3,
            pltpu.VMEM((VIEWS,) + block, F32),
            pltpu.VMEM((VIEWS,) + block, F32),
            [pltpu.VMEM((VIEWS,) + block, BF)] * 3,
            pltpu.VMEM((NEAR, 3, BLK, LINE), F32),
            pltpu.VMEM((2,) + block, BF),
            pltpu.VMEM((2,) + block, BF),
            pltpu.VMEM(block, BF),
            pltpu.VMEM(block, BF),
            pltpu.VMEM((ITERS, NEAR, 3, BLK, LINE), BF),
            pltpu.VMEM((ITERS, NEAR, BLK, LINE), F32),
            pltpu.VMEM((ITERS, 5) + block, BF),
            pltpu.VMEM(block, F32),
            pltpu.VMEM(block, F32),
            pltpu.VMEM((4, 4, 2, 4, BLK, LINE), BF),
            pltpu.VMEM((4, 2, 4, 4, BLK, LINE), BF),
            pltpu.VMEM((1, LINE), jnp.int32),
            pltpu.VMEM((1, LINE), jnp.int32),
            pltpu.SMEM((1, LINE), jnp.int32),
            (dma((3,)), dma((3,))),
            (dma((ITERS, 8)), dma((ITERS, 8))),
            (dma((ITERS, 10)), dma((ITERS, 10))),
            (dma((16,)), dma((16,))),
            (dma((8,)), dma((8,))),
            dma((3,)),
        ],
        compiler_params=pltpu.CompilerParams(
            vmem_limit_bytes=48 << 20, collective_id=0, has_side_effects=True
        ),
    )


def shards(estimate, view_tiles, incoming_label, lateral_bank, axial_kernel, kernel_index):
    nx, nz = lax.axis_size("gx"), lax.axis_size("gz")
    outgoing = view_tiles[0].reshape(4, 2, 4, 4, BLK, LINE)
    return joint_kernel(nx, nz)(
        kernel_index, axial_kernel, axial_kernel, lateral_bank, incoming_label, estimate, outgoing
    )


def solution(mesh):
    return jax.shard_map(
        shards,
        mesh=mesh,
        in_specs=(P("gz", "gx", None), P(("gx", "gz"), None, None), P(("gx", "gz"), None), P(), P(), P()),
        out_specs=P("gz", "gx", None),
        check_vma=False,
    )
```

```python
import jax
import jax.numpy as jnp
from jax import lax
from jax.experimental import pallas as pl
from jax.experimental.pallas import tpu as pltpu
from jax.sharding import PartitionSpec as P

TAPS = 33
ITERS = 2
HALO = 16
VIEWS = 6
KERNELS = 16
BLK = 16
NEAR = 48
LINE = 128
F32 = jnp.float32
BF = jnp.bfloat16
HI = lax.Precision.HIGHEST


def iota(shape, dim):
    return lax.broadcasted_iota(jnp.int32, shape, dim)


def load_taps(bank_ref, axial_in, kx, ky, ax):
    ax[...] = jnp.zeros_like(ax)
    ax[:VIEWS, :TAPS] = axial_in[...]
    for dim, taps in ((0, kx), (1, ky)):
        taps[...] = jnp.zeros_like(taps)
        for v in range(VIEWS):
            taps[:, v, :TAPS] = bank_ref[v, :, dim, :]
        raw = taps[...]
        total = jnp.sum(raw, axis=-1, keepdims=True)
        taps[...] = raw / jnp.where(total > 0.0, total, 1.0)


def line_scale(ax):
    axial = jnp.sum(ax[...], axis=1, keepdims=True)
    return jnp.broadcast_to(1.0 / jnp.where(axial > 0.0, axial, 1.0), (8, LINE))


def reverse_taps(ky, ky_back):
    flip = jnp.where(iota((LINE, LINE), 0) + iota((LINE, LINE), 1) == TAPS - 1, 1.0, 0.0)
    taps = ky[...].reshape(KERNELS * 8, LINE)
    ky_back[...] = jnp.dot(taps, flip, precision=HI, preferred_element_type=F32).reshape(KERNELS, 8, LINE)


def build_bands(ky, kx, ax, bands_y, bands_x, spread_out):
    inside = jnp.abs(iota((LINE, LINE), 0) - iota((LINE, LINE), 1)) <= HALO
    scale = line_scale(ax)

    @pl.loop(0, KERNELS)
    def _(k):
        taps_x = kx[k]
        taps_y = ky[k] * scale
        rows = []
        for v in range(VIEWS):
            band = jnp.broadcast_to(taps_y[v : v + 1], (LINE, LINE))
            band = pltpu.roll(band, LINE - HALO, 1, stride=1, stride_axis=0)
            bands_y[k, v] = jnp.where(inside, band, 0.0).astype(BF)
            rows.append(pltpu.roll(jnp.broadcast_to(taps_x[v : v + 1], (BLK, LINE)), 0, 1, stride=1, stride_axis=0))
        across = jnp.concatenate(rows, 0)
        bands_x[k] = (across.T if spread_out else across).astype(BF)


def ones_response(index_of, ax, kx_ref, ky_ref, col0, depth0, edge_x, edge_y, base_ref, cols, depths):
    tap = iota((LINE, LINE), 0)
    pos = iota((LINE, LINE), 1)
    at_x = col0 + pos - tap + HALO
    at_y = pos - tap + HALO
    ok_x = jnp.where((at_x >= 0) & (at_x < cols), 1.0, 0.0)
    ok_y = jnp.where((at_y >= 0) & (at_y < LINE), 1.0, 0.0)
    kx = kx_ref[...].reshape(KERNELS * 8, LINE)
    ky = ky_ref[...].reshape(KERNELS * 8, LINE)
    edge_x[...] = jnp.dot(kx, ok_x, precision=HI, preferred_element_type=F32).reshape(KERNELS, 8, LINE)
    edge_y[...] = jnp.dot(ky, ok_y, precision=HI, preferred_element_type=F32).reshape(KERNELS, 8, LINE)
    axial = ax[...]
    total = jnp.sum(axial, axis=1, keepdims=True)
    axial = axial / jnp.where(total > 0.0, total, 1.0)
    lane = iota((8, LINE), 1)
    for z in range(BLK):
        k = index_of(HALO + z)
        at_z = depth0 + z - lane + HALO
        part = jnp.sum(jnp.where((at_z >= 0) & (at_z < depths), axial, 0.0), axis=1, keepdims=True)
        left = edge_x[k][:, :BLK] * part
        base_ref[z] = lax.dot_general(
            left, edge_y[k], (((0,), (0,)), ((), ())), precision=HI, preferred_element_type=F32
        )


def slots_of(labels, slots):
    column = jnp.broadcast_to(labels, (LINE, LINE)).T
    hit = column == iota((LINE, LINE), 1)
    slots[...] = jnp.max(jnp.where(hit, iota((LINE, LINE), 0), -1), axis=0, keepdims=True)


def lateral_forward(index_of, fwd_x, fwd_y, wide, mid, grown, first):
    depths = range(first, first + BLK)
    for z in depths:
        mid[z] = jnp.dot(
            fwd_x[index_of(z)][:, :NEAR], wide[z].reshape(NEAR, LINE), preferred_element_type=F32
        ).astype(BF)
    for z in depths:
        for v in range(VIEWS):
            grown[v, z] = jnp.dot(
                mid[z, v * BLK : (v + 1) * BLK, :], fwd_y[index_of(z), v], preferred_element_type=F32
            )


def lateral_backward(index_of, bwd_x, bwd_y, spread, mid, total, first):
    depths = range(first, first + BLK)
    for z in depths:
        for v in range(VIEWS):
            mid[z, v * BLK : (v + 1) * BLK, :] = jnp.dot(
                spread[v, z], bwd_y[index_of(z), v], preferred_element_type=F32
            ).astype(BF)
    for z in depths:
        total[z] = jnp.dot(bwd_x[index_of(z)][:NEAR], mid[z], preferred_element_type=F32).reshape(3, BLK, LINE)


HALVES = (slice(0, 8), slice(8, 16))


def reached(zi):
    return range(max(0, zi - 2 * HALO), min(BLK - 1, zi) + 1)


def axial_backward(axial_ref, excess, spread, first, v, rows):
    for zi in range(first, first + BLK):
        acc = None
        for zo in reached(zi):
            term = axial_ref[v, zi - zo] * excess[zo]
            acc = term if acc is None else acc + term
        spread[v, zi, rows, :] = acc.astype(BF)


def ratios(axial_ref, slot_ref, grown, tile_of, excess, spread):
    @pl.loop(0, VIEWS)
    def _(v):
        seen = jnp.full((8, LINE), slot_ref[0, v * BLK], jnp.int32) >= 0
        for rows in HALVES:
            total = [None] * BLK
            for zi in range(NEAR):
                g = grown[v, zi, rows, :]
                for zo in reached(zi):
                    term = axial_ref[v, zi - zo] * g
                    total[zo] = term if total[zo] is None else total[zo] + term
            over = []
            for zo in range(BLK):
                tile = tile_of(jnp.maximum(slot_ref[0, v * BLK + zo], 0))[rows].astype(F32)
                ratio = (tile / total[zo]).astype(BF).astype(F32)
                over.append(jnp.where(seen, ratio - 1.0, 0.0))
                excess[v, zo, rows, :] = over[-1]
            axial_backward(axial_ref, over, spread, 0, v, rows)


def spread_axial(axial_ref, excess, spread, first):
    @pl.loop(0, VIEWS)
    def _(v):
        for rows in HALVES:
            axial_backward(axial_ref, [excess[v, zo, rows, :] for zo in range(BLK)], spread, first, v, rows)


LOW, OWN, HIGH = slice(0, BLK), slice(BLK, 2 * BLK), slice(2 * BLK, NEAR)
MESH = pl.DeviceIdType.MESH


def worker_of(bx, bz):
    return 2 * (bx // 2) + (bz % 4) // 2, 4 * (bz // 4) + 2 * (bz % 2) + bx % 2


class Copy:
    def __init__(self, src, dst, sems, slot, device, sends, receives):
        self.src, self.sems, self.slot = src, sems, slot
        self.sends, self.receives = sends, receives
        self.out = self.back = self.make(dst, device)
        self.device = device

    def make(self, dst, device):
        return pltpu.make_async_remote_copy(
            src_ref=self.src, dst_ref=dst, send_sem=self.sems[0].at[self.slot], recv_sem=self.sems[1].at[self.slot],
            device_id=device, device_id_type=MESH,
        )

    def lands_in(self, region):
        self.back = self.make(region, self.device)
        return self

    def start(self):
        pl.when(self.sends)(self.out.start)

    def wait_recv(self):
        pl.when(self.receives)(self.back.wait_recv)

    def wait_send(self):
        pl.when(self.sends)(self.out.wait_send)


def joint_kernel(nx, nz):
    def body(index_ref, axial_ref, axial_in, bank_ref, labels_ref, estimate_ref, outgoing,
             out_ref, kx, ky, ky_back, ax, fwd_y, bwd_y, fwd_x, bwd_x, edge_x, edge_y, base, mid, grown, excess, spread, total,
             to_far, to_corner, to_side, staged, wide, part_mate, part, product, back,
             passing, arrived, labels, slots, slot_ref,
             move_sems, halo_sems, sum_sems, first_sems, second_sems, local_sems):
        gx, gz = lax.axis_index("gx"), lax.axis_index("gz")
        core, high_z = gz % 2, gx % 2
        bx, bz = gx - high_z + core, gz - gz % 4 + 2 * high_z + (gz % 4) // 2
        has_d, has_u = bz > 0, bz < nz - 1
        bc = bx - 1 + 2 * core
        has_c = (bc >= 0) & (bc < nx)
        bc, bd, bu = (bc + nx) % nx, (bz + nz - 1) % nz, (bz + 1) % nz
        mate = (gx, gz + 1 - 2 * core)
        across, down, up = worker_of(bc, bz), worker_of(bx, bd), worker_of(bx, bu)
        across_down, across_up = worker_of(bc, bd), worker_of(bc, bu)
        worker, owner = worker_of(gx, gz), (bx, bz)
        moved = (bx != gx) | (bz != gz)
        far_side, mate_side = 2 * core, 2 - 2 * core

        def index_of(z):
            return index_ref[jnp.clip(bz * BLK - HALO + z, 0, nz * BLK - 1)]

        barrier = pltpu.get_barrier_semaphore()

        def greet(device):
            pl.semaphore_signal(barrier, inc=1, device_id=device, device_id_type=MESH)

        for d in range(1, 16):
            greet((2 * ((gx // 2 + d // 4) % 4) + gx % 2, 4 * ((gz // 4 + d % 4) % 4) + gz % 4))
        for d in range(1, 8):
            greet((gx - gx % 2 + (gx % 2 + d // 4) % 2, gz - gz % 4 + (gz % 4 + d % 4) % 4))
        extra = 0
        for there, device in (
            (has_c, across), (has_d, down), (has_u, up), (has_c & has_d, across_down), (has_c & has_u, across_up),
        ):
            pl.when(there)(lambda device=device: greet(device))
            extra = extra + there.astype(jnp.int32)
        staged[...] = estimate_ref[...].astype(BF)
        pl.semaphore_wait(barrier, 22 + extra)

        moves = [
            Copy(staged, wide.at[0, OWN, 1], move_sems, 0, worker, moved, moved),
            Copy(labels_ref, labels, move_sems, 1, worker, moved, moved),
        ]
        bring = Copy(product, back, move_sems, 2, owner, moved, moved)

        def halo(it):
            w = wide.at[it]
            sems = (halo_sems[0].at[it], halo_sems[1].at[it])
            own = w.at[OWN, 1]
            near = [
                Copy(own, w.at[OWN, mate_side], sems, 1, across, has_c, has_c).lands_in(w.at[OWN, far_side]),
                Copy(own, w.at[OWN, far_side], sems, 0, mate, True, True).lands_in(w.at[OWN, mate_side]),
            ]
            straight = [
                Copy(own, w.at[LOW, 1], sems, 2, up, has_u, has_d),
                Copy(own, w.at[HIGH, 1], sems, 3, down, has_d, has_u),
            ]
            corner = [
                Copy(own, w.at[LOW, mate_side], sems, 4, across_up, has_c & has_u, has_c & has_d).lands_in(
                    w.at[LOW, far_side]),
                Copy(own, w.at[HIGH, mate_side], sems, 5, across_down, has_c & has_d, has_c & has_u).lands_in(
                    w.at[HIGH, far_side]),
            ]
            relay = [
                Copy(w.at[LOW, 1], w.at[LOW, far_side], sems, 6, mate, has_d, has_d).lands_in(w.at[LOW, mate_side]),
                Copy(w.at[HIGH, 1], w.at[HIGH, far_side], sems, 7, mate, has_u, has_u).lands_in(w.at[HIGH, mate_side]),
            ]
            return near, straight, corner, relay

        def sums(it):
            sems = (sum_sems[0].at[it], sum_sems[1].at[it])
            p = part.at[it]
            to_mate = [
                Copy(total.at[rows, mate_side], part_mate.at[it, rows], sems, i, mate, there, there)
                for i, (rows, there) in enumerate(((LOW, has_d), (HIGH, has_u), (OWN, True)))
            ]
            straight = [
                Copy(to_far.at[0], p.at[0], sems, 4, down, has_d, has_u),
                Copy(to_far.at[1], p.at[1], sems, 5, up, has_u, has_d),
            ]
            corner = [
                Copy(to_corner.at[0], p.at[2], sems, 6, across_down, has_c & has_d, has_c & has_u),
                Copy(to_corner.at[1], p.at[3], sems, 7, across_up, has_c & has_u, has_c & has_d),
            ]
            aside = [Copy(to_side, p.at[4], sems, 8, across, has_c, has_c)]
            return to_mate, straight, corner, aside

        def first_stage(d):
            y, x = (gx // 2 + d // 4) % 4, (gz // 4 + d % 4) % 4
            return pltpu.make_async_remote_copy(
                src_ref=outgoing.at[y, :, x], dst_ref=passing.at[gx // 2, gz // 4],
                send_sem=first_sems[0].at[d], recv_sem=first_sems[1].at[d],
                device_id=(2 * y + gx % 2, 4 * x + gz % 4), device_id_type=MESH,
            )

        def second_stage(d):
            high, low = (gx % 2 + d // 4) % 2, (gz % 4 + d % 4) % 4
            return pltpu.make_async_remote_copy(
                src_ref=passing.at[:, :, low % 2, 2 * high + low // 2], dst_ref=arrived.at[:, gx % 2, :, gz % 4],
                send_sem=second_sems[0].at[d], recv_sem=second_sems[1].at[d],
                device_id=(gx - gx % 2 + high, gz - gz % 4 + low), device_id_type=MESH,
            )

        stay_first = pltpu.make_async_copy(
            outgoing.at[gx // 2, :, gz // 4], passing.at[gx // 2, gz // 4], local_sems.at[0]
        )
        stay_second = pltpu.make_async_copy(
            passing.at[:, :, core, 2 * high_z + (gz % 4) // 2], arrived.at[:, gx % 2, :, gz % 4], local_sems.at[1]
        )
        slot_copy = pltpu.make_async_copy(slots, slot_ref, local_sems.at[2])

        for copy in moves:
            copy.start()

        @pl.when(jnp.logical_not(moved))
        def _():
            wide[0, OWN, 1] = staged[...]
            labels[...] = labels_ref[...]

        stay_first.start()
        for d in range(1, 16):
            first_stage(d).start()
        load_taps(bank_ref, axial_in, kx, ky, ax)
        for it in range(ITERS):
            @pl.when(jnp.logical_not(has_c))
            def _():
                wide[it, :, far_side] = jnp.zeros((NEAR, BLK, LINE), BF)

            for there, rows in ((has_d, LOW), (has_u, HIGH)):
                @pl.when(jnp.logical_not(there))
                def _():
                    wide[it, rows] = jnp.zeros((BLK, 3, BLK, LINE), BF)

        reverse_taps(ky, ky_back)
        for copy in moves:
            copy.wait_recv()

        for it in range(ITERS):
            w = wide.at[it]
            near, straight, corner, relay = halo(it)
            for copy in near + straight + corner:
                copy.start()
            if it == 0:
                build_bands(ky_back, kx, ax, fwd_y, fwd_x, False)
                slots_of(labels[...], slots)
                slot_copy.start()
            for copy in near:
                copy.wait_recv()
            lateral_forward(index_of, fwd_x, fwd_y, w, mid, grown, BLK)
            for copy in straight:
                copy.wait_recv()
            for copy in relay:
                copy.start()
            if it == 0:
                stay_first.wait()
                for d in range(1, 16):
                    first_stage(d).wait_recv()
                for d in range(1, 8):
                    second_stage(d).start()
                stay_second.start()
            for copy in corner + relay:
                copy.wait_recv()
            lateral_forward(index_of, fwd_x, fwd_y, w, mid, grown, 0)
            lateral_forward(index_of, fwd_x, fwd_y, w, mid, grown, 2 * BLK)
            if it == 0:
                ones_response(index_of, ax, kx, ky, bx * BLK, bz * BLK, edge_x, edge_y, base, nx * BLK, nz * BLK)
                build_bands(ky, kx, ax, bwd_y, bwd_x, True)
                for d in range(1, 16):
                    first_stage(d).wait_send()
                for d in range(1, 8):
                    second_stage(d).wait()
                stay_second.wait()
                slot_copy.wait()
                for copy in moves:
                    copy.wait_send()
            for copy in near + straight + corner + relay:
                copy.wait_send()

            ratios(axial_ref, slot_ref, grown,
                   lambda s: arrived[s // 32, (s // 16) % 2, (s // 4) % 4, s % 4], excess, spread)
            to_mate, straight, corner, aside = sums(it)

            def send_straight(i, rows, there):
                to_mate[i].wait_recv()
                to_far[i] = (total[rows, 1] + jnp.where(there, part_mate[it, rows], 0.0)).astype(BF)
                straight[i].start()

            lateral_backward(index_of, bwd_x, bwd_y, spread, mid, total, 0)
            to_mate[0].start()
            to_corner[0] = total[LOW, far_side].astype(BF)
            corner[0].start()
            spread_axial(axial_ref, excess, spread, 2 * BLK)
            lateral_backward(index_of, bwd_x, bwd_y, spread, mid, total, 2 * BLK)
            to_mate[1].start()
            to_corner[1] = total[HIGH, far_side].astype(BF)
            corner[1].start()
            send_straight(0, LOW, has_d)
            spread_axial(axial_ref, excess, spread, BLK)
            send_straight(1, HIGH, has_u)
            lateral_backward(index_of, bwd_x, bwd_y, spread, mid, total, BLK)
            to_side[...] = total[OWN, far_side].astype(BF)
            aside[0].start()
            to_mate[2].start()
            inner = base[...] + total[OWN, 1]
            gain = (1.0 / VIEWS) if it == 0 else product[...] * (1.0 / VIEWS)
            for copy in to_mate[2:]:
                copy.wait_recv()
            inner = inner + part_mate[it, OWN]
            for copy in straight + corner:
                copy.wait_recv()
            for there, which in ((has_u, 0), (has_d, 1), (has_c & has_u, 2), (has_c & has_d, 3)):
                inner = inner + jnp.where(there, part[it, which].astype(F32), 0.0)
            for copy in aside:
                copy.wait_recv()
            inner = inner + jnp.where(has_c, part[it, 4].astype(F32), 0.0)
            product[...] = inner * gain
            if it + 1 < ITERS:
                wide[it + 1, OWN, 1] = (wide[it, OWN, 1].astype(F32) * product[...]).astype(BF)
            else:
                bring.start()
            for copy in to_mate + straight + corner + aside:
                copy.wait_send()

        @pl.when(jnp.logical_not(moved))
        def _():
            back[...] = product[...]

        bring.wait_recv()
        out_ref[...] = estimate_ref[...] * back[...]
        bring.wait_send()

    smem = pl.BlockSpec(memory_space=pltpu.SMEM)
    vmem = pl.BlockSpec(memory_space=pltpu.VMEM)
    dma = pltpu.SemaphoreType.DMA
    block = (BLK, BLK, LINE)
    return pl.pallas_call(
        body,
        name="joint",
        out_shape=jax.ShapeDtypeStruct(block, F32),
        in_specs=[smem] * 2 + [vmem] * 4 + [pl.BlockSpec(memory_space=pl.ANY)],
        out_specs=vmem,
        scratch_shapes=[
            pltpu.VMEM((KERNELS, 8, LINE), F32),
            pltpu.VMEM((KERNELS, 8, LINE), F32),
            pltpu.VMEM((KERNELS, 8, LINE), F32),
            pltpu.VMEM((8, LINE), F32),
            pltpu.VMEM((KERNELS, VIEWS, LINE, LINE), BF),
            pltpu.VMEM((KERNELS, VIEWS, LINE, LINE), BF),
            pltpu.VMEM((KERNELS, VIEWS * BLK, LINE), BF),
            pltpu.VMEM((KERNELS, LINE, VIEWS * BLK), BF),
            pltpu.VMEM((KERNELS, 8, LINE), F32),
            pltpu.VMEM((KERNELS, 8, LINE), F32),
            pltpu.VMEM(block, F32),
            pltpu.VMEM((NEAR, VIEWS * BLK, LINE), BF),
            pltpu.VMEM((VIEWS, NEAR, BLK, LINE), F32),
            pltpu.VMEM((VIEWS,) + block, F32),
            pltpu.VMEM((VIEWS, NEAR, BLK, LINE), BF),
            pltpu.VMEM((NEAR, 3, BLK, LINE), F32),
            pltpu.VMEM((2,) + block, BF),
            pltpu.VMEM((2,) + block, BF),
            pltpu.VMEM(block, BF),
            pltpu.VMEM(block, BF),
            pltpu.VMEM((ITERS, NEAR, 3, BLK, LINE), BF),
            pltpu.VMEM((ITERS, NEAR, BLK, LINE), F32),
            pltpu.VMEM((ITERS, 5) + block, BF),
            pltpu.VMEM(block, F32),
            pltpu.VMEM(block, F32),
            pltpu.VMEM((4, 4, 2, 4, BLK, LINE), BF),
            pltpu.VMEM((4, 2, 4, 4, BLK, LINE), BF),
            pltpu.VMEM((1, LINE), jnp.int32),
            pltpu.VMEM((1, LINE), jnp.int32),
            pltpu.SMEM((1, LINE), jnp.int32),
            (dma((3,)), dma((3,))),
            (dma((ITERS, 8)), dma((ITERS, 8))),
            (dma((ITERS, 10)), dma((ITERS, 10))),
            (dma((16,)), dma((16,))),
            (dma((8,)), dma((8,))),
            dma((3,)),
        ],
        compiler_params=pltpu.CompilerParams(
            vmem_limit_bytes=48 << 20, collective_id=0, has_side_effects=True
        ),
    )


def shards(estimate, view_tiles, incoming_label, lateral_bank, axial_kernel, kernel_index):
    nx, nz = lax.axis_size("gx"), lax.axis_size("gz")
    outgoing = view_tiles[0].reshape(4, 2, 4, 4, BLK, LINE)
    return joint_kernel(nx, nz)(
        kernel_index, axial_kernel, axial_kernel, lateral_bank, incoming_label, estimate, outgoing
    )


def solution(mesh):
    return jax.shard_map(
        shards,
        mesh=mesh,
        in_specs=(P("gz", "gx", None), P(("gx", "gz"), None, None), P(("gx", "gz"), None), P(), P(), P()),
        out_specs=P("gz", "gx", None),
        check_vma=False,
    )
```

```python
import jax
import jax.numpy as jnp
from jax import lax
from jax.experimental import pallas as pl
from jax.experimental.pallas import tpu as pltpu
from jax.sharding import PartitionSpec as P

TAPS = 33
ITERS = 2
HALO = 16
VIEWS = 6
KERNELS = 16
BLK = 16
NEAR = 48
LINE = 128
F32 = jnp.float32
BF = jnp.bfloat16
HI = lax.Precision.HIGHEST


def iota(shape, dim):
    return lax.broadcasted_iota(jnp.int32, shape, dim)


def load_taps(bank_ref, axial_in, kx, ky, ax):
    ax[...] = jnp.zeros_like(ax)
    ax[:VIEWS, :TAPS] = axial_in[...]
    for dim, taps in ((0, kx), (1, ky)):
        taps[...] = jnp.zeros_like(taps)
        for v in range(VIEWS):
            taps[:, v, :TAPS] = bank_ref[v, :, dim, :]
        raw = taps[...]
        total = jnp.sum(raw, axis=-1, keepdims=True)
        taps[...] = raw / jnp.where(total > 0.0, total, 1.0)


def line_scale(ax):
    axial = jnp.sum(ax[...], axis=1, keepdims=True)
    return jnp.broadcast_to(1.0 / jnp.where(axial > 0.0, axial, 1.0), (8, LINE))


def reverse_taps(ky, ky_back):
    flip = jnp.where(iota((LINE, LINE), 0) + iota((LINE, LINE), 1) == TAPS - 1, 1.0, 0.0)
    taps = ky[...].reshape(KERNELS * 8, LINE)
    ky_back[...] = jnp.dot(taps, flip, precision=HI, preferred_element_type=F32).reshape(KERNELS, 8, LINE)


def build_bands(ky, kx, ax, bands_y, bands_x, spread_out):
    inside = jnp.abs(iota((LINE, LINE), 0) - iota((LINE, LINE), 1)) <= HALO
    scale = line_scale(ax)

    @pl.loop(0, KERNELS)
    def _(k):
        taps_x = kx[k]
        taps_y = ky[k] * scale
        rows = []
        for v in range(VIEWS):
            band = jnp.broadcast_to(taps_y[v : v + 1], (LINE, LINE))
            band = pltpu.roll(band, LINE - HALO, 1, stride=1, stride_axis=0)
            bands_y[k, v] = jnp.where(inside, band, 0.0).astype(BF)
            rows.append(pltpu.roll(jnp.broadcast_to(taps_x[v : v + 1], (BLK, LINE)), 0, 1, stride=1, stride_axis=0))
        across = jnp.concatenate(rows, 0)
        bands_x[k] = (across.T if spread_out else across).astype(BF)


def ones_response(index_of, ax, kx_ref, ky_ref, col0, depth0, edge_x, edge_y, base_ref, cols, depths):
    tap = iota((LINE, LINE), 0)
    pos = iota((LINE, LINE), 1)
    at_x = col0 + pos - tap + HALO
    at_y = pos - tap + HALO
    ok_x = jnp.where((at_x >= 0) & (at_x < cols), 1.0, 0.0)
    ok_y = jnp.where((at_y >= 0) & (at_y < LINE), 1.0, 0.0)
    kx = kx_ref[...].reshape(KERNELS * 8, LINE)
    ky = ky_ref[...].reshape(KERNELS * 8, LINE)
    edge_x[...] = jnp.dot(kx, ok_x, precision=HI, preferred_element_type=F32).reshape(KERNELS, 8, LINE)
    edge_y[...] = jnp.dot(ky, ok_y, precision=HI, preferred_element_type=F32).reshape(KERNELS, 8, LINE)
    axial = ax[...]
    total = jnp.sum(axial, axis=1, keepdims=True)
    axial = axial / jnp.where(total > 0.0, total, 1.0)
    lane = iota((8, LINE), 1)
    for z in range(BLK):
        k = index_of(HALO + z)
        at_z = depth0 + z - lane + HALO
        part = jnp.sum(jnp.where((at_z >= 0) & (at_z < depths), axial, 0.0), axis=1, keepdims=True)
        left = edge_x[k][:, :BLK] * part
        base_ref[z] = lax.dot_general(
            left, edge_y[k], (((0,), (0,)), ((), ())), precision=HI, preferred_element_type=F32
        )


def slots_of(labels, slots):
    column = jnp.broadcast_to(labels, (LINE, LINE)).T
    hit = column == iota((LINE, LINE), 1)
    slots[...] = jnp.max(jnp.where(hit, iota((LINE, LINE), 0), -1), axis=0, keepdims=True)


def lateral_forward(index_of, fwd_x, fwd_y, wide, mid, grown, first):
    depths = range(first, first + BLK)
    for z in depths:
        mid[z] = jnp.dot(
            fwd_x[index_of(z)][:, :NEAR], wide[z].reshape(NEAR, LINE), preferred_element_type=F32
        ).astype(BF)
    for z in depths:
        for v in range(VIEWS):
            grown[v, z] = jnp.dot(
                mid[z, v * BLK : (v + 1) * BLK, :], fwd_y[index_of(z), v], preferred_element_type=F32
            )


def lateral_backward(index_of, bwd_x, bwd_y, spread, mid, total, first):
    depths = range(first, first + BLK)
    for z in depths:
        for v in range(VIEWS):
            mid[z, v * BLK : (v + 1) * BLK, :] = jnp.dot(
                spread[v, z], bwd_y[index_of(z), v], preferred_element_type=F32
            ).astype(BF)
    for z in depths:
        total[z] = jnp.dot(bwd_x[index_of(z)][:NEAR], mid[z], preferred_element_type=F32).reshape(3, BLK, LINE)


HALVES = (slice(0, 8), slice(8, 16))


def reached(zi):
    return range(max(0, zi - 2 * HALO), min(BLK - 1, zi) + 1)


def axial_backward(weights, excess, spread, first, v, rows):
    for zi in range(first, first + BLK):
        acc = None
        for zo in reached(zi):
            term = weights[zi - zo] * excess[zo]
            acc = term if acc is None else acc + term
        spread[v, zi, rows, :] = acc.astype(BF)


def ratios(axial_ref, slot_ref, grown, tile_of, excess, spread):
    @pl.loop(0, VIEWS)
    def _(v):
        weights = [axial_ref[v, t] for t in range(TAPS)]
        seen = jnp.full((8, LINE), slot_ref[0, v * BLK], jnp.int32) >= 0
        for rows in HALVES:
            total = [None] * BLK
            for zi in range(NEAR):
                g = grown[v, zi, rows, :]
                for zo in reached(zi):
                    term = weights[zi - zo] * g
                    total[zo] = term if total[zo] is None else total[zo] + term
            over = []
            for zo in range(BLK):
                tile = tile_of(jnp.maximum(slot_ref[0, v * BLK + zo], 0))[rows].astype(F32)
                ratio = (tile / total[zo]).astype(BF).astype(F32)
                over.append(jnp.where(seen, ratio - 1.0, 0.0))
                excess[v, zo, rows, :] = over[-1]
            axial_backward(weights, over, spread, 0, v, rows)


def spread_axial(axial_ref, excess, spread, first):
    @pl.loop(0, VIEWS)
    def _(v):
        weights = [axial_ref[v, t] for t in range(TAPS)]
        for rows in HALVES:
            axial_backward(weights, [excess[v, zo, rows, :] for zo in range(BLK)], spread, first, v, rows)


LOW, OWN, HIGH = slice(0, BLK), slice(BLK, 2 * BLK), slice(2 * BLK, NEAR)
MESH = pl.DeviceIdType.MESH


def worker_of(bx, bz):
    return 2 * (bx // 2) + (bz % 4) // 2, 4 * (bz // 4) + 2 * (bz % 2) + bx % 2


class Copy:
    def __init__(self, src, dst, sems, slot, device, sends, receives):
        self.src, self.sems, self.slot = src, sems, slot
        self.sends, self.receives = sends, receives
        self.out = self.back = self.make(dst, device)
        self.device = device

    def make(self, dst, device):
        return pltpu.make_async_remote_copy(
            src_ref=self.src, dst_ref=dst, send_sem=self.sems[0].at[self.slot], recv_sem=self.sems[1].at[self.slot],
            device_id=device, device_id_type=MESH,
        )

    def lands_in(self, region):
        self.back = self.make(region, self.device)
        return self

    def start(self):
        pl.when(self.sends)(self.out.start)

    def wait_recv(self):
        pl.when(self.receives)(self.back.wait_recv)

    def wait_send(self):
        pl.when(self.sends)(self.out.wait_send)


def joint_kernel(nx, nz):
    def body(index_ref, axial_ref, axial_in, bank_ref, labels_ref, estimate_ref, outgoing,
             out_ref, kx, ky, ky_back, ax, fwd_y, bwd_y, fwd_x, bwd_x, edge_x, edge_y, base, mid, grown, excess, spread, total,
             to_far, to_corner, to_side, staged, wide, part_mate, part, product, back,
             passing, arrived, labels, slots, slot_ref,
             move_sems, halo_sems, sum_sems, first_sems, second_sems, local_sems):
        gx, gz = lax.axis_index("gx"), lax.axis_index("gz")
        core, high_z = gz % 2, gx % 2
        bx, bz = gx - high_z + core, gz - gz % 4 + 2 * high_z + (gz % 4) // 2
        has_d, has_u = bz > 0, bz < nz - 1
        bc = bx - 1 + 2 * core
        has_c = (bc >= 0) & (bc < nx)
        bc, bd, bu = (bc + nx) % nx, (bz + nz - 1) % nz, (bz + 1) % nz
        mate = (gx, gz + 1 - 2 * core)
        across, down, up = worker_of(bc, bz), worker_of(bx, bd), worker_of(bx, bu)
        across_down, across_up = worker_of(bc, bd), worker_of(bc, bu)
        worker, owner = worker_of(gx, gz), (bx, bz)
        moved = (bx != gx) | (bz != gz)
        far_side, mate_side = 2 * core, 2 - 2 * core

        def index_of(z):
            return index_ref[jnp.clip(bz * BLK - HALO + z, 0, nz * BLK - 1)]

        barrier = pltpu.get_barrier_semaphore()

        def greet(device):
            pl.semaphore_signal(barrier, inc=1, device_id=device, device_id_type=MESH)

        for d in range(1, 16):
            greet((2 * ((gx // 2 + d // 4) % 4) + gx % 2, 4 * ((gz // 4 + d % 4) % 4) + gz % 4))
        for d in range(1, 8):
            greet((gx - gx % 2 + (gx % 2 + d // 4) % 2, gz - gz % 4 + (gz % 4 + d % 4) % 4))
        extra = 0
        for there, device in (
            (has_c, across), (has_d, down), (has_u, up), (has_c & has_d, across_down), (has_c & has_u, across_up),
        ):
            pl.when(there)(lambda device=device: greet(device))
            extra = extra + there.astype(jnp.int32)
        staged[...] = estimate_ref[...].astype(BF)
        pl.semaphore_wait(barrier, 22 + extra)

        moves = [
            Copy(staged, wide.at[0, OWN, 1], move_sems, 0, worker, moved, moved),
            Copy(labels_ref, labels, move_sems, 1, worker, moved, moved),
        ]
        bring = Copy(product, back, move_sems, 2, owner, moved, moved)

        def halo(it):
            w = wide.at[it]
            sems = (halo_sems[0].at[it], halo_sems[1].at[it])
            own = w.at[OWN, 1]
            near = [
                Copy(own, w.at[OWN, mate_side], sems, 1, across, has_c, has_c).lands_in(w.at[OWN, far_side]),
                Copy(own, w.at[OWN, far_side], sems, 0, mate, True, True).lands_in(w.at[OWN, mate_side]),
            ]
            straight = [
                Copy(own, w.at[LOW, 1], sems, 2, up, has_u, has_d),
                Copy(own, w.at[HIGH, 1], sems, 3, down, has_d, has_u),
            ]
            corner = [
                Copy(own, w.at[LOW, mate_side], sems, 4, across_up, has_c & has_u, has_c & has_d).lands_in(
                    w.at[LOW, far_side]),
                Copy(own, w.at[HIGH, mate_side], sems, 5, across_down, has_c & has_d, has_c & has_u).lands_in(
                    w.at[HIGH, far_side]),
            ]
            relay = [
                Copy(w.at[LOW, 1], w.at[LOW, far_side], sems, 6, mate, has_d, has_d).lands_in(w.at[LOW, mate_side]),
                Copy(w.at[HIGH, 1], w.at[HIGH, far_side], sems, 7, mate, has_u, has_u).lands_in(w.at[HIGH, mate_side]),
            ]
            return near, straight, corner, relay

        def sums(it):
            sems = (sum_sems[0].at[it], sum_sems[1].at[it])
            p = part.at[it]
            to_mate = [
                Copy(total.at[rows, mate_side], part_mate.at[it, rows], sems, i, mate, there, there)
                for i, (rows, there) in enumerate(((LOW, has_d), (HIGH, has_u), (OWN, True)))
            ]
            straight = [
                Copy(to_far.at[0], p.at[0], sems, 4, down, has_d, has_u),
                Copy(to_far.at[1], p.at[1], sems, 5, up, has_u, has_d),
            ]
            corner = [
                Copy(to_corner.at[0], p.at[2], sems, 6, across_down, has_c & has_d, has_c & has_u),
                Copy(to_corner.at[1], p.at[3], sems, 7, across_up, has_c & has_u, has_c & has_d),
            ]
            aside = [Copy(to_side, p.at[4], sems, 8, across, has_c, has_c)]
            return to_mate, straight, corner, aside

        def first_stage(d):
            y, x = (gx // 2 + d // 4) % 4, (gz // 4 + d % 4) % 4
            return pltpu.make_async_remote_copy(
                src_ref=outgoing.at[y, :, x], dst_ref=passing.at[gx // 2, gz // 4],
                send_sem=first_sems[0].at[d], recv_sem=first_sems[1].at[d],
                device_id=(2 * y + gx % 2, 4 * x + gz % 4), device_id_type=MESH,
            )

        def second_stage(d):
            high, low = (gx % 2 + d // 4) % 2, (gz % 4 + d % 4) % 4
            return pltpu.make_async_remote_copy(
                src_ref=passing.at[:, :, low % 2, 2 * high + low // 2], dst_ref=arrived.at[:, gx % 2, :, gz % 4],
                send_sem=second_sems[0].at[d], recv_sem=second_sems[1].at[d],
                device_id=(gx - gx % 2 + high, gz - gz % 4 + low), device_id_type=MESH,
            )

        stay_first = pltpu.make_async_copy(
            outgoing.at[gx // 2, :, gz // 4], passing.at[gx // 2, gz // 4], local_sems.at[0]
        )
        stay_second = pltpu.make_async_copy(
            passing.at[:, :, core, 2 * high_z + (gz % 4) // 2], arrived.at[:, gx % 2, :, gz % 4], local_sems.at[1]
        )
        slot_copy = pltpu.make_async_copy(slots, slot_ref, local_sems.at[2])

        for copy in moves:
            copy.start()

        @pl.when(jnp.logical_not(moved))
        def _():
            wide[0, OWN, 1] = staged[...]
            labels[...] = labels_ref[...]

        stay_first.start()
        for d in range(1, 16):
            first_stage(d).start()
        load_taps(bank_ref, axial_in, kx, ky, ax)
        for it in range(ITERS):
            @pl.when(jnp.logical_not(has_c))
            def _():
                wide[it, :, far_side] = jnp.zeros((NEAR, BLK, LINE), BF)

            for there, rows in ((has_d, LOW), (has_u, HIGH)):
                @pl.when(jnp.logical_not(there))
                def _():
                    wide[it, rows] = jnp.zeros((BLK, 3, BLK, LINE), BF)

        reverse_taps(ky, ky_back)
        for copy in moves:
            copy.wait_recv()

        for it in range(ITERS):
            w = wide.at[it]
            near, straight, corner, relay = halo(it)
            for copy in near + straight + corner:
                copy.start()
            if it == 0:
                build_bands(ky_back, kx, ax, fwd_y, fwd_x, False)
                slots_of(labels[...], slots)
                slot_copy.start()
            for copy in near:
                copy.wait_recv()
            lateral_forward(index_of, fwd_x, fwd_y, w, mid, grown, BLK)
            for copy in straight:
                copy.wait_recv()
            for copy in relay:
                copy.start()
            if it == 0:
                stay_first.wait()
                for d in range(1, 16):
                    first_stage(d).wait_recv()
                for d in range(1, 8):
                    second_stage(d).start()
                stay_second.start()
            for copy in corner + relay:
                copy.wait_recv()
            lateral_forward(index_of, fwd_x, fwd_y, w, mid, grown, 0)
            lateral_forward(index_of, fwd_x, fwd_y, w, mid, grown, 2 * BLK)
            if it == 0:
                ones_response(index_of, ax, kx, ky, bx * BLK, bz * BLK, edge_x, edge_y, base, nx * BLK, nz * BLK)
                build_bands(ky, kx, ax, bwd_y, bwd_x, True)
                for d in range(1, 16):
                    first_stage(d).wait_send()
                for d in range(1, 8):
                    second_stage(d).wait()
                stay_second.wait()
                slot_copy.wait()
                for copy in moves:
                    copy.wait_send()
            for copy in near + straight + corner + relay:
                copy.wait_send()

            ratios(axial_ref, slot_ref, grown,
                   lambda s: arrived[s // 32, (s // 16) % 2, (s // 4) % 4, s % 4], excess, spread)
            to_mate, straight, corner, aside = sums(it)

            def send_straight(i, rows, there):
                to_mate[i].wait_recv()
                to_far[i] = (total[rows, 1] + jnp.where(there, part_mate[it, rows], 0.0)).astype(BF)
                straight[i].start()

            lateral_backward(index_of, bwd_x, bwd_y, spread, mid, total, 0)
            to_mate[0].start()
            to_corner[0] = total[LOW, far_side].astype(BF)
            corner[0].start()
            spread_axial(axial_ref, excess, spread, 2 * BLK)
            lateral_backward(index_of, bwd_x, bwd_y, spread, mid, total, 2 * BLK)
            to_mate[1].start()
            to_corner[1] = total[HIGH, far_side].astype(BF)
            corner[1].start()
            send_straight(0, LOW, has_d)
            spread_axial(axial_ref, excess, spread, BLK)
            send_straight(1, HIGH, has_u)
            lateral_backward(index_of, bwd_x, bwd_y, spread, mid, total, BLK)
            to_side[...] = total[OWN, far_side].astype(BF)
            aside[0].start()
            to_mate[2].start()
            inner = base[...] + total[OWN, 1]
            gain = (1.0 / VIEWS) if it == 0 else product[...] * (1.0 / VIEWS)
            for copy in to_mate[2:]:
                copy.wait_recv()
            inner = inner + part_mate[it, OWN]
            for copy in straight + corner:
                copy.wait_recv()
            for there, which in ((has_u, 0), (has_d, 1), (has_c & has_u, 2), (has_c & has_d, 3)):
                inner = inner + jnp.where(there, part[it, which].astype(F32), 0.0)
            for copy in aside:
                copy.wait_recv()
            inner = inner + jnp.where(has_c, part[it, 4].astype(F32), 0.0)
            product[...] = inner * gain
            if it + 1 < ITERS:
                wide[it + 1, OWN, 1] = (wide[it, OWN, 1].astype(F32) * product[...]).astype(BF)
            else:
                bring.start()
            for copy in to_mate + straight + corner + aside:
                copy.wait_send()

        @pl.when(jnp.logical_not(moved))
        def _():
            back[...] = product[...]

        bring.wait_recv()
        out_ref[...] = estimate_ref[...] * back[...]
        bring.wait_send()

    smem = pl.BlockSpec(memory_space=pltpu.SMEM)
    vmem = pl.BlockSpec(memory_space=pltpu.VMEM)
    dma = pltpu.SemaphoreType.DMA
    block = (BLK, BLK, LINE)
    return pl.pallas_call(
        body,
        name="joint",
        out_shape=jax.ShapeDtypeStruct(block, F32),
        in_specs=[smem] * 2 + [vmem] * 4 + [pl.BlockSpec(memory_space=pl.ANY)],
        out_specs=vmem,
        scratch_shapes=[
            pltpu.VMEM((KERNELS, 8, LINE), F32),
            pltpu.VMEM((KERNELS, 8, LINE), F32),
            pltpu.VMEM((KERNELS, 8, LINE), F32),
            pltpu.VMEM((8, LINE), F32),
            pltpu.VMEM((KERNELS, VIEWS, LINE, LINE), BF),
            pltpu.VMEM((KERNELS, VIEWS, LINE, LINE), BF),
            pltpu.VMEM((KERNELS, VIEWS * BLK, LINE), BF),
            pltpu.VMEM((KERNELS, LINE, VIEWS * BLK), BF),
            pltpu.VMEM((KERNELS, 8, LINE), F32),
            pltpu.VMEM((KERNELS, 8, LINE), F32),
            pltpu.VMEM(block, F32),
            pltpu.VMEM((NEAR, VIEWS * BLK, LINE), BF),
            pltpu.VMEM((VIEWS, NEAR, BLK, LINE), F32),
            pltpu.VMEM((VIEWS,) + block, F32),
            pltpu.VMEM((VIEWS, NEAR, BLK, LINE), BF),
            pltpu.VMEM((NEAR, 3, BLK, LINE), F32),
            pltpu.VMEM((2,) + block, BF),
            pltpu.VMEM((2,) + block, BF),
            pltpu.VMEM(block, BF),
            pltpu.VMEM(block, BF),
            pltpu.VMEM((ITERS, NEAR, 3, BLK, LINE), BF),
            pltpu.VMEM((ITERS, NEAR, BLK, LINE), F32),
            pltpu.VMEM((ITERS, 5) + block, BF),
            pltpu.VMEM(block, F32),
            pltpu.VMEM(block, F32),
            pltpu.VMEM((4, 4, 2, 4, BLK, LINE), BF),
            pltpu.VMEM((4, 2, 4, 4, BLK, LINE), BF),
            pltpu.VMEM((1, LINE), jnp.int32),
            pltpu.VMEM((1, LINE), jnp.int32),
            pltpu.SMEM((1, LINE), jnp.int32),
            (dma((3,)), dma((3,))),
            (dma((ITERS, 8)), dma((ITERS, 8))),
            (dma((ITERS, 10)), dma((ITERS, 10))),
            (dma((16,)), dma((16,))),
            (dma((8,)), dma((8,))),
            dma((3,)),
        ],
        compiler_params=pltpu.CompilerParams(
            vmem_limit_bytes=48 << 20, collective_id=0, has_side_effects=True
        ),
    )


def shards(estimate, view_tiles, incoming_label, lateral_bank, axial_kernel, kernel_index):
    nx, nz = lax.axis_size("gx"), lax.axis_size("gz")
    outgoing = view_tiles[0].reshape(4, 2, 4, 4, BLK, LINE)
    return joint_kernel(nx, nz)(
        kernel_index, axial_kernel, axial_kernel, lateral_bank, incoming_label, estimate, outgoing
    )


def solution(mesh):
    return jax.shard_map(
        shards,
        mesh=mesh,
        in_specs=(P("gz", "gx", None), P(("gx", "gz"), None, None), P(("gx", "gz"), None), P(), P(), P()),
        out_specs=P("gz", "gx", None),
        check_vma=False,
    )
```

```python
import jax
import jax.numpy as jnp
from jax import lax
from jax.experimental import pallas as pl
from jax.experimental.pallas import tpu as pltpu
from jax.sharding import PartitionSpec as P

TAPS = 33
ITERS = 2
HALO = 16
VIEWS = 6
KERNELS = 16
BLK = 16
NEAR = 48
LINE = 128
F32 = jnp.float32
BF = jnp.bfloat16
HI = lax.Precision.HIGHEST


def iota(shape, dim):
    return lax.broadcasted_iota(jnp.int32, shape, dim)


def load_taps(bank_ref, axial_in, kx, ky, ax):
    ax[...] = jnp.zeros_like(ax)
    ax[:VIEWS, :TAPS] = axial_in[...]
    for dim, taps in ((0, kx), (1, ky)):
        taps[...] = jnp.zeros_like(taps)
        for v in range(VIEWS):
            taps[:, v, :TAPS] = bank_ref[v, :, dim, :]
        raw = taps[...]
        total = jnp.sum(raw, axis=-1, keepdims=True)
        taps[...] = raw / jnp.where(total > 0.0, total, 1.0)


def line_scale(ax):
    axial = jnp.sum(ax[...], axis=1, keepdims=True)
    return jnp.broadcast_to(1.0 / jnp.where(axial > 0.0, axial, 1.0), (8, LINE))


def reverse_taps(ky, ky_back):
    flip = jnp.where(iota((LINE, LINE), 0) + iota((LINE, LINE), 1) == TAPS - 1, 1.0, 0.0)
    taps = ky[...].reshape(KERNELS * 8, LINE)
    ky_back[...] = jnp.dot(taps, flip, precision=HI, preferred_element_type=F32).reshape(KERNELS, 8, LINE)


def build_bands(ky, kx, ax, bands_y, bands_x, spread_out):
    inside = jnp.abs(iota((LINE, LINE), 0) - iota((LINE, LINE), 1)) <= HALO
    scale = line_scale(ax)

    @pl.loop(0, KERNELS)
    def _(k):
        taps_x = kx[k]
        taps_y = ky[k] * scale
        rows = []
        for v in range(VIEWS):
            band = jnp.broadcast_to(taps_y[v : v + 1], (LINE, LINE))
            band = pltpu.roll(band, LINE - HALO, 1, stride=1, stride_axis=0)
            bands_y[k, v] = jnp.where(inside, band, 0.0).astype(BF)
            rows.append(pltpu.roll(jnp.broadcast_to(taps_x[v : v + 1], (BLK, LINE)), 0, 1, stride=1, stride_axis=0))
        across = jnp.concatenate(rows, 0)
        bands_x[k] = (across.T if spread_out else across).astype(BF)


def ones_response(index_of, ax, kx_ref, ky_ref, col0, depth0, edge_x, edge_y, base_ref, cols, depths):
    tap = iota((LINE, LINE), 0)
    pos = iota((LINE, LINE), 1)
    at_x = col0 + pos - tap + HALO
    at_y = pos - tap + HALO
    ok_x = jnp.where((at_x >= 0) & (at_x < cols), 1.0, 0.0)
    ok_y = jnp.where((at_y >= 0) & (at_y < LINE), 1.0, 0.0)
    kx = kx_ref[...].reshape(KERNELS * 8, LINE)
    ky = ky_ref[...].reshape(KERNELS * 8, LINE)
    edge_x[...] = jnp.dot(kx, ok_x, precision=HI, preferred_element_type=F32).reshape(KERNELS, 8, LINE)
    edge_y[...] = jnp.dot(ky, ok_y, precision=HI, preferred_element_type=F32).reshape(KERNELS, 8, LINE)
    axial = ax[...]
    total = jnp.sum(axial, axis=1, keepdims=True)
    axial = axial / jnp.where(total > 0.0, total, 1.0)
    lane = iota((8, LINE), 1)
    for z in range(BLK):
        k = index_of(HALO + z)
        at_z = depth0 + z - lane + HALO
        part = jnp.sum(jnp.where((at_z >= 0) & (at_z < depths), axial, 0.0), axis=1, keepdims=True)
        left = edge_x[k][:, :BLK] * part
        base_ref[z] = lax.dot_general(
            left, edge_y[k], (((0,), (0,)), ((), ())), precision=HI, preferred_element_type=F32
        )


def slots_of(labels, slots):
    column = jnp.broadcast_to(labels, (LINE, LINE)).T
    hit = column == iota((LINE, LINE), 1)
    slots[...] = jnp.max(jnp.where(hit, iota((LINE, LINE), 0), -1), axis=0, keepdims=True)


def lateral_forward(index_of, fwd_x, fwd_y, wide, mid, grown, first):
    depths = range(first, first + BLK)
    for z in depths:
        mid[z] = jnp.dot(
            fwd_x[index_of(z)][:, :NEAR], wide[z].reshape(NEAR, LINE), preferred_element_type=F32
        ).astype(BF)
    for z in depths:
        for v in range(VIEWS):
            grown[v, z] = jnp.dot(
                mid[z, v * BLK : (v + 1) * BLK, :], fwd_y[index_of(z), v], preferred_element_type=F32
            )


def lateral_backward(index_of, bwd_x, bwd_y, spread, mid, total, first):
    depths = range(first, first + BLK)
    for z in depths:
        for v in range(VIEWS):
            mid[z, v * BLK : (v + 1) * BLK, :] = jnp.dot(
                spread[v, z], bwd_y[index_of(z), v], preferred_element_type=F32
            ).astype(BF)
    for z in depths:
        total[z] = jnp.dot(bwd_x[index_of(z)][:NEAR], mid[z], preferred_element_type=F32).reshape(3, BLK, LINE)


HALVES = (slice(0, 8), slice(8, 16))


def reached(zi):
    return range(max(0, zi - 2 * HALO), min(BLK - 1, zi) + 1)


def axial_backward(weights, excess, spread, first, v, rows):
    for zi in range(first, first + BLK):
        acc = None
        for zo in reached(zi):
            term = weights[zi - zo] * excess[zo]
            acc = term if acc is None else acc + term
        spread[v, zi, rows, :] = acc.astype(BF)


def ratios(axial_ref, slot_ref, grown, tile_of, excess, spread):
    @pl.loop(0, VIEWS)
    def _(v):
        weights = [axial_ref[v, t] for t in range(TAPS)]
        seen = jnp.full((8, LINE), slot_ref[0, v * BLK], jnp.int32) >= 0
        for rows in HALVES:
            total = [None] * BLK
            for zi in range(NEAR):
                g = grown[v, zi, rows, :]
                for zo in reached(zi):
                    term = weights[zi - zo] * g
                    total[zo] = term if total[zo] is None else total[zo] + term
            over = []
            for zo in range(BLK):
                tile = tile_of(jnp.maximum(slot_ref[0, v * BLK + zo], 0))[rows].astype(F32)
                ratio = (tile / total[zo]).astype(BF).astype(F32)
                over.append(jnp.where(seen, ratio - 1.0, 0.0))
                excess[v, zo, rows, :] = over[-1]
            axial_backward(weights, over, spread, 0, v, rows)


def spread_axial(axial_ref, excess, spread, first):
    @pl.loop(0, VIEWS)
    def _(v):
        weights = [axial_ref[v, t] for t in range(TAPS)]
        for rows in HALVES:
            axial_backward(weights, [excess[v, zo, rows, :] for zo in range(BLK)], spread, first, v, rows)


LOW, OWN, HIGH = slice(0, BLK), slice(BLK, 2 * BLK), slice(2 * BLK, NEAR)
MESH = pl.DeviceIdType.MESH


def worker_of(bx, bz):
    return 2 * (bx // 2) + (bz % 4) // 2, 4 * (bz // 4) + 2 * (bz % 2) + bx % 2


class Copy:
    def __init__(self, src, dst, sems, slot, device, sends, receives):
        self.src, self.sems, self.slot = src, sems, slot
        self.sends, self.receives = sends, receives
        self.out = self.back = self.make(dst, device)
        self.device = device

    def make(self, dst, device):
        return pltpu.make_async_remote_copy(
            src_ref=self.src, dst_ref=dst, send_sem=self.sems[0].at[self.slot], recv_sem=self.sems[1].at[self.slot],
            device_id=device, device_id_type=MESH,
        )

    def lands_in(self, region):
        self.back = self.make(region, self.device)
        return self

    def start(self):
        pl.when(self.sends)(self.out.start)

    def wait_recv(self):
        pl.when(self.receives)(self.back.wait_recv)

    def wait_send(self):
        pl.when(self.sends)(self.out.wait_send)


def joint_kernel(nx, nz):
    def body(index_ref, axial_ref, axial_in, bank_ref, labels_ref, estimate_ref, outgoing,
             out_ref, kx, ky, ky_back, ax, fwd_y, bwd_y, fwd_x, bwd_x, edge_x, edge_y, base, mid, grown, excess, spread, total,
             to_far, to_corner, to_side, staged, wide, part_mate, part, product, back,
             passing, arrived, labels, slots, slot_ref,
             move_sems, halo_sems, sum_sems, first_sems, second_sems, local_sems):
        gx, gz = lax.axis_index("gx"), lax.axis_index("gz")
        core, high_z = gz % 2, gx % 2
        bx, bz = gx - high_z + core, gz - gz % 4 + 2 * high_z + (gz % 4) // 2
        has_d, has_u = bz > 0, bz < nz - 1
        bc = bx - 1 + 2 * core
        has_c = (bc >= 0) & (bc < nx)
        bc, bd, bu = (bc + nx) % nx, (bz + nz - 1) % nz, (bz + 1) % nz
        mate = (gx, gz + 1 - 2 * core)
        across, down, up = worker_of(bc, bz), worker_of(bx, bd), worker_of(bx, bu)
        across_down, across_up = worker_of(bc, bd), worker_of(bc, bu)
        worker, owner = worker_of(gx, gz), (bx, bz)
        moved = (bx != gx) | (bz != gz)
        far_side, mate_side = 2 * core, 2 - 2 * core

        def index_of(z):
            return index_ref[jnp.clip(bz * BLK - HALO + z, 0, nz * BLK - 1)]

        barrier = pltpu.get_barrier_semaphore()

        def greet(device):
            pl.semaphore_signal(barrier, inc=1, device_id=device, device_id_type=MESH)

        for d in range(1, 16):
            greet((2 * ((gx // 2 + d // 4) % 4) + gx % 2, 4 * ((gz // 4 + d % 4) % 4) + gz % 4))
        for d in range(1, 8):
            greet((gx - gx % 2 + (gx % 2 + d // 4) % 2, gz - gz % 4 + (gz % 4 + d % 4) % 4))
        extra = 0
        for there, device in (
            (has_c, across), (has_d, down), (has_u, up), (has_c & has_d, across_down), (has_c & has_u, across_up),
        ):
            pl.when(there)(lambda device=device: greet(device))
            extra = extra + there.astype(jnp.int32)
        staged[...] = estimate_ref[...].astype(BF)
        pl.semaphore_wait(barrier, 22 + extra)

        moves = [
            Copy(staged, wide.at[0, OWN, 1], move_sems, 0, worker, moved, moved),
            Copy(labels_ref, labels, move_sems, 1, worker, moved, moved),
        ]
        bring = Copy(product, back, move_sems, 2, owner, moved, moved)

        def halo(it):
            w = wide.at[it]
            sems = (halo_sems[0].at[it], halo_sems[1].at[it])
            own = w.at[OWN, 1]
            near = [
                Copy(own, w.at[OWN, mate_side], sems, 1, across, has_c, has_c).lands_in(w.at[OWN, far_side]),
                Copy(own, w.at[OWN, far_side], sems, 0, mate, True, True).lands_in(w.at[OWN, mate_side]),
            ]
            straight = [
                Copy(own, w.at[LOW, 1], sems, 2, up, has_u, has_d),
                Copy(own, w.at[HIGH, 1], sems, 3, down, has_d, has_u),
            ]
            corner = [
                Copy(own, w.at[LOW, mate_side], sems, 4, across_up, has_c & has_u, has_c & has_d).lands_in(
                    w.at[LOW, far_side]),
                Copy(own, w.at[HIGH, mate_side], sems, 5, across_down, has_c & has_d, has_c & has_u).lands_in(
                    w.at[HIGH, far_side]),
            ]
            relay = [
                Copy(w.at[LOW, 1], w.at[LOW, far_side], sems, 6, mate, has_d, has_d).lands_in(w.at[LOW, mate_side]),
                Copy(w.at[HIGH, 1], w.at[HIGH, far_side], sems, 7, mate, has_u, has_u).lands_in(w.at[HIGH, mate_side]),
            ]
            return near, straight, corner, relay

        def sums(it):
            sems = (sum_sems[0].at[it], sum_sems[1].at[it])
            p = part.at[it]
            to_mate = [
                Copy(total.at[rows, mate_side], part_mate.at[it, rows], sems, i, mate, there, there)
                for i, (rows, there) in enumerate(((LOW, has_d), (HIGH, has_u), (OWN, True)))
            ]
            straight = [
                Copy(to_far.at[0], p.at[0], sems, 4, down, has_d, has_u),
                Copy(to_far.at[1], p.at[1], sems, 5, up, has_u, has_d),
            ]
            corner = [
                Copy(to_corner.at[0], p.at[2], sems, 6, across_down, has_c & has_d, has_c & has_u),
                Copy(to_corner.at[1], p.at[3], sems, 7, across_up, has_c & has_u, has_c & has_d),
            ]
            aside = [Copy(to_side, p.at[4], sems, 8, across, has_c, has_c)]
            return to_mate, straight, corner, aside

        def first_stage(d):
            y, x = (gx // 2 + d // 4) % 4, (gz // 4 + d % 4) % 4
            return pltpu.make_async_remote_copy(
                src_ref=outgoing.at[y, :, x], dst_ref=passing.at[gx // 2, gz // 4],
                send_sem=first_sems[0].at[d], recv_sem=first_sems[1].at[d],
                device_id=(2 * y + gx % 2, 4 * x + gz % 4), device_id_type=MESH,
            )

        def second_stage(d):
            high, low = (gx % 2 + d // 4) % 2, (gz % 4 + d % 4) % 4
            return pltpu.make_async_remote_copy(
                src_ref=passing.at[:, :, low % 2, 2 * high + low // 2], dst_ref=arrived.at[:, gx % 2, :, gz % 4],
                send_sem=second_sems[0].at[d], recv_sem=second_sems[1].at[d],
                device_id=(gx - gx % 2 + high, gz - gz % 4 + low), device_id_type=MESH,
            )

        stay_first = pltpu.make_async_copy(
            outgoing.at[gx // 2, :, gz // 4], passing.at[gx // 2, gz // 4], local_sems.at[0]
        )
        stay_second = pltpu.make_async_copy(
            passing.at[:, :, core, 2 * high_z + (gz % 4) // 2], arrived.at[:, gx % 2, :, gz % 4], local_sems.at[1]
        )
        slot_copy = pltpu.make_async_copy(slots, slot_ref, local_sems.at[2])

        for copy in moves:
            copy.start()

        @pl.when(jnp.logical_not(moved))
        def _():
            wide[0, OWN, 1] = staged[...]
            labels[...] = labels_ref[...]

        stay_first.start()
        for d in range(1, 16):
            first_stage(d).start()
        load_taps(bank_ref, axial_in, kx, ky, ax)
        for it in range(ITERS):
            @pl.when(jnp.logical_not(has_c))
            def _():
                wide[it, :, far_side] = jnp.zeros((NEAR, BLK, LINE), BF)

            for there, rows in ((has_d, LOW), (has_u, HIGH)):
                @pl.when(jnp.logical_not(there))
                def _():
                    wide[it, rows] = jnp.zeros((BLK, 3, BLK, LINE), BF)

        reverse_taps(ky, ky_back)
        build_bands(ky_back, kx, ax, fwd_y, fwd_x, False)
        for copy in moves:
            copy.wait_recv()

        pending = []
        for it in range(ITERS):
            w = wide.at[it]
            near, straight, corner, relay = halo(it)
            for copy in near + straight + corner:
                copy.start()
            for copy in pending:
                copy.wait_send()
            if it == 0:
                build_bands(ky, kx, ax, bwd_y, bwd_x, True)
                slots_of(labels[...], slots)
                slot_copy.start()
            for copy in near:
                copy.wait_recv()
            if it == 0:
                stay_first.wait()
                for d in range(1, 16):
                    first_stage(d).wait_recv()
                for d in range(1, 8):
                    second_stage(d).start()
                stay_second.start()
            lateral_forward(index_of, fwd_x, fwd_y, w, mid, grown, BLK)
            for copy in straight:
                copy.wait_recv()
            for copy in relay:
                copy.start()
            for copy in corner + relay:
                copy.wait_recv()
            lateral_forward(index_of, fwd_x, fwd_y, w, mid, grown, 0)
            lateral_forward(index_of, fwd_x, fwd_y, w, mid, grown, 2 * BLK)
            if it == 0:
                ones_response(index_of, ax, kx, ky, bx * BLK, bz * BLK, edge_x, edge_y, base, nx * BLK, nz * BLK)
                for d in range(1, 16):
                    first_stage(d).wait_send()
                for d in range(1, 8):
                    second_stage(d).wait()
                stay_second.wait()
                slot_copy.wait()
                for copy in moves:
                    copy.wait_send()
            for copy in near + straight + corner + relay:
                copy.wait_send()

            ratios(axial_ref, slot_ref, grown,
                   lambda s: arrived[s // 32, (s // 16) % 2, (s // 4) % 4, s % 4], excess, spread)
            to_mate, straight, corner, aside = sums(it)

            def send_straight(i, rows, there):
                to_mate[i].wait_recv()
                to_far[i] = (total[rows, 1] + jnp.where(there, part_mate[it, rows], 0.0)).astype(BF)
                straight[i].start()

            lateral_backward(index_of, bwd_x, bwd_y, spread, mid, total, 0)
            to_mate[0].start()
            to_corner[0] = total[LOW, far_side].astype(BF)
            corner[0].start()
            spread_axial(axial_ref, excess, spread, 2 * BLK)
            lateral_backward(index_of, bwd_x, bwd_y, spread, mid, total, 2 * BLK)
            to_mate[1].start()
            to_corner[1] = total[HIGH, far_side].astype(BF)
            corner[1].start()
            send_straight(0, LOW, has_d)
            spread_axial(axial_ref, excess, spread, BLK)
            send_straight(1, HIGH, has_u)
            lateral_backward(index_of, bwd_x, bwd_y, spread, mid, total, BLK)
            to_side[...] = total[OWN, far_side].astype(BF)
            aside[0].start()
            to_mate[2].start()
            inner = base[...] + total[OWN, 1]
            gain = (1.0 / VIEWS) if it == 0 else product[...] * (1.0 / VIEWS)
            for copy in to_mate[2:]:
                copy.wait_recv()
            inner = inner + part_mate[it, OWN]
            for copy in straight + corner:
                copy.wait_recv()
            for there, which in ((has_u, 0), (has_d, 1), (has_c & has_u, 2), (has_c & has_d, 3)):
                inner = inner + jnp.where(there, part[it, which].astype(F32), 0.0)
            for copy in aside:
                copy.wait_recv()
            inner = inner + jnp.where(has_c, part[it, 4].astype(F32), 0.0)
            product[...] = inner * gain
            if it + 1 < ITERS:
                wide[it + 1, OWN, 1] = (wide[it, OWN, 1].astype(F32) * product[...]).astype(BF)
            else:
                bring.start()
            pending = to_mate + straight + corner + aside

        @pl.when(jnp.logical_not(moved))
        def _():
            back[...] = product[...]

        for copy in pending:
            copy.wait_send()
        bring.wait_recv()
        out_ref[...] = estimate_ref[...] * back[...]
        bring.wait_send()

    smem = pl.BlockSpec(memory_space=pltpu.SMEM)
    vmem = pl.BlockSpec(memory_space=pltpu.VMEM)
    dma = pltpu.SemaphoreType.DMA
    block = (BLK, BLK, LINE)
    return pl.pallas_call(
        body,
        name="joint",
        out_shape=jax.ShapeDtypeStruct(block, F32),
        in_specs=[smem] * 2 + [vmem] * 4 + [pl.BlockSpec(memory_space=pl.ANY)],
        out_specs=vmem,
        scratch_shapes=[
            pltpu.VMEM((KERNELS, 8, LINE), F32),
            pltpu.VMEM((KERNELS, 8, LINE), F32),
            pltpu.VMEM((KERNELS, 8, LINE), F32),
            pltpu.VMEM((8, LINE), F32),
            pltpu.VMEM((KERNELS, VIEWS, LINE, LINE), BF),
            pltpu.VMEM((KERNELS, VIEWS, LINE, LINE), BF),
            pltpu.VMEM((KERNELS, VIEWS * BLK, LINE), BF),
            pltpu.VMEM((KERNELS, LINE, VIEWS * BLK), BF),
            pltpu.VMEM((KERNELS, 8, LINE), F32),
            pltpu.VMEM((KERNELS, 8, LINE), F32),
            pltpu.VMEM(block, F32),
            pltpu.VMEM((NEAR, VIEWS * BLK, LINE), BF),
            pltpu.VMEM((VIEWS, NEAR, BLK, LINE), F32),
            pltpu.VMEM((VIEWS,) + block, F32),
            pltpu.VMEM((VIEWS, NEAR, BLK, LINE), BF),
            pltpu.VMEM((NEAR, 3, BLK, LINE), F32),
            pltpu.VMEM((2,) + block, BF),
            pltpu.VMEM((2,) + block, BF),
            pltpu.VMEM(block, BF),
            pltpu.VMEM(block, BF),
            pltpu.VMEM((ITERS, NEAR, 3, BLK, LINE), BF),
            pltpu.VMEM((ITERS, NEAR, BLK, LINE), F32),
            pltpu.VMEM((ITERS, 5) + block, BF),
            pltpu.VMEM(block, F32),
            pltpu.VMEM(block, F32),
            pltpu.VMEM((4, 4, 2, 4, BLK, LINE), BF),
            pltpu.VMEM((4, 2, 4, 4, BLK, LINE), BF),
            pltpu.VMEM((1, LINE), jnp.int32),
            pltpu.VMEM((1, LINE), jnp.int32),
            pltpu.SMEM((1, LINE), jnp.int32),
            (dma((3,)), dma((3,))),
            (dma((ITERS, 8)), dma((ITERS, 8))),
            (dma((ITERS, 10)), dma((ITERS, 10))),
            (dma((16,)), dma((16,))),
            (dma((8,)), dma((8,))),
            dma((3,)),
        ],
        compiler_params=pltpu.CompilerParams(
            vmem_limit_bytes=48 << 20, collective_id=0, has_side_effects=True
        ),
    )


def shards(estimate, view_tiles, incoming_label, lateral_bank, axial_kernel, kernel_index):
    nx, nz = lax.axis_size("gx"), lax.axis_size("gz")
    outgoing = view_tiles[0].reshape(4, 2, 4, 4, BLK, LINE)
    return joint_kernel(nx, nz)(
        kernel_index, axial_kernel, axial_kernel, lateral_bank, incoming_label, estimate, outgoing
    )


def solution(mesh):
    return jax.shard_map(
        shards,
        mesh=mesh,
        in_specs=(P("gz", "gx", None), P(("gx", "gz"), None, None), P(("gx", "gz"), None), P(), P(), P()),
        out_specs=P("gz", "gx", None),
        check_vma=False,
    )
```

```python
import jax
import jax.numpy as jnp
from jax import lax
from jax.experimental import pallas as pl
from jax.experimental.pallas import tpu as pltpu
from jax.sharding import PartitionSpec as P

TAPS = 33
ITERS = 2
HALO = 16
VIEWS = 6
KERNELS = 16
BLK = 16
NEAR = 48
LINE = 128
F32 = jnp.float32
BF = jnp.bfloat16
HI = lax.Precision.HIGHEST


def iota(shape, dim):
    return lax.broadcasted_iota(jnp.int32, shape, dim)


def load_taps(bank_ref, axial_in, kx, ky, ax):
    ax[...] = jnp.zeros_like(ax)
    ax[:VIEWS, :TAPS] = axial_in[...]
    for dim, taps in ((0, kx), (1, ky)):
        taps[...] = jnp.zeros_like(taps)
        for v in range(VIEWS):
            taps[:, v, :TAPS] = bank_ref[v, :, dim, :]
        raw = taps[...]
        total = jnp.sum(raw, axis=-1, keepdims=True)
        taps[...] = raw / jnp.where(total > 0.0, total, 1.0)


def line_scale(ax):
    axial = jnp.sum(ax[...], axis=1, keepdims=True)
    return jnp.broadcast_to(1.0 / jnp.where(axial > 0.0, axial, 1.0), (8, LINE))


def reverse_taps(ky, ky_back):
    flip = jnp.where(iota((LINE, LINE), 0) + iota((LINE, LINE), 1) == TAPS - 1, 1.0, 0.0)
    taps = ky[...].reshape(KERNELS * 8, LINE)
    ky_back[...] = jnp.dot(taps, flip, precision=HI, preferred_element_type=F32).reshape(KERNELS, 8, LINE)


def build_bands(ky, kx, ax, bands_y, bands_x, spread_out):
    inside = jnp.abs(iota((LINE, LINE), 0) - iota((LINE, LINE), 1)) <= HALO
    scale = line_scale(ax)

    @pl.loop(0, KERNELS)
    def _(k):
        taps_x = kx[k]
        taps_y = ky[k] * scale
        rows = []
        for v in range(VIEWS):
            band = jnp.broadcast_to(taps_y[v : v + 1], (LINE, LINE))
            band = pltpu.roll(band, LINE - HALO, 1, stride=1, stride_axis=0)
            bands_y[k, v] = jnp.where(inside, band, 0.0).astype(BF)
            rows.append(pltpu.roll(jnp.broadcast_to(taps_x[v : v + 1], (BLK, LINE)), 0, 1, stride=1, stride_axis=0))
        across = jnp.concatenate(rows, 0)
        bands_x[k] = (across.T if spread_out else across).astype(BF)


def ones_response(index_of, ax, kx_ref, ky_ref, col0, depth0, edge_x, edge_y, base_ref, cols, depths):
    tap = iota((LINE, LINE), 0)
    pos = iota((LINE, LINE), 1)
    at_x = col0 + pos - tap + HALO
    at_y = pos - tap + HALO
    ok_x = jnp.where((at_x >= 0) & (at_x < cols), 1.0, 0.0)
    ok_y = jnp.where((at_y >= 0) & (at_y < LINE), 1.0, 0.0)
    kx = kx_ref[...].reshape(KERNELS * 8, LINE)
    ky = ky_ref[...].reshape(KERNELS * 8, LINE)
    edge_x[...] = jnp.dot(kx, ok_x, precision=HI, preferred_element_type=F32).reshape(KERNELS, 8, LINE)
    edge_y[...] = jnp.dot(ky, ok_y, precision=HI, preferred_element_type=F32).reshape(KERNELS, 8, LINE)
    axial = ax[...]
    total = jnp.sum(axial, axis=1, keepdims=True)
    axial = axial / jnp.where(total > 0.0, total, 1.0)
    lane = iota((8, LINE), 1)
    for z in range(BLK):
        k = index_of(HALO + z)
        at_z = depth0 + z - lane + HALO
        part = jnp.sum(jnp.where((at_z >= 0) & (at_z < depths), axial, 0.0), axis=1, keepdims=True)
        left = edge_x[k][:, :BLK] * part
        base_ref[z] = lax.dot_general(
            left, edge_y[k], (((0,), (0,)), ((), ())), precision=HI, preferred_element_type=F32
        )


def slots_of(labels, slots):
    column = jnp.broadcast_to(labels, (LINE, LINE)).T
    hit = column == iota((LINE, LINE), 1)
    slots[...] = jnp.max(jnp.where(hit, iota((LINE, LINE), 0), -1), axis=0, keepdims=True)


def lateral_forward(index_of, fwd_x, fwd_y, wide, mid, grown, first):
    depths = range(first, first + BLK)
    for z in depths:
        mid[z] = jnp.dot(
            fwd_x[index_of(z)][:, :NEAR], wide[z].reshape(NEAR, LINE), preferred_element_type=F32
        ).astype(BF)
    for z in depths:
        for v in range(VIEWS):
            grown[v, z] = jnp.dot(
                mid[z, v * BLK : (v + 1) * BLK, :], fwd_y[index_of(z), v], preferred_element_type=F32
            )


def lateral_backward(index_of, bwd_x, bwd_y, spread, mid, total, first):
    depths = range(first, first + BLK)
    for z in depths:
        for v in range(VIEWS):
            mid[z, v * BLK : (v + 1) * BLK, :] = jnp.dot(
                spread[v, z], bwd_y[index_of(z), v], preferred_element_type=F32
            ).astype(BF)
    for z in depths:
        total[z] = jnp.dot(bwd_x[index_of(z)][:NEAR], mid[z], preferred_element_type=F32).reshape(3, BLK, LINE)


HALVES = (slice(0, 8), slice(8, 16))


def reached(zi):
    return range(max(0, zi - 2 * HALO), min(BLK - 1, zi) + 1)


def axial_backward(weights, excess, spread, first, v, rows):
    for zi in range(first, first + BLK):
        acc = None
        for zo in reached(zi):
            term = weights[zi - zo] * excess[zo]
            acc = term if acc is None else acc + term
        spread[v, zi, rows, :] = acc.astype(BF)


def ratios(axial_ref, slot_ref, grown, tile_of, excess, spread):
    @pl.loop(0, VIEWS)
    def _(v):
        weights = [axial_ref[v, t] for t in range(TAPS)]
        seen = jnp.full((8, LINE), slot_ref[0, v * BLK], jnp.int32) >= 0
        for rows in HALVES:
            total = [None] * BLK
            for zi in range(NEAR):
                g = grown[v, zi, rows, :]
                for zo in reached(zi):
                    term = weights[zi - zo] * g
                    total[zo] = term if total[zo] is None else total[zo] + term
            over = []
            for zo in range(BLK):
                tile = tile_of(jnp.maximum(slot_ref[0, v * BLK + zo], 0))[rows].astype(F32)
                ratio = (tile / total[zo]).astype(BF).astype(F32)
                over.append(jnp.where(seen, ratio - 1.0, 0.0))
                excess[v, zo, rows, :] = over[-1]
            axial_backward(weights, over, spread, 0, v, rows)


def spread_axial(axial_ref, excess, spread, first):
    @pl.loop(0, VIEWS)
    def _(v):
        weights = [axial_ref[v, t] for t in range(TAPS)]
        for rows in HALVES:
            axial_backward(weights, [excess[v, zo, rows, :] for zo in range(BLK)], spread, first, v, rows)


LOW, OWN, HIGH = slice(0, BLK), slice(BLK, 2 * BLK), slice(2 * BLK, NEAR)
MESH = pl.DeviceIdType.MESH


def worker_of(bx, bz):
    return 2 * (bx // 2) + (bz % 4) // 2, 4 * (bz // 4) + 2 * (bz % 2) + bx % 2


class Copy:
    def __init__(self, src, dst, sems, slot, device, sends, receives):
        self.src, self.sems, self.slot = src, sems, slot
        self.sends, self.receives = sends, receives
        self.out = self.back = self.make(dst, device)
        self.device = device

    def make(self, dst, device):
        return pltpu.make_async_remote_copy(
            src_ref=self.src, dst_ref=dst, send_sem=self.sems[0].at[self.slot], recv_sem=self.sems[1].at[self.slot],
            device_id=device, device_id_type=MESH,
        )

    def lands_in(self, region):
        self.back = self.make(region, self.device)
        return self

    def start(self):
        pl.when(self.sends)(self.out.start)

    def wait_recv(self):
        pl.when(self.receives)(self.back.wait_recv)

    def wait_send(self):
        pl.when(self.sends)(self.out.wait_send)


def joint_kernel(nx, nz):
    def body(index_ref, axial_ref, axial_in, bank_ref, labels_ref, estimate_ref, outgoing,
             out_ref, kx, ky, ky_back, ax, fwd_y, bwd_y, fwd_x, bwd_x, edge_x, edge_y, base, mid, grown, excess, spread, total,
             to_far, to_corner, to_side, staged, wide, part_mate, part, product, back,
             passing, arrived, labels, slots, slot_ref,
             move_sems, halo_sems, sum_sems, first_sems, second_sems, local_sems):
        gx, gz = lax.axis_index("gx"), lax.axis_index("gz")
        core, high_z = gz % 2, gx % 2
        bx, bz = gx - high_z + core, gz - gz % 4 + 2 * high_z + (gz % 4) // 2
        has_d, has_u = bz > 0, bz < nz - 1
        bc = bx - 1 + 2 * core
        has_c = (bc >= 0) & (bc < nx)
        bc, bd, bu = (bc + nx) % nx, (bz + nz - 1) % nz, (bz + 1) % nz
        mate = (gx, gz + 1 - 2 * core)
        across, down, up = worker_of(bc, bz), worker_of(bx, bd), worker_of(bx, bu)
        across_down, across_up = worker_of(bc, bd), worker_of(bc, bu)
        worker, owner = worker_of(gx, gz), (bx, bz)
        moved = (bx != gx) | (bz != gz)
        far_side, mate_side = 2 * core, 2 - 2 * core

        def index_of(z):
            return index_ref[jnp.clip(bz * BLK - HALO + z, 0, nz * BLK - 1)]

        barrier = pltpu.get_barrier_semaphore()

        def greet(device):
            pl.semaphore_signal(barrier, inc=1, device_id=device, device_id_type=MESH)

        for d in range(1, 16):
            greet((2 * ((gx // 2 + d // 4) % 4) + gx % 2, 4 * ((gz // 4 + d % 4) % 4) + gz % 4))
        for d in range(1, 8):
            greet((gx - gx % 2 + (gx % 2 + d // 4) % 2, gz - gz % 4 + (gz % 4 + d % 4) % 4))
        extra = 0
        for there, device in (
            (has_c, across), (has_d, down), (has_u, up), (has_c & has_d, across_down), (has_c & has_u, across_up),
        ):
            pl.when(there)(lambda device=device: greet(device))
            extra = extra + there.astype(jnp.int32)
        staged[...] = estimate_ref[...].astype(BF)
        pl.semaphore_wait(barrier, 22 + extra)

        moves = [
            Copy(staged, wide.at[0, OWN, 1], move_sems, 0, worker, moved, moved),
            Copy(labels_ref, labels, move_sems, 1, worker, moved, moved),
        ]
        bring = [Copy(product.at[rows], back.at[rows], move_sems, 2 + i, owner, moved, moved) for i, rows in enumerate(HALVES)]

        def halo(it):
            w = wide.at[it]
            sems = (halo_sems[0].at[it], halo_sems[1].at[it])
            own = w.at[OWN, 1]
            near = [
                Copy(own, w.at[OWN, mate_side], sems, 1, across, has_c, has_c).lands_in(w.at[OWN, far_side]),
                Copy(own, w.at[OWN, far_side], sems, 0, mate, True, True).lands_in(w.at[OWN, mate_side]),
            ]
            straight = [
                Copy(own, w.at[LOW, 1], sems, 2, up, has_u, has_d),
                Copy(own, w.at[HIGH, 1], sems, 3, down, has_d, has_u),
            ]
            corner = [
                Copy(own, w.at[LOW, mate_side], sems, 4, across_up, has_c & has_u, has_c & has_d).lands_in(
                    w.at[LOW, far_side]),
                Copy(own, w.at[HIGH, mate_side], sems, 5, across_down, has_c & has_d, has_c & has_u).lands_in(
                    w.at[HIGH, far_side]),
            ]
            relay = [
                Copy(w.at[LOW, 1], w.at[LOW, far_side], sems, 6, mate, has_d, has_d).lands_in(w.at[LOW, mate_side]),
                Copy(w.at[HIGH, 1], w.at[HIGH, far_side], sems, 7, mate, has_u, has_u).lands_in(w.at[HIGH, mate_side]),
            ]
            return near, straight, corner, relay

        def sums(it):
            sems = (sum_sems[0].at[it], sum_sems[1].at[it])
            p = part.at[it]
            to_mate = [
                Copy(total.at[rows, mate_side], part_mate.at[it, rows], sems, i, mate, there, there)
                for i, (rows, there) in enumerate(((LOW, has_d), (HIGH, has_u), (OWN, True)))
            ]
            straight = [
                Copy(to_far.at[0], p.at[0], sems, 4, down, has_d, has_u),
                Copy(to_far.at[1], p.at[1], sems, 5, up, has_u, has_d),
            ]
            corner = [
                Copy(to_corner.at[0], p.at[2], sems, 6, across_down, has_c & has_d, has_c & has_u),
                Copy(to_corner.at[1], p.at[3], sems, 7, across_up, has_c & has_u, has_c & has_d),
            ]
            aside = [Copy(to_side, p.at[4], sems, 8, across, has_c, has_c)]
            return to_mate, straight, corner, aside

        def first_stage(d):
            y, x = (gx // 2 + d // 4) % 4, (gz // 4 + d % 4) % 4
            return pltpu.make_async_remote_copy(
                src_ref=outgoing.at[y, :, x], dst_ref=passing.at[gx // 2, gz // 4],
                send_sem=first_sems[0].at[d], recv_sem=first_sems[1].at[d],
                device_id=(2 * y + gx % 2, 4 * x + gz % 4), device_id_type=MESH,
            )

        def second_stage(d):
            high, low = (gx % 2 + d // 4) % 2, (gz % 4 + d % 4) % 4
            return pltpu.make_async_remote_copy(
                src_ref=passing.at[:, :, low % 2, 2 * high + low // 2], dst_ref=arrived.at[:, gx % 2, :, gz % 4],
                send_sem=second_sems[0].at[d], recv_sem=second_sems[1].at[d],
                device_id=(gx - gx % 2 + high, gz - gz % 4 + low), device_id_type=MESH,
            )

        stay_first = pltpu.make_async_copy(
            outgoing.at[gx // 2, :, gz // 4], passing.at[gx // 2, gz // 4], local_sems.at[0]
        )
        stay_second = pltpu.make_async_copy(
            passing.at[:, :, core, 2 * high_z + (gz % 4) // 2], arrived.at[:, gx % 2, :, gz % 4], local_sems.at[1]
        )
        slot_copy = pltpu.make_async_copy(slots, slot_ref, local_sems.at[2])

        for copy in moves:
            copy.start()

        @pl.when(jnp.logical_not(moved))
        def _():
            wide[0, OWN, 1] = staged[...]
            labels[...] = labels_ref[...]

        stay_first.start()
        for d in range(1, 16):
            first_stage(d).start()
        load_taps(bank_ref, axial_in, kx, ky, ax)
        for it in range(ITERS):
            @pl.when(jnp.logical_not(has_c))
            def _():
                wide[it, :, far_side] = jnp.zeros((NEAR, BLK, LINE), BF)

            for there, rows in ((has_d, LOW), (has_u, HIGH)):
                @pl.when(jnp.logical_not(there))
                def _():
                    wide[it, rows] = jnp.zeros((BLK, 3, BLK, LINE), BF)

        reverse_taps(ky, ky_back)
        build_bands(ky_back, kx, ax, fwd_y, fwd_x, False)
        for copy in moves:
            copy.wait_recv()

        pending = []
        for it in range(ITERS):
            w = wide.at[it]
            near, straight, corner, relay = halo(it)
            for copy in near + straight + corner:
                copy.start()
            for copy in pending:
                copy.wait_send()
            if it == 0:
                build_bands(ky, kx, ax, bwd_y, bwd_x, True)
                slots_of(labels[...], slots)
                slot_copy.start()
            for copy in near:
                copy.wait_recv()
            if it == 0:
                stay_first.wait()
                for d in range(1, 16):
                    first_stage(d).wait_recv()
                for d in range(1, 8):
                    second_stage(d).start()
                stay_second.start()
            lateral_forward(index_of, fwd_x, fwd_y, w, mid, grown, BLK)
            for copy in straight:
                copy.wait_recv()
            for copy in relay:
                copy.start()
            for copy in corner + relay:
                copy.wait_recv()
            lateral_forward(index_of, fwd_x, fwd_y, w, mid, grown, 0)
            lateral_forward(index_of, fwd_x, fwd_y, w, mid, grown, 2 * BLK)
            if it == 0:
                ones_response(index_of, ax, kx, ky, bx * BLK, bz * BLK, edge_x, edge_y, base, nx * BLK, nz * BLK)
                for d in range(1, 16):
                    first_stage(d).wait_send()
                for d in range(1, 8):
                    second_stage(d).wait()
                stay_second.wait()
                slot_copy.wait()
                for copy in moves:
                    copy.wait_send()
            for copy in near + straight + corner + relay:
                copy.wait_send()

            ratios(axial_ref, slot_ref, grown,
                   lambda s: arrived[s // 32, (s // 16) % 2, (s // 4) % 4, s % 4], excess, spread)
            to_mate, straight, corner, aside = sums(it)

            def send_straight(i, rows, there):
                to_mate[i].wait_recv()
                to_far[i] = (total[rows, 1] + jnp.where(there, part_mate[it, rows], 0.0)).astype(BF)
                straight[i].start()

            lateral_backward(index_of, bwd_x, bwd_y, spread, mid, total, 0)
            to_mate[0].start()
            to_corner[0] = total[LOW, far_side].astype(BF)
            corner[0].start()
            spread_axial(axial_ref, excess, spread, 2 * BLK)
            lateral_backward(index_of, bwd_x, bwd_y, spread, mid, total, 2 * BLK)
            to_mate[1].start()
            to_corner[1] = total[HIGH, far_side].astype(BF)
            corner[1].start()
            send_straight(0, LOW, has_d)
            spread_axial(axial_ref, excess, spread, BLK)
            send_straight(1, HIGH, has_u)
            lateral_backward(index_of, bwd_x, bwd_y, spread, mid, total, BLK)
            to_side[...] = total[OWN, far_side].astype(BF)
            aside[0].start()
            to_mate[2].start()
            inner = base[...] + total[OWN, 1]
            gain = (1.0 / VIEWS) if it == 0 else product[...] * (1.0 / VIEWS)
            for copy in to_mate[2:]:
                copy.wait_recv()
            inner = inner + part_mate[it, OWN]
            for copy in straight + corner:
                copy.wait_recv()
            for there, which in ((has_u, 0), (has_d, 1), (has_c & has_u, 2), (has_c & has_d, 3)):
                inner = inner + jnp.where(there, part[it, which].astype(F32), 0.0)
            for copy in aside:
                copy.wait_recv()
            inner = inner + jnp.where(has_c, part[it, 4].astype(F32), 0.0)
            scaled = inner * gain
            if it + 1 < ITERS:
                product[...] = scaled
                wide[it + 1, OWN, 1] = (wide[it, OWN, 1].astype(F32) * product[...]).astype(BF)
            else:
                for rows, copy in zip(HALVES, bring):
                    product[rows] = scaled[rows]
                    copy.start()
            pending = to_mate + straight + corner + aside

        @pl.when(jnp.logical_not(moved))
        def _():
            back[...] = product[...]

        for copy in pending:
            copy.wait_send()
        for rows, copy in zip(HALVES, bring):
            copy.wait_recv()
            out_ref[rows] = estimate_ref[rows] * back[rows]
        for copy in bring:
            copy.wait_send()

    smem = pl.BlockSpec(memory_space=pltpu.SMEM)
    vmem = pl.BlockSpec(memory_space=pltpu.VMEM)
    dma = pltpu.SemaphoreType.DMA
    block = (BLK, BLK, LINE)
    return pl.pallas_call(
        body,
        name="joint",
        out_shape=jax.ShapeDtypeStruct(block, F32),
        in_specs=[smem] * 2 + [vmem] * 4 + [pl.BlockSpec(memory_space=pl.ANY)],
        out_specs=vmem,
        scratch_shapes=[
            pltpu.VMEM((KERNELS, 8, LINE), F32),
            pltpu.VMEM((KERNELS, 8, LINE), F32),
            pltpu.VMEM((KERNELS, 8, LINE), F32),
            pltpu.VMEM((8, LINE), F32),
            pltpu.VMEM((KERNELS, VIEWS, LINE, LINE), BF),
            pltpu.VMEM((KERNELS, VIEWS, LINE, LINE), BF),
            pltpu.VMEM((KERNELS, VIEWS * BLK, LINE), BF),
            pltpu.VMEM((KERNELS, LINE, VIEWS * BLK), BF),
            pltpu.VMEM((KERNELS, 8, LINE), F32),
            pltpu.VMEM((KERNELS, 8, LINE), F32),
            pltpu.VMEM(block, F32),
            pltpu.VMEM((NEAR, VIEWS * BLK, LINE), BF),
            pltpu.VMEM((VIEWS, NEAR, BLK, LINE), F32),
            pltpu.VMEM((VIEWS,) + block, F32),
            pltpu.VMEM((VIEWS, NEAR, BLK, LINE), BF),
            pltpu.VMEM((NEAR, 3, BLK, LINE), F32),
            pltpu.VMEM((2,) + block, BF),
            pltpu.VMEM((2,) + block, BF),
            pltpu.VMEM(block, BF),
            pltpu.VMEM(block, BF),
            pltpu.VMEM((ITERS, NEAR, 3, BLK, LINE), BF),
            pltpu.VMEM((ITERS, NEAR, BLK, LINE), F32),
            pltpu.VMEM((ITERS, 5) + block, BF),
            pltpu.VMEM(block, F32),
            pltpu.VMEM(block, F32),
            pltpu.VMEM((4, 4, 2, 4, BLK, LINE), BF),
            pltpu.VMEM((4, 2, 4, 4, BLK, LINE), BF),
            pltpu.VMEM((1, LINE), jnp.int32),
            pltpu.VMEM((1, LINE), jnp.int32),
            pltpu.SMEM((1, LINE), jnp.int32),
            (dma((4,)), dma((4,))),
            (dma((ITERS, 8)), dma((ITERS, 8))),
            (dma((ITERS, 10)), dma((ITERS, 10))),
            (dma((16,)), dma((16,))),
            (dma((8,)), dma((8,))),
            dma((3,)),
        ],
        compiler_params=pltpu.CompilerParams(
            vmem_limit_bytes=48 << 20, collective_id=0, has_side_effects=True
        ),
    )


def shards(estimate, view_tiles, incoming_label, lateral_bank, axial_kernel, kernel_index):
    nx, nz = lax.axis_size("gx"), lax.axis_size("gz")
    outgoing = view_tiles[0].reshape(4, 2, 4, 4, BLK, LINE)
    return joint_kernel(nx, nz)(
        kernel_index, axial_kernel, axial_kernel, lateral_bank, incoming_label, estimate, outgoing
    )


def solution(mesh):
    return jax.shard_map(
        shards,
        mesh=mesh,
        in_specs=(P("gz", "gx", None), P(("gx", "gz"), None, None), P(("gx", "gz"), None), P(), P(), P()),
        out_specs=P("gz", "gx", None),
        check_vma=False,
    )
```
